32 devices in a mesh: gy: 8 (over y, x, core), gz: 4 (over z).
Axes of the slice: x: 2, y: 2, z: 4, core: 2. Of those that a mesh axis runs over, the one named last changes fastest.
Arguments:
- pressure_cotangent: bfloat16 [32, 1024, 2048], P('gz', 'gy'), may hold values from -6 to 6
- velocity_cotangent: bfloat16 [32, 1024, 2048], P('gz', 'gy'), may hold values from -6 to 6
- inverse_spacing: float32 [32], P('gz'), may hold values from 0.5 to 4
- inverse_pivot: float32 [32, 2048, 1024], P('gz', 'gy'), may hold values from 0.02 to 0.1
- lower_factor: float32 [32, 2048, 1024], P('gz', 'gy'), may hold values from 0.04 to 0.998, as said below
- upper_factor: float32 [32, 2048, 1024], P('gz', 'gy'), may hold values from 0.04 to 0.998, as said below
Outputs:
- pressure_adjoint: bfloat16 [32, 1024, 2048], P('gz', 'gy')
The draws below stay inside these ranges and needn't reach their ends.
Inputs may be any that keep to these rules, and one draw needn't show every extreme that they name: `lower_factor`: multiplier carried from one level to the next. `upper_factor`: multiplier carried from one level to the next.
All inputs are finite; a program needn't handle non-finite values.
Results may differ from the reference program's by a relative error of at most 0.0018.
Values may be sent and summed in bfloat16 or wider, within the bound.
A program may use at most 192 MiB of HBM per device.

```python
import math
import jax
import jax.numpy as jnp
from jax import lax

NX = 2048
NY = 1024
VERTICAL_LAYERS = 32


def rate_field(key):
    stochastic_seed_sequence = jax.random.split(key, 6)
    slow_share = 0.5
    slow_mask = jax.random.bernoulli(stochastic_seed_sequence[0], slow_share, (1, NX, NY))
    slow_rate = jax.random.uniform(stochastic_seed_sequence[1], (1, NX, NY), jnp.float32, 0.93, 0.998)
    fast_rate = jax.random.uniform(stochastic_seed_sequence[2], (1, NX, NY), jnp.float32, 0.1, 0.6)
    base_rate = jnp.where(slow_mask, slow_rate, fast_rate)
    jitter = jax.random.uniform(stochastic_seed_sequence[3], (VERTICAL_LAYERS, NX, NY), jnp.float32, 0.97, 1.0)
    sudden_level_set = jax.random.randint(stochastic_seed_sequence[4], (2,), 0, VERTICAL_LAYERS)
    level_heights = jnp.arange(VERTICAL_LAYERS)
    abrupt_change_indicator = jnp.any(level_heights[:, None] == sudden_level_set[None, :], axis=1)
    abrupt_change_cutoff = jax.random.uniform(stochastic_seed_sequence[5], (VERTICAL_LAYERS, 1, 1), jnp.float32, 0.5, 0.8)
    decomposition_coefficients = jnp.where(abrupt_change_indicator[:, None, None], abrupt_change_cutoff, 1.0)
    return (base_rate * jitter * decomposition_coefficients).astype(jnp.float32)


def draw_lower_factor(key, part):
    return rate_field(jax.random.fold_in(key, 11))


def draw_upper_factor(key, part):
    return rate_field(jax.random.fold_in(key, 23))


def level_of(key, extent, cuts, low, high):
    gain, own = 1.0, jax.random.fold_in(key, 6)
    for axis_at, parts in cuts:
        heights = jnp.exp(jax.random.uniform(jax.random.fold_in(own, axis_at), (parts,), jnp.float32, low / len(cuts), high / len(cuts)))
        gain = gain * jnp.repeat(heights, extent[axis_at] // parts).reshape([-1 if axis == axis_at else 1 for axis in range(len(extent))])
    return gain


def bell_draw(rng, extent, width, bound, shards=(), kind=jnp.bfloat16):
    level = level_of(rng, extent, shards, -0.22, 0.18) if shards else 1.0
    result = jax.random.normal(rng, extent, jnp.float32) * width * level
    return jnp.minimum(jnp.maximum(result, -bound), bound).astype(kind)


def setup_inputs(seed: int = 0) -> dict:
    key_of = jax.random.split(jax.random.key(seed), 7)
    return {
        "pressure_cotangent": bell_draw(key_of[0], (VERTICAL_LAYERS, NY, NX), 1.0, 6.0, ((0, 4), (1, 8))),
        "velocity_cotangent": bell_draw(key_of[1], (VERTICAL_LAYERS, NY, NX), 1.0, 6.0, ((0, 4), (1, 8))),
        "inverse_spacing": jnp.clip(jnp.exp(math.log(4.0) - 2.0794415 * jax.random.uniform(key_of[2], (VERTICAL_LAYERS,), jnp.float32) ** level_of(key_of[2], (VERTICAL_LAYERS,), ((0, 4),), -0.2, 0.2)), 0.5, 4.0),
        "inverse_pivot": jnp.clip(jnp.exp(math.log(0.1) - 1.609438 * jax.random.uniform(key_of[3], (VERTICAL_LAYERS, NX, NY), jnp.float32) ** level_of(key_of[3], (VERTICAL_LAYERS, NX, NY), ((0, 4), (1, 8)), -0.2, 0.2)), 0.02, 0.1),
        "lower_factor": draw_lower_factor(jax.random.fold_in(key_of[6], 71), 0),
        "upper_factor": draw_upper_factor(jax.random.fold_in(key_of[6], 71), 0),
    }


def reference(pressure_cotangent, velocity_cotangent, inverse_spacing, inverse_pivot, lower_factor, upper_factor):
    velocity = velocity_cotangent.astype(jnp.float32)
    shifted = jnp.concatenate([velocity[1:], jnp.zeros_like(velocity[:1])], 0)
    source = pressure_cotangent.astype(jnp.float32) + inverse_spacing[:, None, None] * (shifted - velocity)
    spectrum = jnp.fft.fft2(source, axes=(1, 2))
    spectrum = jnp.transpose(spectrum, (0, 2, 1))
    empty_field = jnp.zeros(spectrum.shape[1:], spectrum.dtype)

    def advance_down(running, layer_values):
        forcing, pivot_values, lower_values = layer_values
        running = pivot_values * forcing + lower_values * running
        return running, running

    _, lowered = lax.scan(advance_down, empty_field, (spectrum, inverse_pivot, lower_factor))

    def advance_up(running, layer_values):
        forcing, upper_values = layer_values
        running = forcing + upper_values * running
        return running, running

    _, solved = lax.scan(advance_up, empty_field, (lowered, upper_factor), reverse=True)
    pressure_field = jnp.fft.ifft2(jnp.transpose(solved, (0, 2, 1)), axes=(1, 2)).real
    return pressure_field.astype(jnp.bfloat16)
```

```python
import functools
import math

import jax
import jax.numpy as jnp
import ml_dtypes
import numpy as np
from jax import lax
from jax.experimental import pallas as pl
from jax.experimental.pallas import tpu as pltpu
from jax.sharding import PartitionSpec as P

PREC = lax.Precision.HIGH
F32 = jnp.float32


def passed_along(x, axis, by):
    size = lax.axis_size(axis)
    pairs = [(i, i + by) for i in range(size) if 0 <= i + by < size]
    return lax.ppermute(x, axis, pairs)


def unit_circle(phase, count):
    angle = (phase % count).astype(F32) * (2.0 * math.pi / count)
    return jnp.cos(angle), jnp.sin(angle)


def circle_table(count):
    low = 32
    high = count // low
    k = jnp.arange(count, dtype=jnp.int32)[None, :]
    ch, sh = unit_circle(jnp.arange(high, dtype=jnp.int32)[:, None] * low * k, count)
    cl, sl = unit_circle(jnp.arange(low, dtype=jnp.int32)[:, None] * k, count)
    ch, sh, cl, sl = lax.optimization_barrier((ch, sh, cl, sl))
    ch, sh, cl, sl = ch[:, None], sh[:, None], cl[None], sl[None]
    cosine = (ch * cl - sh * sl).reshape(count, count)
    sine = (sh * cl + ch * sl).reshape(count, count)
    return cosine, sine


def split_table(count, half):
    low = 32
    column = jnp.arange(2 * count, dtype=jnp.int32)[None, :]
    k = column // (2 * half) * half + column % half
    quarter = jnp.where(column % (2 * half) < half, 0, count // 4)
    ch, sh = unit_circle(jnp.arange(count // low, dtype=jnp.int32)[:, None] * low * k, count)
    cl, sl = unit_circle(jnp.arange(low, dtype=jnp.int32)[:, None] * k + quarter, count)
    ch, sh, cl, sl = lax.optimization_barrier((ch, sh, cl, sl))
    return (ch[:, None] * cl[None] - sh[:, None] * sl[None]).reshape(count, 2 * count)


def down_kernel(chunks, per, *refs):
    cos_refs, sin_refs = refs[:chunks], refs[chunks : 2 * chunks]
    pivot, lower, low, summary = refs[2 * chunks :]
    re = im = jnp.zeros(pivot.shape[1:], F32)
    gain = jnp.ones(pivot.shape[1:], F32)
    for z in range(chunks * per):
        c, s = cos_refs[z // per], sin_refs[z // per]
        q = z % per
        d, m = pivot[z], lower[z]
        re = d * (c[q, 0] + s[q, 1]) + m * re
        im = d * (c[q, 1] - s[q, 0]) + m * im
        gain = m * gain
        low[z, 0] = re
        low[z, 1] = im
    summary[0] = gain
    summary[1] = re
    summary[2] = im


def up_summary_kernel(levels, low, lower, upper, enter, summary):
    er, ei = enter[0, 0], enter[0, 1]
    re = im = jnp.zeros(lower.shape[1:], F32)
    gain = jnp.ones(lower.shape[1:], F32)
    carried = jnp.ones(lower.shape[1:], F32)
    for z in range(levels):
        carried = carried * lower[z]
        re = re + gain * (low[z, 0] + carried * er)
        im = im + gain * (low[z, 1] + carried * ei)
        gain = gain * upper[z]
    summary[0] = gain
    summary[1] = re
    summary[2] = im


def solve_kernel(levels, per, low, lower, upper, enter, above, *outs):
    er, ei = enter[0, 0], enter[0, 1]
    gains = []
    carried = jnp.ones(lower.shape[1:], F32)
    for z in range(levels):
        carried = carried * lower[z]
        gains.append(carried)
    re, im = above[0, 0], above[0, 1]
    for z in range(levels - 1, -1, -1):
        re = low[z, 0] + gains[z] * er + upper[z] * re
        im = low[z, 1] + gains[z] * ei + upper[z] * im
        outs[z // per][z % per, 0] = re
        outs[z // per][z % per, 1] = im


def entering(summary, reverse):
    count = lax.axis_size("gz")
    _, width, span = summary.shape
    parts = summary.reshape(3, count, width // count, span)
    got = lax.all_to_all(parts, "gz", split_axis=1, concat_axis=1, tiled=True)
    order = list(range(count))
    if reverse:
        order.reverse()
    states = [None] * count
    state = jnp.zeros((2, width // count, span), F32)
    for at in order:
        states[at] = state
        state = got[1:, at] + got[0, at][None] * state
    return lax.all_to_all(jnp.stack(states), "gz", split_axis=0, concat_axis=0, tiled=True)


def on_device(
    pressure_cotangent,
    velocity_cotangent,
    inverse_spacing,
    inverse_pivot,
    lower_factor,
    upper_factor,
):
    levels, rows, nx = pressure_cotangent.shape
    level_above = passed_along(velocity_cotangent[:1], "gz", -1)
    gy = lax.axis_size("gy")
    gz = lax.axis_size("gz")
    ny = rows * gy
    half = nx // gy
    per = 2 if levels % 2 == 0 else 1
    chunks = levels // per
    velocity = velocity_cotangent.astype(F32)
    shifted = jnp.concatenate([velocity[1:], level_above.astype(F32)], 0)
    source = pressure_cotangent.astype(F32) + inverse_spacing[:, None, None] * (shifted - velocity)

    table = lax.optimization_barrier(split_table(nx, half))
    cy, sy = lax.optimization_barrier(circle_table(ny))

    cos_parts, sin_parts = [], []
    for i in range(chunks):
        piece = source[i * per : (i + 1) * per]
        spec = jnp.einsum("zyn,nc->zyc", piece, table, precision=PREC)
        spec = jnp.transpose(spec.reshape(per, rows, gy, 2 * half), (2, 0, 1, 3))
        if i >= 2:
            spec, cos_parts[i - 2], sin_parts[i - 2] = lax.optimization_barrier(
                (spec, cos_parts[i - 2], sin_parts[i - 2])
            )
        got = lax.all_to_all(spec, "gy", split_axis=0, concat_axis=0, tiled=True)
        got = jnp.transpose(got, (1, 0, 2, 3)).reshape(per, ny, 2 * half)
        c = jnp.einsum("zyc,yk->zck", got, cy, precision=PREC)
        s = jnp.einsum("zyc,yk->zck", got, sy, precision=PREC)
        cos_parts.append(c.reshape(per, 2, half, ny))
        sin_parts.append(s.reshape(per, 2, half, ny))

    quarter = half // gz
    kb = min(16, quarter)
    in_quarter = quarter // kb
    grid = (half // kb,)
    chunk_spec = pl.BlockSpec((per, 2, kb, ny), lambda i: (0, 0, i, 0))
    factor_spec = pl.BlockSpec((levels, kb, ny), lambda i: (0, i, 0))
    low_spec = pl.BlockSpec((levels, 2, kb, ny), lambda i: (0, 0, i, 0))
    summary_spec = pl.BlockSpec((3, kb, ny), lambda i: (0, i, 0))
    state_spec = pl.BlockSpec((1, 2, kb, ny), lambda i: (i // in_quarter, 0, i % in_quarter, 0))
    summary_shape = jax.ShapeDtypeStruct((3, half, ny), F32)

    low, summary = pl.pallas_call(
        functools.partial(down_kernel, chunks, per),
        grid=grid,
        in_specs=[chunk_spec] * (2 * chunks) + [factor_spec] * 2,
        out_specs=[low_spec, summary_spec],
        out_shape=[jax.ShapeDtypeStruct((levels, 2, half, ny), F32), summary_shape],
    )(*cos_parts, *sin_parts, inverse_pivot, lower_factor)
    enter = entering(summary, False)
    summary = pl.pallas_call(
        functools.partial(up_summary_kernel, levels),
        grid=grid,
        in_specs=[low_spec, factor_spec, factor_spec, state_spec],
        out_specs=summary_spec,
        out_shape=summary_shape,
    )(low, lower_factor, upper_factor, enter)
    above = entering(summary, True)
    solved = pl.pallas_call(
        functools.partial(solve_kernel, levels, per),
        grid=grid,
        in_specs=[low_spec, factor_spec, factor_spec, state_spec, state_spec],
        out_specs=[chunk_spec] * chunks,
        out_shape=[jax.ShapeDtypeStruct((per, 2, half, ny), F32)] * chunks,
    )(low, lower_factor, upper_factor, enter, above)

    normalizer = 1.0 / (nx * ny)
    fields = []
    for i in range(chunks):
        flat = solved[i].reshape(per, 2 * half, ny)
        c = jnp.einsum("ky,zck->zyc", cy, flat, precision=PREC)
        s = jnp.einsum("ky,zck->zyc", sy, flat, precision=PREC)
        back = jnp.concatenate([c[..., :half] - s[..., half:], c[..., half:] + s[..., :half]], 2)
        back = jnp.transpose(back.reshape(per, gy, rows, 2 * half), (1, 0, 2, 3))
        if i >= 2:
            back, fields[i - 2] = lax.optimization_barrier((back, fields[i - 2]))
        got = lax.all_to_all(back, "gy", split_axis=0, concat_axis=0, tiled=True)
        got = jnp.transpose(got, (1, 2, 0, 3)).reshape(per, rows, 2 * nx)
        field = jnp.einsum("zyc,nc->zyn", got, table, precision=PREC) * normalizer
        fields.append(field.astype(jnp.bfloat16))
    return jnp.concatenate(fields, 0)


BF16 = jnp.bfloat16
MESH = pl.DeviceIdType.MESH
TINY = 1e-36
PEAK = 2.0**14
ROWS = 32
NT = (((1,), (1,)), ((), ()))
NN = (((1,), (0,)), ((), ()))


def split(x):
    high = x.astype(BF16)
    return high, (x - high.astype(F32)).astype(BF16)


def split_host(x):
    high = x.astype(np.float32).astype(ml_dtypes.bfloat16)
    low = (x - high.astype(np.float64)).astype(np.float32).astype(ml_dtypes.bfloat16)
    return high, low


def along_table(nx, gy):
    width = nx // gy
    chunk, g, j = np.meshgrid(np.arange(width // ROWS), np.arange(gy), np.arange(8), indexing="ij")
    parts = []
    for q in (0, 2, 1, 3):
        kx = g * width + ROWS * chunk + 4 * j + q
        turn = 2 * np.pi * ((kx[..., None] * np.arange(nx // 4)) % nx) / nx
        c, s = np.cos(turn), np.sin(turn)
        pair = np.stack([c, -s], 2)
        if q == 1:
            pair = np.concatenate([pair, np.stack([-s, -c], 2)], -1)
        if q == 3:
            pair = np.concatenate([pair, np.stack([s, c], 2)], -1)
        parts.append(pair.reshape(-1, pair.shape[-1]))
    return split_host(np.concatenate(parts, 1))


def across_table(ny):
    quarter = ny // 4
    lane = np.arange(quarter)
    block, inner = lane // 128, lane % 128
    tables = []
    for q in range(4):
        ky = 512 * block + 128 * (inner % 4) + 4 * (inner // 4) + q
        turn = 2 * np.pi * ((np.arange(quarter)[:, None] * ky) % ny) / ny
        c, s = np.cos(turn), np.sin(turn)
        tables.append(np.block([[c, -s], [s, c]]))
    return split_host(np.stack(tables))


def exchange_lanes(vs):
    lane = lax.broadcasted_iota(jnp.int32, vs[0].shape, 1)
    odd = lane % 2 == 1
    upper = lane % 4 >= 2
    a, b, c, d = vs
    a, b = jnp.where(odd, pltpu.roll(b, 1, 1), a), jnp.where(odd, b, pltpu.roll(a, 127, 1))
    c, d = jnp.where(odd, pltpu.roll(d, 1, 1), c), jnp.where(odd, d, pltpu.roll(c, 127, 1))
    a, c = jnp.where(upper, pltpu.roll(c, 2, 1), a), jnp.where(upper, c, pltpu.roll(a, 126, 1))
    b, d = jnp.where(upper, pltpu.roll(d, 2, 1), b), jnp.where(upper, d, pltpu.roll(b, 126, 1))
    return a, b, c, d


def encode(v):
    v2 = v * v
    v4 = v2 * v2
    return (v4 * v4 * v).astype(BF16)


def decode(w, scale):
    w = w.astype(F32)
    size = jnp.maximum(jnp.abs(w), 2.0**-126)
    return w * jnp.exp2(jnp.log(size) * (-8.0 / (9.0 * math.log(2.0)))) * scale


def dot3(ah, al, bh, bl, dims):
    def one(a, b):
        return lax.dot_general(a, b, dims, preferred_element_type=F32)

    return one(ah, bh) + one(al, bh) + one(ah, bl)


def greet(devices):
    barrier = pltpu.get_barrier_semaphore()
    for device in devices:
        pl.semaphore_signal(barrier, inc=1, device_id=device, device_id_type=MESH)


def forward_kernel(
    n, levels, nx,
    p_ref, v_hbm, spacing, th, tl, yh, yl, pivot_hbm, lower_hbm,
    low_hbm, top, gain,
    v_all, ah, al, stage, got, bh, bl, spec, pivot, lower,
    v_sem, edge_send, edge_recv, send_sem, recv_sem, own_sem, factor_sem, low_sem,
):
    me, z, zs = lax.axis_index("gy"), lax.axis_index("gz"), lax.axis_size("gz")
    rows = p_ref.shape[1]
    x4 = nx // 4
    width = nx // n
    chunks = width // ROWS
    y4 = n * rows // 4
    pairs = levels // 2
    body = 4 * width

    v_copy = pltpu.make_async_copy(v_hbm, v_all.at[pl.ds(0, levels)], v_sem)
    v_copy.start()
    barrier = pltpu.get_barrier_semaphore()
    greet([{"gy": lax.rem(me + d, n)} for d in range(1, n)])

    @pl.when(z < zs - 1)
    def _():
        greet([{"gz": z + 1}])

    pl.semaphore_wait(barrier, n - 1 + jnp.minimum(z, 1))

    def edge():
        return pltpu.make_async_remote_copy(
            src_ref=v_hbm.at[pl.ds(0, 1)], dst_ref=v_all.at[pl.ds(levels, 1)],
            send_sem=edge_send, recv_sem=edge_recv, device_id={"gz": z - 1}, device_id_type=MESH,
        )

    @pl.when(z > 0)
    def _():
        edge().start()

    @pl.when(z == zs - 1)
    def _():
        v_all[levels] = jnp.zeros((rows, nx), BF16)

    top[...] = jnp.zeros_like(top)
    gain[...] = jnp.ones_like(gain)

    def factors(lp):
        return [
            pltpu.make_async_copy(
                hbm.at[pl.ds(2 * lp, 2), :, pl.ds(128 * k, 128)], ref.at[k], factor_sem.at[i, k]
            )
            for i, (hbm, ref) in enumerate(((pivot_hbm, pivot), (lower_hbm, lower)))
            for k in range(y4 // 32)
        ]

    for copy in factors(0):
        copy.start()
    v_copy.wait()

    def own(lp):
        return pltpu.make_async_copy(stage.at[lax.rem(lp, 2), me], got.at[lp, me], own_sem.at[lp])

    def send(lp, d):
        peer = lax.rem(me + d, n)
        return pltpu.make_async_remote_copy(
            src_ref=stage.at[lax.rem(lp, 2), peer], dst_ref=got.at[lp, me],
            send_sem=send_sem.at[lp, d], recv_sem=recv_sem.at[lp, me],
            device_id={"gy": peer}, device_id_type=MESH,
        )

    def arrival(lp, d):
        peer = lax.rem(me + d, n)
        return pltpu.make_async_remote_copy(
            src_ref=stage.at[lax.rem(lp, 2), peer], dst_ref=got.at[lp, peer],
            send_sem=send_sem.at[lp, d], recv_sem=recv_sem.at[lp, peer],
            device_id={"gy": peer}, device_id_type=MESH,
        )

    def low_copy(lp):
        return pltpu.make_async_copy(spec, low_hbm.at[lp], low_sem)

    def spectra(lp):
        @pl.when(lp >= 2)
        def _():
            for d in range(1, n):
                send(lp - 2, d).wait_send()

        @pl.when((lp == pairs - 1) & (z < zs - 1))
        def _():
            edge().wait_recv()

        tile = 16
        peak = jnp.zeros((8, 128), F32)
        for lev in range(2):
            at = 2 * lp + lev
            factor = spacing[at]

            def source(i, peak, lev=lev, at=at, factor=factor):
                r = pl.ds(pl.multiple_of(i * tile, tile), tile)
                q = [pl.ds(k * x4, x4) for k in range(4)]
                xs = [
                    p_ref[at, r, s].astype(F32)
                    + factor * (v_all[at + 1, r, s].astype(F32) - v_all[at, r, s].astype(F32))
                    for s in q
                ]
                size = functools.reduce(jnp.maximum, [jnp.abs(x) for x in xs])
                e, o = xs[0] + xs[2], xs[1] + xs[3]
                to = pl.ds(pl.multiple_of(lev * rows + i * tile, tile), tile)
                for s, a in zip(q, (e + o, e - o, xs[0] - xs[2], xs[1] - xs[3])):
                    ah[to, s], al[to, s] = split(a)
                for k in range(x4 // 128):
                    part = size[:, k * 128 : (k + 1) * 128]
                    peak = jnp.maximum(peak, jnp.maximum(part[:8], part[8:]))
                return peak

            peak = lax.fori_loop(0, rows // tile, source, peak)
        peak = jnp.maximum(jnp.max(peak), TINY)
        held = jnp.full((16, 128), peak, F32).astype(BF16)
        shrink = PEAK / (nx * held.astype(F32)[:1, :1])
        slot = lax.rem(lp, 2)
        for g in range(n):
            stage[slot, g, pl.ds(body, 16), :] = held

        per = 2 if chunks % 2 == 0 else 1
        tall = per * 16 * n

        def transform(i, _):
            m = pl.ds(pl.multiple_of(i * tall, tall), tall)
            outs, at = [None] * 4, 0
            for q in (0, 2, 1, 3):
                wide = x4 if q % 2 == 0 else 2 * x4
                start = (0, 2 * x4, x4, 2 * x4)[q]
                t, a = pl.ds(at, wide), pl.ds(start, wide)
                outs[q] = dot3(th[m, t], tl[m, t], ah[:, a], al[:, a], NT) * shrink
                at += wide
            for k in range(per):
                for g in range(n):
                    for c in range(2):
                        s = (k * n + g) * 16 + c * 8
                        block = encode(jnp.concatenate([o[s : s + 8] for o in outs], 0))
                        for lev in range(2):
                            r = (lev * 2 + c) * width + (i * per + k) * ROWS
                            stage[slot, g, pl.ds(pl.multiple_of(r, ROWS), ROWS), :] = block[
                                :, lev * rows : (lev + 1) * rows
                            ]
            return 0

        lax.fori_loop(0, chunks // per, transform, 0)
        own(lp).start()
        for d in range(1, n):
            send(lp, d).start()

    def substitute(lp):
        own(lp).wait()
        for d in range(1, n):
            arrival(lp, d).wait_recv()

        tile = 16
        quads = n // 4
        scales = [got[lp, s, pl.ds(body, 16), :].astype(F32)[:1, :] * (nx / PEAK) for s in range(n)]

        def unpack(i, _):
            for lev in range(2):
                for h in range(quads):
                    xs = []
                    for c in range(2):
                        r = pl.ds(pl.multiple_of((lev * 2 + c) * width + i * tile, tile), tile)
                        xs.append([decode(got[lp, k * quads + h, r, :], scales[k * quads + h]) for k in range(4)])
                    (r0, r1, r2, r3), (i0, i1, i2, i3) = xs
                    er, fr, ei, fi = r0 + r2, r0 - r2, i0 + i2, i0 - i2
                    gr, hr, gi, hi = r1 + r3, r1 - r3, i1 + i3, i1 - i3
                    real = (er + gr, fr + hi, er - gr, fr - hi)
                    imag = (ei + gi, fi - hr, ei - gi, fi + hr)
                    to = pl.ds(pl.multiple_of(lev * width + i * tile, tile), tile)
                    for q in range(4):
                        for c, x in enumerate((real[q], imag[q])):
                            s = pl.ds(c * y4 + h * 128, 128)
                            bh[q, to, s], bl[q, to, s] = split(x)
            return 0

        lax.fori_loop(0, width // tile, unpack, 0)

        @pl.when(lp > 0)
        def _():
            low_copy(lp - 1).wait()

        tall = min(width, 256)

        def transform(i, _):
            q, m = i // (2 * width // tall), lax.rem(i, 2 * width // tall)
            r = pl.ds(pl.multiple_of(m * tall, tall), tall)
            spec[q, r, :] = dot3(bh[q, r, :], bl[q, r, :], yh[q], yl[q], NN)
            return 0

        lax.fori_loop(0, 4 * (2 * width // tall), transform, 0)
        for copy in factors(lp):
            copy.wait()

        def solve(i, _):
            chunk, q = i // 4, lax.rem(i, 4)
            strided = pl.ds(chunk * ROWS + q, 8, stride=4)
            r = pl.ds(pl.multiple_of(i * 8, 8), 8)
            for b in range(y4 // 128):
                for lev in range(2):
                    rl = pl.ds(pl.multiple_of(lev * width + i * 8, 8), 8)
                    natural = [pl.ds(512 * b + 128 * t, 128) for t in range(4)]
                    ms = [lower[4 * b + t, lev, strided, :] for t in range(4)]
                    ds = [pivot[4 * b + t, lev, strided, :] for t in range(4)]
                    for s, m in zip(natural, ms):
                        gain[r, s] = gain[r, s] * m
                    for c in range(2):
                        lanes = pl.ds(c * y4 + b * 128, 128)
                        vs = exchange_lanes([spec[k, rl, lanes] for k in range(4)])
                        for t in range(4):
                            new = ds[t] * vs[t] + ms[t] * top[c, r, natural[t]]
                            top[c, r, natural[t]] = new
                            spec[t, rl, lanes] = new
            return 0

        lax.fori_loop(0, width // 8, solve, 0)
        low_copy(lp).start()

        @pl.when(lp < pairs - 1)
        def _():
            for copy in factors(lp + 1):
                copy.start()

    def step(t, _):
        @pl.when(t < pairs)
        def _():
            spectra(t)

        @pl.when(t >= 1)
        def _():
            substitute(t - 1)

        return 0

    lax.fori_loop(0, pairs + 1, step, 0)
    low_copy(pairs - 1).wait()
    for lp in range(max(pairs - 2, 0), pairs):
        for d in range(1, n):
            send(lp, d).wait_send()

    @pl.when(z > 0)
    def _():
        edge().wait_send()


def backward_kernel(
    n, levels, nx,
    low_hbm, top_hbm, gain_hbm, lower_hbm, upper_hbm, th, tl, yh, yl,
    out_hbm,
    low, lower, upper, top, gain, enter, above, d_send, u_send, sh, sl, yo, stage, got, xh, xl, acc, out,
    low_sem, load_sem, sum_sem, ds_sem, dr_sem, us_sem, ur_sem, send_sem, recv_sem, own_sem, out_sem,
):
    me, z, zs = lax.axis_index("gy"), lax.axis_index("gz"), lax.axis_size("gz")
    width = nx // n
    chunks = width // ROWS
    rows = out_hbm.shape[1]
    ny = n * rows
    y4, x4 = ny // 4, nx // 4
    body = levels * 2 * ROWS
    per = 2 if chunks % 2 == 0 else 1

    def loads(c):
        slot = lax.rem(c, 2)
        r = pl.ds(pl.multiple_of(c * ROWS, ROWS), ROWS)
        return [
            pltpu.make_async_copy(low_hbm.at[:, :, :, r, :], low.at[slot], low_sem.at[slot]),
        ] + [
            pltpu.make_async_copy(hbm.at[:, r, pl.ds(128 * k, 128)], ref.at[slot, k], load_sem.at[slot, i, k])
            for i, (hbm, ref) in enumerate(((lower_hbm, lower), (upper_hbm, upper)))
            for k in range(ny // 128)
        ]

    def sums(c):
        slot = lax.rem(c, 2)
        r = pl.ds(pl.multiple_of(c * ROWS, ROWS), ROWS)
        return [
            pltpu.make_async_copy(top_hbm.at[:, r, :], top.at[slot], sum_sem.at[slot, 0]),
            pltpu.make_async_copy(gain_hbm.at[r, :], gain.at[slot], sum_sem.at[slot, 1]),
        ]

    for copy in sums(0) + loads(0):
        copy.start()
    acc[...] = jnp.zeros_like(acc)

    barrier = pltpu.get_barrier_semaphore()
    greet([{"gy": lax.rem(me + d, n)} for d in range(1, n)])

    @pl.when(z < zs - 1)
    def _():
        greet([{"gz": z + 1}])

    @pl.when(z > 0)
    def _():
        greet([{"gz": z - 1}])

    pl.semaphore_wait(barrier, n - 1 + jnp.minimum(z, 1) + jnp.minimum(zs - 1 - z, 1))

    @pl.when(z == 0)
    def _():
        enter[...] = jnp.zeros_like(enter)

    @pl.when(z == zs - 1)
    def _():
        above[...] = jnp.zeros_like(above)

    def pass_down(c):
        return pltpu.make_async_remote_copy(
            src_ref=d_send.at[lax.rem(c, 2)], dst_ref=enter.at[c], send_sem=ds_sem.at[c], recv_sem=dr_sem.at[c],
            device_id={"gz": z + 1}, device_id_type=MESH,
        )

    def pass_up(c):
        return pltpu.make_async_remote_copy(
            src_ref=u_send.at[lax.rem(c, 2)], dst_ref=above.at[c], send_sem=us_sem.at[c], recv_sem=ur_sem.at[c],
            device_id={"gz": z - 1}, device_id_type=MESH,
        )

    def own(c):
        return pltpu.make_async_copy(stage.at[lax.rem(c, 2), me], got.at[c, me], own_sem.at[c])

    def send(c, d):
        peer = lax.rem(me + d, n)
        return pltpu.make_async_remote_copy(
            src_ref=stage.at[lax.rem(c, 2), peer], dst_ref=got.at[c, me],
            send_sem=send_sem.at[c, d], recv_sem=recv_sem.at[c, me],
            device_id={"gy": peer}, device_id_type=MESH,
        )

    def arrival(c, d):
        peer = lax.rem(me + d, n)
        return pltpu.make_async_remote_copy(
            src_ref=stage.at[lax.rem(c, 2), peer], dst_ref=got.at[c, peer],
            send_sem=send_sem.at[c, d], recv_sem=recv_sem.at[c, peer],
            device_id={"gy": peer}, device_id_type=MESH,
        )

    def relay(c):
        for copy in sums(c):
            copy.wait()

        @pl.when(c + 1 < chunks)
        def _():
            for copy in sums(c + 1):
                copy.start()

        @pl.when(z > 0)
        def _():
            pass_down(c).wait_recv()

        @pl.when(z < zs - 1)
        def _():
            @pl.when(c >= 2)
            def _():
                pass_down(c - 2).wait_send()

            slot = lax.rem(c, 2)

            def carry(i, _):
                r = pl.ds(pl.multiple_of(i * 8, 8), 8)
                for k in range(2):
                    d_send[slot, k, r, :] = top[slot, k, r, :] + gain[slot, r, :] * enter[c, k, r, :]
                return 0

            lax.fori_loop(0, ROWS // 8, carry, 0)
            pass_down(c).start()

    def solve(c):
        slot = lax.rem(c, 2)
        for copy in loads(c):
            copy.wait()

        @pl.when(c + 1 < chunks)
        def _():
            for copy in loads(c + 1):
                copy.start()

        @pl.when(z < zs - 1)
        def _():
            pass_up(c).wait_recv()

        @pl.when((z > 0) & (c >= 2))
        def _():
            pass_up(c - 2).wait_send()

        def sweep(q, _):
            strided = pl.ds(q, 8, stride=4)
            r = pl.ds(pl.multiple_of(q * 8, 8), 8)
            for b in range(y4 // 128):
                natural = [pl.ds(512 * b + 128 * t, 128) for t in range(4)]
                gains = [[] for _ in range(4)]
                for t in range(4):
                    for lev in range(levels):
                        m = lower[slot, 4 * b + t, lev, strided, :]
                        gains[t].append(m if lev == 0 else gains[t][-1] * m)
                state = [[above[c, k, r, s] for s in natural] for k in range(2)]
                entry = [[enter[c, k, r, s] for s in natural] for k in range(2)]
                for lev in range(levels - 1, -1, -1):
                    ups = [upper[slot, 4 * b + t, lev, strided, :] for t in range(4)]
                    for k in range(2):
                        lanes = pl.ds(k * y4 + b * 128, 128)
                        state[k] = [
                            low[slot, lev // 2, t, lev % 2, r, lanes] + gains[t][lev] * entry[k][t] + ups[t] * state[k][t]
                            for t in range(4)
                        ]
                        to = pl.ds(pl.multiple_of(lev * ROWS + q * 8, 8), 8)
                        for p, x in enumerate(exchange_lanes(state[k])):
                            yo[p, to, lanes] = x
                for k in range(2):
                    for t in range(4):
                        u_send[slot, k, r, natural[t]] = state[k][t]
            return 0

        lax.fori_loop(0, ROWS // 8, sweep, 0)

        @pl.when(z > 0)
        def _():
            pass_up(c).start()

        @pl.when(c >= 2)
        def _():
            own(c - 2).wait()
            for d in range(1, n):
                send(c - 2, d).wait_send()

        count = levels * ROWS

        def halve(i, _):
            r = pl.ds(pl.multiple_of(i * 16, 16), 16)
            for q in range(4):
                sh[q, r, :], sl[q, r, :] = split(yo[q, r, :])
            return 0

        lax.fori_loop(0, count // 16, halve, 0)

        def transform(q, _):
            yo[q] = dot3(sh[q], sl[q], yh[q], yl[q], NT)
            return 0

        lax.fori_loop(0, 4, transform, 0)

        def combine(i, peak):
            r = pl.ds(pl.multiple_of(i * 8, 8), 8)
            for h in range(y4 // 128):
                rs = pl.ds(h * 128, 128)
                cs = pl.ds(y4 + h * 128, 128)
                r0, r1, r2, r3 = [yo[q, r, rs] for q in range(4)]
                i0, i1, i2, i3 = [yo[q, r, cs] for q in range(4)]
                er, fr, ei, fi = r0 + r2, r0 - r2, i0 + i2, i0 - i2
                gr, hr, gi, hi = r1 + r3, r1 - r3, i1 + i3, i1 - i3
                real = (er + gr, fr - hi, er - gr, fr + hi)
                imag = (ei + gi, fi + hr, ei - gi, fi - hr)
                for q in range(4):
                    yo[q, r, rs] = real[q]
                    yo[q, r, cs] = imag[q]
                    peak = jnp.maximum(peak, jnp.maximum(jnp.abs(real[q]), jnp.abs(imag[q])))
            return peak

        peak = lax.fori_loop(0, count // 8, combine, jnp.zeros((8, 128), F32))
        held = jnp.full((16, 128), jnp.maximum(jnp.max(peak), TINY), F32).astype(BF16)
        shrink = PEAK / held.astype(F32)[:1, :1]
        quads = n // 4
        for g in range(n):
            stage[slot, g, pl.ds(body, 16), :] = held

        def pack(lev, _):
            r = pl.ds(pl.multiple_of(lev * ROWS, ROWS), ROWS)
            for g in range(n):
                for k in range(2):
                    x = yo[g // quads, r, pl.ds(k * y4 + (g % quads) * 128, 128)]
                    to = pl.ds(pl.multiple_of((lev * 2 + k) * ROWS, ROWS), ROWS)
                    stage[slot, g, to, :] = encode(x * shrink)
            return 0

        lax.fori_loop(0, levels, pack, 0)
        own(c).start()
        for d in range(1, n):
            send(c, d).start()

    def gather(pair):
        for k in range(per):
            c = pair * per + k

            for d in range(1, n):
                arrival(c, d).wait_recv()

        scales = [
            [got[pair * per + k, s, pl.ds(body, 16), :].astype(F32)[:1, :] * (1.0 / (PEAK * nx * ny)) for s in range(n)]
            for k in range(per)
        ]
        deep = per * 16 * n

        def two_levels(lp, _):
            for lev in range(2):
                for k in range(per):
                    parts = []
                    for s in range(n):
                        for j in range(2):
                            r = ((lp * 2 + lev) * 2 + j) * ROWS
                            r = pl.ds(pl.multiple_of(r, ROWS), ROWS)
                            parts.append(decode(got[pair * per + k, s, r, :], scales[k][s]))
                    for q in range(4):
                        block = jnp.concatenate([x[q * 8 : q * 8 + 8] for x in parts], 0)
                        high, low_part = split(block.T)
                        lanes = pl.ds(k * 16 * n, 16 * n)
                        xh[q, pl.ds(lev * rows, rows), lanes] = high
                        xl[q, pl.ds(lev * rows, rows), lanes] = low_part
            m = pl.ds(pl.multiple_of(pair * deep, deep), deep)
            to = pl.ds(pl.multiple_of(lp * 2 * rows, 2 * rows), 2 * rows)

            def part(q, start, wide):
                t = pl.ds(start, wide)
                return dot3(xh[q], xl[q], th[m, t], tl[m, t], NN)

            acc[to, pl.ds(0, x4)] += part(0, 0, x4)
            acc[to, pl.ds(x4, x4)] += part(2, x4, x4)
            acc[to, pl.ds(2 * x4, 2 * x4)] += part(1, 2 * x4, 2 * x4) + part(3, 4 * x4, 2 * x4)
            return 0

        lax.fori_loop(0, levels // 2, two_levels, 0)

    lag = 2 * (zs - 1)
    halves = chunks // per

    def step(t, _):
        down = t - z

        @pl.when((down >= 0) & (down < chunks))
        def _():
            relay(down)

        c = t - lag + z

        @pl.when((c >= 0) & (c < chunks))
        def _():
            solve(c)

        @pl.when((c >= 2 * per - 1) & (c < chunks) & (lax.rem(c + 1 + 2 * per, per) == 0))
        def _():
            gather((c + 1) // per - 2)

        return 0

    last = chunks - 1
    lax.fori_loop(0, chunks + lag, step, 0)
    for c in range(max(chunks - 2, 0), chunks):
        own(c).wait()
        for d in range(1, n):
            send(c, d).wait_send()

        @pl.when(z < zs - 1)
        def _():
            pass_down(c).wait_send()

        @pl.when(z > 0)
        def _():
            pass_up(c).wait_send()

    gather(halves - 1)

    def finish(i, _):
        lev = i
        r = pl.ds(pl.multiple_of(lev * rows, rows), rows)
        slot = lax.rem(lev, 2)

        @pl.when(lev >= 2)
        def _():
            pltpu.make_async_copy(out.at[slot], out_hbm.at[lev], out_sem.at[slot]).wait()

        def emit(k, _):
            r = pl.ds(pl.multiple_of(lev * rows + k * 16, 16), 16)
            ro = pl.ds(pl.multiple_of(k * 16, 16), 16)
            a0, a2, u, w = [acc[r, pl.ds(s * x4, x4)] for s in range(4)]
            e, o = a0 + a2, a0 - a2
            for s, x in enumerate((e + u, o + w, e - u, o - w)):
                out[slot, ro, pl.ds(s * x4, x4)] = x.astype(BF16)
            return 0

        lax.fori_loop(0, rows // 16, emit, 0)
        pltpu.make_async_copy(out.at[slot], out_hbm.at[lev], out_sem.at[slot]).start()
        return 0

    lax.fori_loop(0, levels, finish, 0)
    for lev in range(levels - min(2, levels), levels):
        pltpu.make_async_copy(out.at[lev % 2], out_hbm.at[lev], out_sem.at[lev % 2]).wait()


def fast_device(p, v, inverse_spacing, inverse_pivot, lower_factor, upper_factor):
    levels, rows, nx = p.shape
    n = lax.axis_size("gy")
    width, ny = nx // n, n * rows
    y4 = ny // 4
    pairs, chunks = levels // 2, nx // n // ROWS
    th, tl = [jnp.asarray(t) for t in along_table(nx, n)]
    yh, yl = [jnp.asarray(t) for t in across_table(ny)]
    anyspace = pl.BlockSpec(memory_space=pl.ANY)
    vmem = pl.BlockSpec(memory_space=pltpu.VMEM)
    dma = pltpu.SemaphoreType.DMA
    message = 4 * width + 16
    low, top, gain = pl.pallas_call(
        functools.partial(forward_kernel, n, levels, nx),
        out_shape=[
            jax.ShapeDtypeStruct((pairs, 4, 2 * width, 2 * y4), F32),
            jax.ShapeDtypeStruct((2, width, ny), F32),
            jax.ShapeDtypeStruct((width, ny), F32),
        ],
        in_specs=[vmem, anyspace, pl.BlockSpec(memory_space=pltpu.SMEM), vmem, vmem, vmem, vmem, anyspace, anyspace],
        out_specs=[anyspace, vmem, vmem],
        scratch_shapes=[
            pltpu.VMEM((levels + 1, rows, nx), BF16),
            pltpu.VMEM((2 * rows, nx), BF16),
            pltpu.VMEM((2 * rows, nx), BF16),
            pltpu.VMEM((2, n, message, 128), BF16),
            pltpu.VMEM((pairs, n, message, 128), BF16),
            pltpu.VMEM((4, 2 * width, 2 * y4), BF16),
            pltpu.VMEM((4, 2 * width, 2 * y4), BF16),
            pltpu.VMEM((4, 2 * width, 2 * y4), F32),
            pltpu.VMEM((ny // 128, 2, width, 128), F32),
            pltpu.VMEM((ny // 128, 2, width, 128), F32),
            dma, dma, dma,
            dma((pairs, n)), dma((pairs, n)), dma((pairs,)), dma((2, ny // 128)), dma,
        ],
        compiler_params=pltpu.CompilerParams(
            collective_id=0, has_side_effects=True, vmem_limit_bytes=62 * 2**20
        ),
        name="forward",
    )(p, v, inverse_spacing, th, tl, yh, yl, inverse_pivot, lower_factor)

    low = low.reshape(pairs, 4, 2, width, 2 * y4)
    message = levels * 2 * ROWS + 16
    per = 2 if chunks % 2 == 0 else 1
    count = levels * ROWS
    return pl.pallas_call(
        functools.partial(backward_kernel, n, levels, nx),
        out_shape=jax.ShapeDtypeStruct((levels, rows, nx), BF16),
        in_specs=[anyspace] * 5 + [vmem] * 4,
        out_specs=anyspace,
        scratch_shapes=[
            pltpu.VMEM((2, pairs, 4, 2, ROWS, 2 * y4), F32),
            pltpu.VMEM((2, ny // 128, levels, ROWS, 128), F32),
            pltpu.VMEM((2, ny // 128, levels, ROWS, 128), F32),
            pltpu.VMEM((2, 2, ROWS, ny), F32),
            pltpu.VMEM((2, ROWS, ny), F32),
            pltpu.VMEM((chunks, 2, ROWS, ny), F32),
            pltpu.VMEM((chunks, 2, ROWS, ny), F32),
            pltpu.VMEM((2, 2, ROWS, ny), F32),
            pltpu.VMEM((2, 2, ROWS, ny), F32),
            pltpu.VMEM((4, count, 2 * y4), BF16),
            pltpu.VMEM((4, count, 2 * y4), BF16),
            pltpu.VMEM((4, count, 2 * y4), F32),
            pltpu.VMEM((2, n, message, 128), BF16),
            pltpu.VMEM((chunks, n, message, 128), BF16),
            pltpu.VMEM((4, 2 * rows, per * 16 * n), BF16),
            pltpu.VMEM((4, 2 * rows, per * 16 * n), BF16),
            pltpu.VMEM((levels * rows, nx), F32),
            pltpu.VMEM((2, rows, nx), BF16),
            dma((2,)), dma((2, 2, ny // 128)), dma((2, 2)),
            dma((chunks,)), dma((chunks,)), dma((chunks,)), dma((chunks,)),
            dma((chunks, n)), dma((chunks, n)), dma((chunks,)), dma((2,)),
        ],
        compiler_params=pltpu.CompilerParams(
            collective_id=1, has_side_effects=True, vmem_limit_bytes=62 * 2**20
        ),
        name="backward",
    )(low, top, gain, lower_factor, upper_factor, th, tl, yh, yl)


def solution(mesh):
    spec = P("gz", "gy", None)

    def program(*arrays):
        levels, ny, nx = arrays[0].shape
        gy, gz = mesh.shape["gy"], mesh.shape["gz"]
        fast = ny // gy == 128 and gy % 4 == 0 and levels // gz % 2 == 0 and nx // gy % ROWS == 0
        return jax.shard_map(
            fast_device if fast else on_device,
            mesh=mesh,
            in_specs=(spec, spec, P("gz"), spec, spec, spec),
            out_specs=spec,
            check_vma=False,
        )(*arrays)

    return program
```

```python
import functools
import math

import jax
import jax.numpy as jnp
import ml_dtypes
import numpy as np
from jax import lax
from jax.experimental import pallas as pl
from jax.experimental.pallas import tpu as pltpu
from jax.sharding import PartitionSpec as P

PREC = lax.Precision.HIGH
F32 = jnp.float32


def passed_along(x, axis, by):
    size = lax.axis_size(axis)
    pairs = [(i, i + by) for i in range(size) if 0 <= i + by < size]
    return lax.ppermute(x, axis, pairs)


def unit_circle(phase, count):
    angle = (phase % count).astype(F32) * (2.0 * math.pi / count)
    return jnp.cos(angle), jnp.sin(angle)


def circle_table(count):
    low = 32
    high = count // low
    k = jnp.arange(count, dtype=jnp.int32)[None, :]
    ch, sh = unit_circle(jnp.arange(high, dtype=jnp.int32)[:, None] * low * k, count)
    cl, sl = unit_circle(jnp.arange(low, dtype=jnp.int32)[:, None] * k, count)
    ch, sh, cl, sl = lax.optimization_barrier((ch, sh, cl, sl))
    ch, sh, cl, sl = ch[:, None], sh[:, None], cl[None], sl[None]
    cosine = (ch * cl - sh * sl).reshape(count, count)
    sine = (sh * cl + ch * sl).reshape(count, count)
    return cosine, sine


def split_table(count, half):
    low = 32
    column = jnp.arange(2 * count, dtype=jnp.int32)[None, :]
    k = column // (2 * half) * half + column % half
    quarter = jnp.where(column % (2 * half) < half, 0, count // 4)
    ch, sh = unit_circle(jnp.arange(count // low, dtype=jnp.int32)[:, None] * low * k, count)
    cl, sl = unit_circle(jnp.arange(low, dtype=jnp.int32)[:, None] * k + quarter, count)
    ch, sh, cl, sl = lax.optimization_barrier((ch, sh, cl, sl))
    return (ch[:, None] * cl[None] - sh[:, None] * sl[None]).reshape(count, 2 * count)


def down_kernel(chunks, per, *refs):
    cos_refs, sin_refs = refs[:chunks], refs[chunks : 2 * chunks]
    pivot, lower, low, summary = refs[2 * chunks :]
    re = im = jnp.zeros(pivot.shape[1:], F32)
    gain = jnp.ones(pivot.shape[1:], F32)
    for z in range(chunks * per):
        c, s = cos_refs[z // per], sin_refs[z // per]
        q = z % per
        d, m = pivot[z], lower[z]
        re = d * (c[q, 0] + s[q, 1]) + m * re
        im = d * (c[q, 1] - s[q, 0]) + m * im
        gain = m * gain
        low[z, 0] = re
        low[z, 1] = im
    summary[0] = gain
    summary[1] = re
    summary[2] = im


def up_summary_kernel(levels, low, lower, upper, enter, summary):
    er, ei = enter[0, 0], enter[0, 1]
    re = im = jnp.zeros(lower.shape[1:], F32)
    gain = jnp.ones(lower.shape[1:], F32)
    carried = jnp.ones(lower.shape[1:], F32)
    for z in range(levels):
        carried = carried * lower[z]
        re = re + gain * (low[z, 0] + carried * er)
        im = im + gain * (low[z, 1] + carried * ei)
        gain = gain * upper[z]
    summary[0] = gain
    summary[1] = re
    summary[2] = im


def solve_kernel(levels, per, low, lower, upper, enter, above, *outs):
    er, ei = enter[0, 0], enter[0, 1]
    gains = []
    carried = jnp.ones(lower.shape[1:], F32)
    for z in range(levels):
        carried = carried * lower[z]
        gains.append(carried)
    re, im = above[0, 0], above[0, 1]
    for z in range(levels - 1, -1, -1):
        re = low[z, 0] + gains[z] * er + upper[z] * re
        im = low[z, 1] + gains[z] * ei + upper[z] * im
        outs[z // per][z % per, 0] = re
        outs[z // per][z % per, 1] = im


def entering(summary, reverse):
    count = lax.axis_size("gz")
    _, width, span = summary.shape
    parts = summary.reshape(3, count, width // count, span)
    got = lax.all_to_all(parts, "gz", split_axis=1, concat_axis=1, tiled=True)
    order = list(range(count))
    if reverse:
        order.reverse()
    states = [None] * count
    state = jnp.zeros((2, width // count, span), F32)
    for at in order:
        states[at] = state
        state = got[1:, at] + got[0, at][None] * state
    return lax.all_to_all(jnp.stack(states), "gz", split_axis=0, concat_axis=0, tiled=True)


def on_device(
    pressure_cotangent,
    velocity_cotangent,
    inverse_spacing,
    inverse_pivot,
    lower_factor,
    upper_factor,
):
    levels, rows, nx = pressure_cotangent.shape
    level_above = passed_along(velocity_cotangent[:1], "gz", -1)
    gy = lax.axis_size("gy")
    gz = lax.axis_size("gz")
    ny = rows * gy
    half = nx // gy
    per = 2 if levels % 2 == 0 else 1
    chunks = levels // per
    velocity = velocity_cotangent.astype(F32)
    shifted = jnp.concatenate([velocity[1:], level_above.astype(F32)], 0)
    source = pressure_cotangent.astype(F32) + inverse_spacing[:, None, None] * (shifted - velocity)

    table = lax.optimization_barrier(split_table(nx, half))
    cy, sy = lax.optimization_barrier(circle_table(ny))

    cos_parts, sin_parts = [], []
    for i in range(chunks):
        piece = source[i * per : (i + 1) * per]
        spec = jnp.einsum("zyn,nc->zyc", piece, table, precision=PREC)
        spec = jnp.transpose(spec.reshape(per, rows, gy, 2 * half), (2, 0, 1, 3))
        if i >= 2:
            spec, cos_parts[i - 2], sin_parts[i - 2] = lax.optimization_barrier(
                (spec, cos_parts[i - 2], sin_parts[i - 2])
            )
        got = lax.all_to_all(spec, "gy", split_axis=0, concat_axis=0, tiled=True)
        got = jnp.transpose(got, (1, 0, 2, 3)).reshape(per, ny, 2 * half)
        c = jnp.einsum("zyc,yk->zck", got, cy, precision=PREC)
        s = jnp.einsum("zyc,yk->zck", got, sy, precision=PREC)
        cos_parts.append(c.reshape(per, 2, half, ny))
        sin_parts.append(s.reshape(per, 2, half, ny))

    quarter = half // gz
    kb = min(16, quarter)
    in_quarter = quarter // kb
    grid = (half // kb,)
    chunk_spec = pl.BlockSpec((per, 2, kb, ny), lambda i: (0, 0, i, 0))
    factor_spec = pl.BlockSpec((levels, kb, ny), lambda i: (0, i, 0))
    low_spec = pl.BlockSpec((levels, 2, kb, ny), lambda i: (0, 0, i, 0))
    summary_spec = pl.BlockSpec((3, kb, ny), lambda i: (0, i, 0))
    state_spec = pl.BlockSpec((1, 2, kb, ny), lambda i: (i // in_quarter, 0, i % in_quarter, 0))
    summary_shape = jax.ShapeDtypeStruct((3, half, ny), F32)

    low, summary = pl.pallas_call(
        functools.partial(down_kernel, chunks, per),
        grid=grid,
        in_specs=[chunk_spec] * (2 * chunks) + [factor_spec] * 2,
        out_specs=[low_spec, summary_spec],
        out_shape=[jax.ShapeDtypeStruct((levels, 2, half, ny), F32), summary_shape],
    )(*cos_parts, *sin_parts, inverse_pivot, lower_factor)
    enter = entering(summary, False)
    summary = pl.pallas_call(
        functools.partial(up_summary_kernel, levels),
        grid=grid,
        in_specs=[low_spec, factor_spec, factor_spec, state_spec],
        out_specs=summary_spec,
        out_shape=summary_shape,
    )(low, lower_factor, upper_factor, enter)
    above = entering(summary, True)
    solved = pl.pallas_call(
        functools.partial(solve_kernel, levels, per),
        grid=grid,
        in_specs=[low_spec, factor_spec, factor_spec, state_spec, state_spec],
        out_specs=[chunk_spec] * chunks,
        out_shape=[jax.ShapeDtypeStruct((per, 2, half, ny), F32)] * chunks,
    )(low, lower_factor, upper_factor, enter, above)

    normalizer = 1.0 / (nx * ny)
    fields = []
    for i in range(chunks):
        flat = solved[i].reshape(per, 2 * half, ny)
        c = jnp.einsum("ky,zck->zyc", cy, flat, precision=PREC)
        s = jnp.einsum("ky,zck->zyc", sy, flat, precision=PREC)
        back = jnp.concatenate([c[..., :half] - s[..., half:], c[..., half:] + s[..., :half]], 2)
        back = jnp.transpose(back.reshape(per, gy, rows, 2 * half), (1, 0, 2, 3))
        if i >= 2:
            back, fields[i - 2] = lax.optimization_barrier((back, fields[i - 2]))
        got = lax.all_to_all(back, "gy", split_axis=0, concat_axis=0, tiled=True)
        got = jnp.transpose(got, (1, 2, 0, 3)).reshape(per, rows, 2 * nx)
        field = jnp.einsum("zyc,nc->zyn", got, table, precision=PREC) * normalizer
        fields.append(field.astype(jnp.bfloat16))
    return jnp.concatenate(fields, 0)


BF16 = jnp.bfloat16
MESH = pl.DeviceIdType.MESH
TINY = 1e-36
PEAK = 2.0**14
ROWS = 32
NT = (((1,), (1,)), ((), ()))
NN = (((1,), (0,)), ((), ()))


def split(x):
    high = x.astype(BF16)
    return high, (x - high.astype(F32)).astype(BF16)


def split_host(x):
    high = x.astype(np.float32).astype(ml_dtypes.bfloat16)
    low = (x - high.astype(np.float64)).astype(np.float32).astype(ml_dtypes.bfloat16)
    return high, low


def along_table(nx, gy):
    width = nx // gy
    chunk, g, j = np.meshgrid(np.arange(width // ROWS), np.arange(gy), np.arange(8), indexing="ij")
    parts = []
    for q in (0, 2, 1, 3):
        kx = g * width + ROWS * chunk + 4 * j + q
        turn = 2 * np.pi * ((kx[..., None] * np.arange(nx // 4)) % nx) / nx
        c, s = np.cos(turn), np.sin(turn)
        pair = np.stack([c, -s], 2)
        if q == 1:
            pair = np.concatenate([pair, np.stack([-s, -c], 2)], -1)
        if q == 3:
            pair = np.concatenate([pair, np.stack([s, c], 2)], -1)
        parts.append(pair.reshape(-1, pair.shape[-1]))
    return split_host(np.concatenate(parts, 1))


def across_table(ny):
    quarter = ny // 4
    lane = np.arange(quarter)
    block, inner = lane // 128, lane % 128
    tables = []
    for q in range(4):
        ky = 512 * block + 128 * (inner % 4) + 4 * (inner // 4) + q
        turn = 2 * np.pi * ((np.arange(quarter)[:, None] * ky) % ny) / ny
        c, s = np.cos(turn), np.sin(turn)
        tables.append(np.block([[c, -s], [s, c]]))
    return split_host(np.stack(tables))


def exchange_lanes(vs):
    lane = lax.broadcasted_iota(jnp.int32, vs[0].shape, 1)
    odd, upper = lane % 2 == 1, lane % 4 >= 2

    def turned(xs, sign):
        xs = [jnp.where(odd, xs[(d + sign) % 4], xs[d]) for d in range(4)]
        return [jnp.where(upper, xs[(d + 2) % 4], xs[d]) for d in range(4)]

    ds = turned([vs[-d % 4] for d in range(4)], -1)
    es = [ds[0]] + [
        jnp.take_along_axis(ds[d], lane // 4 * 4 + (lane + d) % 4, axis=1) for d in range(1, 4)
    ]
    return turned(es, -1)


def encode(v):
    v2 = v * v
    v4 = v2 * v2
    return (v4 * v4 * v).astype(BF16)


def decode(w, scale):
    w = w.astype(F32)
    size = jnp.maximum(jnp.abs(w), 2.0**-126)
    return w * jnp.exp2(jnp.log(size) * (-8.0 / (9.0 * math.log(2.0)))) * scale


def dot3(ah, al, bh, bl, dims):
    def one(a, b):
        return lax.dot_general(a, b, dims, preferred_element_type=F32)

    return one(ah, bh) + one(al, bh) + one(ah, bl)


def greet(devices):
    barrier = pltpu.get_barrier_semaphore()
    for device in devices:
        pl.semaphore_signal(barrier, inc=1, device_id=device, device_id_type=MESH)


def forward_kernel(
    n, levels, nx,
    p_ref, v_hbm, spacing, th, tl, yh, yl, pivot_hbm, lower_hbm,
    low_hbm, top, gain,
    v_all, ah, al, stage, got, bh, bl, spec, pivot, lower,
    v_sem, edge_send, edge_recv, send_sem, recv_sem, own_sem, factor_sem, low_sem,
):
    me, z, zs = lax.axis_index("gy"), lax.axis_index("gz"), lax.axis_size("gz")
    rows = p_ref.shape[1]
    x4 = nx // 4
    width = nx // n
    chunks = width // ROWS
    y4 = n * rows // 4
    pairs = levels // 2
    body = 4 * width

    v_copy = pltpu.make_async_copy(v_hbm, v_all.at[pl.ds(0, levels)], v_sem)
    v_copy.start()
    barrier = pltpu.get_barrier_semaphore()
    greet([{"gy": lax.rem(me + d, n)} for d in range(1, n)])

    @pl.when(z < zs - 1)
    def _():
        greet([{"gz": z + 1}])

    pl.semaphore_wait(barrier, n - 1 + jnp.minimum(z, 1))

    def edge():
        return pltpu.make_async_remote_copy(
            src_ref=v_hbm.at[pl.ds(0, 1)], dst_ref=v_all.at[pl.ds(levels, 1)],
            send_sem=edge_send, recv_sem=edge_recv, device_id={"gz": z - 1}, device_id_type=MESH,
        )

    @pl.when(z > 0)
    def _():
        edge().start()

    @pl.when(z == zs - 1)
    def _():
        v_all[levels] = jnp.zeros((rows, nx), BF16)

    top[...] = jnp.zeros_like(top)
    gain[...] = jnp.ones_like(gain)

    def factors(lp):
        return [
            pltpu.make_async_copy(
                hbm.at[pl.ds(2 * lp, 2), :, pl.ds(128 * k, 128)], ref.at[k], factor_sem.at[i, k]
            )
            for i, (hbm, ref) in enumerate(((pivot_hbm, pivot), (lower_hbm, lower)))
            for k in range(y4 // 32)
        ]

    for copy in factors(0):
        copy.start()
    v_copy.wait()

    def own(lp):
        return pltpu.make_async_copy(stage.at[lax.rem(lp, 2), me], got.at[lp, me], own_sem.at[lp])

    def send(lp, d):
        peer = lax.rem(me + d, n)
        return pltpu.make_async_remote_copy(
            src_ref=stage.at[lax.rem(lp, 2), peer], dst_ref=got.at[lp, me],
            send_sem=send_sem.at[lp, d], recv_sem=recv_sem.at[lp, me],
            device_id={"gy": peer}, device_id_type=MESH,
        )

    def arrival(lp, d):
        peer = lax.rem(me + d, n)
        return pltpu.make_async_remote_copy(
            src_ref=stage.at[lax.rem(lp, 2), peer], dst_ref=got.at[lp, peer],
            send_sem=send_sem.at[lp, d], recv_sem=recv_sem.at[lp, peer],
            device_id={"gy": peer}, device_id_type=MESH,
        )

    def low_copy(lp):
        return pltpu.make_async_copy(spec, low_hbm.at[lp], low_sem)

    def spectra(lp):
        @pl.when(lp >= 2)
        def _():
            for d in range(1, n):
                send(lp - 2, d).wait_send()

        @pl.when((lp == pairs - 1) & (z < zs - 1))
        def _():
            edge().wait_recv()

        tile = 16
        peak = jnp.zeros((8, 128), F32)
        for lev in range(2):
            at = 2 * lp + lev
            factor = spacing[at]

            def source(i, peak, lev=lev, at=at, factor=factor):
                r = pl.ds(pl.multiple_of(i * tile, tile), tile)
                q = [pl.ds(k * x4, x4) for k in range(4)]
                xs = [
                    p_ref[at, r, s].astype(F32)
                    + factor * (v_all[at + 1, r, s].astype(F32) - v_all[at, r, s].astype(F32))
                    for s in q
                ]
                size = functools.reduce(jnp.maximum, [jnp.abs(x) for x in xs])
                e, o = xs[0] + xs[2], xs[1] + xs[3]
                to = pl.ds(pl.multiple_of(lev * rows + i * tile, tile), tile)
                for s, a in zip(q, (e + o, e - o, xs[0] - xs[2], xs[1] - xs[3])):
                    ah[to, s], al[to, s] = split(a)
                for k in range(x4 // 128):
                    part = size[:, k * 128 : (k + 1) * 128]
                    peak = jnp.maximum(peak, jnp.maximum(part[:8], part[8:]))
                return peak

            peak = lax.fori_loop(0, rows // tile, source, peak)
        peak = jnp.maximum(jnp.max(peak), TINY)
        held = jnp.full((16, 128), peak, F32).astype(BF16)
        shrink = PEAK / (nx * held.astype(F32)[:1, :1])
        slot = lax.rem(lp, 2)
        for g in range(n):
            stage[slot, g, pl.ds(body, 16), :] = held

        per = 2 if chunks % 2 == 0 else 1
        tall = per * 16 * n

        def transform(i, _):
            m = pl.ds(pl.multiple_of(i * tall, tall), tall)
            outs, at = [None] * 4, 0
            for q in (0, 2, 1, 3):
                wide = x4 if q % 2 == 0 else 2 * x4
                start = (0, 2 * x4, x4, 2 * x4)[q]
                t, a = pl.ds(at, wide), pl.ds(start, wide)
                outs[q] = dot3(th[m, t], tl[m, t], ah[:, a], al[:, a], NT) * shrink
                at += wide
            for k in range(per):
                for g in range(n):
                    for c in range(2):
                        s = (k * n + g) * 16 + c * 8
                        block = encode(jnp.concatenate([o[s : s + 8] for o in outs], 0))
                        for lev in range(2):
                            r = (lev * 2 + c) * width + (i * per + k) * ROWS
                            stage[slot, g, pl.ds(pl.multiple_of(r, ROWS), ROWS), :] = block[
                                :, lev * rows : (lev + 1) * rows
                            ]
            return 0

        lax.fori_loop(0, chunks // per, transform, 0)
        own(lp).start()
        for d in range(1, n):
            send(lp, d).start()

    def substitute(lp):
        own(lp).wait()
        for d in range(1, n):
            arrival(lp, d).wait_recv()

        tile = 16
        quads = n // 4
        scales = [got[lp, s, pl.ds(body, 16), :].astype(F32)[:1, :] * (nx / PEAK) for s in range(n)]

        def unpack(i, _):
            for lev in range(2):
                for h in range(quads):
                    xs = []
                    for c in range(2):
                        r = pl.ds(pl.multiple_of((lev * 2 + c) * width + i * tile, tile), tile)
                        xs.append([decode(got[lp, k * quads + h, r, :], scales[k * quads + h]) for k in range(4)])
                    (r0, r1, r2, r3), (i0, i1, i2, i3) = xs
                    er, fr, ei, fi = r0 + r2, r0 - r2, i0 + i2, i0 - i2
                    gr, hr, gi, hi = r1 + r3, r1 - r3, i1 + i3, i1 - i3
                    real = (er + gr, fr + hi, er - gr, fr - hi)
                    imag = (ei + gi, fi - hr, ei - gi, fi + hr)
                    to = pl.ds(pl.multiple_of(lev * width + i * tile, tile), tile)
                    for q in range(4):
                        for c, x in enumerate((real[q], imag[q])):
                            s = pl.ds(c * y4 + h * 128, 128)
                            bh[q, to, s], bl[q, to, s] = split(x)
            return 0

        lax.fori_loop(0, width // tile, unpack, 0)

        @pl.when(lp > 0)
        def _():
            low_copy(lp - 1).wait()

        tall = min(width, 256)

        def transform(i, _):
            r = pl.ds(pl.multiple_of(i * tall, tall), tall)
            for k in range(2 * y4 // 256):
                w = pl.ds(k * 256, 256)
                parts = [dot3(bh[q, r, :], bl[q, r, :], yh[q, :, w], yl[q, :, w], NN) for q in range(4)]
                for j in range(2):
                    for t, x in enumerate(exchange_lanes([x[:, j * 128 : (j + 1) * 128] for x in parts])):
                        spec[t, r, pl.ds(k * 256 + j * 128, 128)] = x
            return 0

        lax.fori_loop(0, 2 * width // tall, transform, 0)
        for copy in factors(lp):
            copy.wait()

        def solve(i, _):
            r = pl.ds(pl.multiple_of(i * ROWS, ROWS), ROWS)
            strided = [pl.ds(i * ROWS + q, 8, stride=4) for q in range(4)]
            for b in range(y4 // 128):
                for t in range(4):
                    s = pl.ds(512 * b + 128 * t, 128)
                    lanes = [pl.ds(c * y4 + b * 128, 128) for c in range(2)]
                    rl = [pl.ds(pl.multiple_of(lev * width + i * ROWS, ROWS), ROWS) for lev in range(2)]
                    ms, ds = [
                        [jnp.concatenate([f[4 * b + t, lev, x, :] for x in strided], 0) for lev in range(2)]
                        for f in (lower, pivot)
                    ]
                    xs = [[spec[t, rl[lev], lanes[c]] for c in range(2)] for lev in range(2)]
                    held, run = [top[c, r, s] for c in range(2)], gain[r, s]
                    first = [ds[0] * xs[0][c] + ms[0] * held[c] for c in range(2)]
                    second = [ds[1] * xs[1][c] + ms[1] * first[c] for c in range(2)]
                    gain[r, s] = run * ms[0] * ms[1]
                    for c in range(2):
                        spec[t, rl[0], lanes[c]] = first[c]
                        spec[t, rl[1], lanes[c]] = second[c]
                        top[c, r, s] = second[c]
            return 0

        lax.fori_loop(0, chunks, solve, 0)
        low_copy(lp).start()

        @pl.when(lp < pairs - 1)
        def _():
            for copy in factors(lp + 1):
                copy.start()

    def step(t, _):
        @pl.when(t < pairs)
        def _():
            spectra(t)

        @pl.when(t >= 1)
        def _():
            substitute(t - 1)

        return 0

    lax.fori_loop(0, pairs + 1, step, 0)
    low_copy(pairs - 1).wait()
    for lp in range(max(pairs - 2, 0), pairs):
        for d in range(1, n):
            send(lp, d).wait_send()

    @pl.when(z > 0)
    def _():
        edge().wait_send()


def backward_kernel(
    n, levels, nx,
    low_hbm, top_hbm, gain_hbm, lower_hbm, upper_hbm, th, tl, yh, yl,
    out_hbm,
    low, lower, upper, top, gain, enter, above, d_send, u_send, sh, sl, yo, stage, got, xh, xl, acc, out,
    low_sem, load_sem, sum_sem, ds_sem, dr_sem, us_sem, ur_sem, send_sem, recv_sem, own_sem, out_sem,
):
    me, z, zs = lax.axis_index("gy"), lax.axis_index("gz"), lax.axis_size("gz")
    width = nx // n
    chunks = width // ROWS
    rows = out_hbm.shape[1]
    ny = n * rows
    y4, x4 = ny // 4, nx // 4
    body = levels * 2 * ROWS
    per = 2 if chunks % 2 == 0 else 1

    def loads(c):
        slot = lax.rem(c, 2)
        r = pl.ds(pl.multiple_of(c * ROWS, ROWS), ROWS)
        return [
            pltpu.make_async_copy(low_hbm.at[:, :, :, r, :], low.at[slot], low_sem.at[slot]),
        ] + [
            pltpu.make_async_copy(hbm.at[:, r, pl.ds(128 * k, 128)], ref.at[slot, k], load_sem.at[slot, i, k])
            for i, (hbm, ref) in enumerate(((lower_hbm, lower), (upper_hbm, upper)))
            for k in range(ny // 128)
        ]

    def sums(c):
        slot = lax.rem(c, 2)
        r = pl.ds(pl.multiple_of(c * ROWS, ROWS), ROWS)
        return [
            pltpu.make_async_copy(top_hbm.at[:, r, :], top.at[slot], sum_sem.at[slot, 0]),
            pltpu.make_async_copy(gain_hbm.at[r, :], gain.at[slot], sum_sem.at[slot, 1]),
        ]

    for copy in sums(0) + loads(0):
        copy.start()
    acc[...] = jnp.zeros_like(acc)

    barrier = pltpu.get_barrier_semaphore()
    greet([{"gy": lax.rem(me + d, n)} for d in range(1, n)])

    @pl.when(z < zs - 1)
    def _():
        greet([{"gz": z + 1}])

    @pl.when(z > 0)
    def _():
        greet([{"gz": z - 1}])

    pl.semaphore_wait(barrier, n - 1 + jnp.minimum(z, 1) + jnp.minimum(zs - 1 - z, 1))

    @pl.when(z == 0)
    def _():
        enter[...] = jnp.zeros_like(enter)

    @pl.when(z == zs - 1)
    def _():
        above[...] = jnp.zeros_like(above)

    def pass_down(c):
        return pltpu.make_async_remote_copy(
            src_ref=d_send.at[lax.rem(c, 2)], dst_ref=enter.at[c], send_sem=ds_sem.at[c], recv_sem=dr_sem.at[c],
            device_id={"gz": z + 1}, device_id_type=MESH,
        )

    def pass_up(c):
        return pltpu.make_async_remote_copy(
            src_ref=u_send.at[lax.rem(c, 2)], dst_ref=above.at[c], send_sem=us_sem.at[c], recv_sem=ur_sem.at[c],
            device_id={"gz": z - 1}, device_id_type=MESH,
        )

    def own(c):
        return pltpu.make_async_copy(stage.at[lax.rem(c, 2), me], got.at[c, me], own_sem.at[c])

    def send(c, d):
        peer = lax.rem(me + d, n)
        return pltpu.make_async_remote_copy(
            src_ref=stage.at[lax.rem(c, 2), peer], dst_ref=got.at[c, me],
            send_sem=send_sem.at[c, d], recv_sem=recv_sem.at[c, me],
            device_id={"gy": peer}, device_id_type=MESH,
        )

    def arrival(c, d):
        peer = lax.rem(me + d, n)
        return pltpu.make_async_remote_copy(
            src_ref=stage.at[lax.rem(c, 2), peer], dst_ref=got.at[c, peer],
            send_sem=send_sem.at[c, d], recv_sem=recv_sem.at[c, peer],
            device_id={"gy": peer}, device_id_type=MESH,
        )

    def relay(c):
        for copy in sums(c):
            copy.wait()

        @pl.when(c + 1 < chunks)
        def _():
            for copy in sums(c + 1):
                copy.start()

        @pl.when(z > 0)
        def _():
            pass_down(c).wait_recv()

        @pl.when(z < zs - 1)
        def _():
            @pl.when(c >= 2)
            def _():
                pass_down(c - 2).wait_send()

            slot = lax.rem(c, 2)

            def carry(i, _):
                r = pl.ds(pl.multiple_of(i * 8, 8), 8)
                for k in range(2):
                    d_send[slot, k, r, :] = top[slot, k, r, :] + gain[slot, r, :] * enter[c, k, r, :]
                return 0

            lax.fori_loop(0, ROWS // 8, carry, 0)
            pass_down(c).start()

    def solve(c):
        slot = lax.rem(c, 2)
        for copy in loads(c):
            copy.wait()

        @pl.when(c + 1 < chunks)
        def _():
            for copy in loads(c + 1):
                copy.start()

        @pl.when(z < zs - 1)
        def _():
            pass_up(c).wait_recv()

        @pl.when((z > 0) & (c >= 2))
        def _():
            pass_up(c - 2).wait_send()

        def sweep(q, _):
            strided = pl.ds(q, 8, stride=4)
            r = pl.ds(pl.multiple_of(q * 8, 8), 8)
            for b in range(y4 // 128):
                natural = [pl.ds(512 * b + 128 * t, 128) for t in range(4)]
                gains = [[] for _ in range(4)]
                for t in range(4):
                    for lev in range(levels):
                        m = lower[slot, 4 * b + t, lev, strided, :]
                        gains[t].append(m if lev == 0 else gains[t][-1] * m)
                state = [[above[c, k, r, s] for s in natural] for k in range(2)]
                entry = [[enter[c, k, r, s] for s in natural] for k in range(2)]
                for lev in range(levels - 1, -1, -1):
                    ups = [upper[slot, 4 * b + t, lev, strided, :] for t in range(4)]
                    for k in range(2):
                        lanes = pl.ds(k * y4 + b * 128, 128)
                        state[k] = [
                            low[slot, lev // 2, t, lev % 2, r, lanes] + gains[t][lev] * entry[k][t] + ups[t] * state[k][t]
                            for t in range(4)
                        ]
                        to = pl.ds(pl.multiple_of(lev * ROWS + q * 8, 8), 8)
                        for t in range(4):
                            yo[t, to, lanes] = state[k][t]
                for k in range(2):
                    for t in range(4):
                        u_send[slot, k, r, natural[t]] = state[k][t]
            return 0

        lax.fori_loop(0, ROWS // 8, sweep, 0)

        @pl.when(z > 0)
        def _():
            pass_up(c).start()

        @pl.when(c >= 2)
        def _():
            own(c - 2).wait()
            for d in range(1, n):
                send(c - 2, d).wait_send()

        count = levels * ROWS

        def halve(i, _):
            r = pl.ds(pl.multiple_of(i * ROWS, ROWS), ROWS)
            for k in range(2 * y4 // 128):
                s = pl.ds(k * 128, 128)
                for q, x in enumerate(exchange_lanes([yo[t, r, s] for t in range(4)])):
                    sh[q, r, s], sl[q, r, s] = split(x)
            return 0

        lax.fori_loop(0, levels, halve, 0)

        def transform(q, _):
            yo[q] = dot3(sh[q], sl[q], yh[q], yl[q], NT)
            return 0

        lax.fori_loop(0, 4, transform, 0)

        def combine(i, peak):
            r = pl.ds(pl.multiple_of(i * 8, 8), 8)
            for h in range(y4 // 128):
                rs = pl.ds(h * 128, 128)
                cs = pl.ds(y4 + h * 128, 128)
                r0, r1, r2, r3 = [yo[q, r, rs] for q in range(4)]
                i0, i1, i2, i3 = [yo[q, r, cs] for q in range(4)]
                er, fr, ei, fi = r0 + r2, r0 - r2, i0 + i2, i0 - i2
                gr, hr, gi, hi = r1 + r3, r1 - r3, i1 + i3, i1 - i3
                real = (er + gr, fr - hi, er - gr, fr + hi)
                imag = (ei + gi, fi + hr, ei - gi, fi - hr)
                for q in range(4):
                    yo[q, r, rs] = real[q]
                    yo[q, r, cs] = imag[q]
                    peak = jnp.maximum(peak, jnp.maximum(jnp.abs(real[q]), jnp.abs(imag[q])))
            return peak

        peak = lax.fori_loop(0, count // 8, combine, jnp.zeros((8, 128), F32))
        held = jnp.full((16, 128), jnp.maximum(jnp.max(peak), TINY), F32).astype(BF16)
        shrink = PEAK / held.astype(F32)[:1, :1]
        quads = n // 4
        for g in range(n):
            stage[slot, g, pl.ds(body, 16), :] = held

        def pack(lev, _):
            r = pl.ds(pl.multiple_of(lev * ROWS, ROWS), ROWS)
            for g in range(n):
                for k in range(2):
                    x = yo[g // quads, r, pl.ds(k * y4 + (g % quads) * 128, 128)]
                    to = pl.ds(pl.multiple_of((lev * 2 + k) * ROWS, ROWS), ROWS)
                    stage[slot, g, to, :] = encode(x * shrink)
            return 0

        lax.fori_loop(0, levels, pack, 0)
        own(c).start()
        for d in range(1, n):
            send(c, d).start()

    def gather(pair):
        for k in range(per):
            c = pair * per + k

            for d in range(1, n):
                arrival(c, d).wait_recv()

        scales = [
            [got[pair * per + k, s, pl.ds(body, 16), :].astype(F32)[:1, :] * (1.0 / (PEAK * nx * ny)) for s in range(n)]
            for k in range(per)
        ]
        deep = per * 16 * n

        def two_levels(lp, _):
            for lev in range(2):
                for k in range(per):
                    parts = []
                    for s in range(n):
                        for j in range(2):
                            r = ((lp * 2 + lev) * 2 + j) * ROWS
                            r = pl.ds(pl.multiple_of(r, ROWS), ROWS)
                            parts.append(decode(got[pair * per + k, s, r, :], scales[k][s]))
                    for q in range(4):
                        block = jnp.concatenate([x[q * 8 : q * 8 + 8] for x in parts], 0)
                        high, low_part = split(block.T)
                        lanes = pl.ds(k * 16 * n, 16 * n)
                        xh[q, pl.ds(lev * rows, rows), lanes] = high
                        xl[q, pl.ds(lev * rows, rows), lanes] = low_part
            m = pl.ds(pl.multiple_of(pair * deep, deep), deep)
            to = pl.ds(pl.multiple_of(lp * 2 * rows, 2 * rows), 2 * rows)

            def part(q, start, wide):
                t = pl.ds(start, wide)
                return dot3(xh[q], xl[q], th[m, t], tl[m, t], NN)

            acc[to, pl.ds(0, x4)] += part(0, 0, x4)
            acc[to, pl.ds(x4, x4)] += part(2, x4, x4)
            acc[to, pl.ds(2 * x4, 2 * x4)] += part(1, 2 * x4, 2 * x4) + part(3, 4 * x4, 2 * x4)
            return 0

        lax.fori_loop(0, levels // 2, two_levels, 0)

    lag = 2 * (zs - 1)
    halves = chunks // per

    def step(t, _):
        down = t - z

        @pl.when((down >= 0) & (down < chunks))
        def _():
            relay(down)

        c = t - lag + z

        @pl.when((c >= 0) & (c < chunks))
        def _():
            solve(c)

        @pl.when((c >= 2 * per - 1) & (c < chunks) & (lax.rem(c + 1 + 2 * per, per) == 0))
        def _():
            gather((c + 1) // per - 2)

        return 0

    last = chunks - 1
    lax.fori_loop(0, chunks + lag, step, 0)
    for c in range(max(chunks - 2, 0), chunks):
        own(c).wait()
        for d in range(1, n):
            send(c, d).wait_send()

        @pl.when(z < zs - 1)
        def _():
            pass_down(c).wait_send()

        @pl.when(z > 0)
        def _():
            pass_up(c).wait_send()

    gather(halves - 1)

    def finish(i, _):
        lev = i
        r = pl.ds(pl.multiple_of(lev * rows, rows), rows)
        slot = lax.rem(lev, 2)

        @pl.when(lev >= 2)
        def _():
            pltpu.make_async_copy(out.at[slot], out_hbm.at[lev], out_sem.at[slot]).wait()

        def emit(k, _):
            r = pl.ds(pl.multiple_of(lev * rows + k * 16, 16), 16)
            ro = pl.ds(pl.multiple_of(k * 16, 16), 16)
            a0, a2, u, w = [acc[r, pl.ds(s * x4, x4)] for s in range(4)]
            e, o = a0 + a2, a0 - a2
            for s, x in enumerate((e + u, o + w, e - u, o - w)):
                out[slot, ro, pl.ds(s * x4, x4)] = x.astype(BF16)
            return 0

        lax.fori_loop(0, rows // 16, emit, 0)
        pltpu.make_async_copy(out.at[slot], out_hbm.at[lev], out_sem.at[slot]).start()
        return 0

    lax.fori_loop(0, levels, finish, 0)
    for lev in range(levels - min(2, levels), levels):
        pltpu.make_async_copy(out.at[lev % 2], out_hbm.at[lev], out_sem.at[lev % 2]).wait()


def fast_device(p, v, inverse_spacing, inverse_pivot, lower_factor, upper_factor):
    levels, rows, nx = p.shape
    n = lax.axis_size("gy")
    width, ny = nx // n, n * rows
    y4 = ny // 4
    pairs, chunks = levels // 2, nx // n // ROWS
    th, tl = [jnp.asarray(t) for t in along_table(nx, n)]
    yh, yl = [jnp.asarray(t) for t in across_table(ny)]
    anyspace = pl.BlockSpec(memory_space=pl.ANY)
    vmem = pl.BlockSpec(memory_space=pltpu.VMEM)
    dma = pltpu.SemaphoreType.DMA
    message = 4 * width + 16
    low, top, gain = pl.pallas_call(
        functools.partial(forward_kernel, n, levels, nx),
        out_shape=[
            jax.ShapeDtypeStruct((pairs, 4, 2 * width, 2 * y4), F32),
            jax.ShapeDtypeStruct((2, width, ny), F32),
            jax.ShapeDtypeStruct((width, ny), F32),
        ],
        in_specs=[vmem, anyspace, pl.BlockSpec(memory_space=pltpu.SMEM), vmem, vmem, vmem, vmem, anyspace, anyspace],
        out_specs=[anyspace, vmem, vmem],
        scratch_shapes=[
            pltpu.VMEM((levels + 1, rows, nx), BF16),
            pltpu.VMEM((2 * rows, nx), BF16),
            pltpu.VMEM((2 * rows, nx), BF16),
            pltpu.VMEM((2, n, message, 128), BF16),
            pltpu.VMEM((pairs, n, message, 128), BF16),
            pltpu.VMEM((4, 2 * width, 2 * y4), BF16),
            pltpu.VMEM((4, 2 * width, 2 * y4), BF16),
            pltpu.VMEM((4, 2 * width, 2 * y4), F32),
            pltpu.VMEM((ny // 128, 2, width, 128), F32),
            pltpu.VMEM((ny // 128, 2, width, 128), F32),
            dma, dma, dma,
            dma((pairs, n)), dma((pairs, n)), dma((pairs,)), dma((2, ny // 128)), dma,
        ],
        compiler_params=pltpu.CompilerParams(
            collective_id=0, has_side_effects=True, vmem_limit_bytes=62 * 2**20
        ),
        name="forward",
    )(p, v, inverse_spacing, th, tl, yh, yl, inverse_pivot, lower_factor)

    low = low.reshape(pairs, 4, 2, width, 2 * y4)
    message = levels * 2 * ROWS + 16
    per = 2 if chunks % 2 == 0 else 1
    count = levels * ROWS
    return pl.pallas_call(
        functools.partial(backward_kernel, n, levels, nx),
        out_shape=jax.ShapeDtypeStruct((levels, rows, nx), BF16),
        in_specs=[anyspace] * 5 + [vmem] * 4,
        out_specs=anyspace,
        scratch_shapes=[
            pltpu.VMEM((2, pairs, 4, 2, ROWS, 2 * y4), F32),
            pltpu.VMEM((2, ny // 128, levels, ROWS, 128), F32),
            pltpu.VMEM((2, ny // 128, levels, ROWS, 128), F32),
            pltpu.VMEM((2, 2, ROWS, ny), F32),
            pltpu.VMEM((2, ROWS, ny), F32),
            pltpu.VMEM((chunks, 2, ROWS, ny), F32),
            pltpu.VMEM((chunks, 2, ROWS, ny), F32),
            pltpu.VMEM((2, 2, ROWS, ny), F32),
            pltpu.VMEM((2, 2, ROWS, ny), F32),
            pltpu.VMEM((4, count, 2 * y4), BF16),
            pltpu.VMEM((4, count, 2 * y4), BF16),
            pltpu.VMEM((4, count, 2 * y4), F32),
            pltpu.VMEM((2, n, message, 128), BF16),
            pltpu.VMEM((chunks, n, message, 128), BF16),
            pltpu.VMEM((4, 2 * rows, per * 16 * n), BF16),
            pltpu.VMEM((4, 2 * rows, per * 16 * n), BF16),
            pltpu.VMEM((levels * rows, nx), F32),
            pltpu.VMEM((2, rows, nx), BF16),
            dma((2,)), dma((2, 2, ny // 128)), dma((2, 2)),
            dma((chunks,)), dma((chunks,)), dma((chunks,)), dma((chunks,)),
            dma((chunks, n)), dma((chunks, n)), dma((chunks,)), dma((2,)),
        ],
        compiler_params=pltpu.CompilerParams(
            collective_id=1, has_side_effects=True, vmem_limit_bytes=62 * 2**20
        ),
        name="backward",
    )(low, top, gain, lower_factor, upper_factor, th, tl, yh, yl)


def solution(mesh):
    spec = P("gz", "gy", None)

    def program(*arrays):
        levels, ny, nx = arrays[0].shape
        gy, gz = mesh.shape["gy"], mesh.shape["gz"]
        fast = ny // gy == 128 and gy % 4 == 0 and levels // gz % 2 == 0 and nx // gy % ROWS == 0
        return jax.shard_map(
            fast_device if fast else on_device,
            mesh=mesh,
            in_specs=(spec, spec, P("gz"), spec, spec, spec),
            out_specs=spec,
            check_vma=False,
        )(*arrays)

    return program
```

```python
import functools
import math

import jax
import jax.numpy as jnp
import ml_dtypes
import numpy as np
from jax import lax
from jax.experimental import pallas as pl
from jax.experimental.pallas import tpu as pltpu
from jax.sharding import PartitionSpec as P

PREC = lax.Precision.HIGH
F32 = jnp.float32


def passed_along(x, axis, by):
    size = lax.axis_size(axis)
    pairs = [(i, i + by) for i in range(size) if 0 <= i + by < size]
    return lax.ppermute(x, axis, pairs)


def unit_circle(phase, count):
    angle = (phase % count).astype(F32) * (2.0 * math.pi / count)
    return jnp.cos(angle), jnp.sin(angle)


def circle_table(count):
    low = 32
    high = count // low
    k = jnp.arange(count, dtype=jnp.int32)[None, :]
    ch, sh = unit_circle(jnp.arange(high, dtype=jnp.int32)[:, None] * low * k, count)
    cl, sl = unit_circle(jnp.arange(low, dtype=jnp.int32)[:, None] * k, count)
    ch, sh, cl, sl = lax.optimization_barrier((ch, sh, cl, sl))
    ch, sh, cl, sl = ch[:, None], sh[:, None], cl[None], sl[None]
    cosine = (ch * cl - sh * sl).reshape(count, count)
    sine = (sh * cl + ch * sl).reshape(count, count)
    return cosine, sine


def split_table(count, half):
    low = 32
    column = jnp.arange(2 * count, dtype=jnp.int32)[None, :]
    k = column // (2 * half) * half + column % half
    quarter = jnp.where(column % (2 * half) < half, 0, count // 4)
    ch, sh = unit_circle(jnp.arange(count // low, dtype=jnp.int32)[:, None] * low * k, count)
    cl, sl = unit_circle(jnp.arange(low, dtype=jnp.int32)[:, None] * k + quarter, count)
    ch, sh, cl, sl = lax.optimization_barrier((ch, sh, cl, sl))
    return (ch[:, None] * cl[None] - sh[:, None] * sl[None]).reshape(count, 2 * count)


def down_kernel(chunks, per, *refs):
    cos_refs, sin_refs = refs[:chunks], refs[chunks : 2 * chunks]
    pivot, lower, low, summary = refs[2 * chunks :]
    re = im = jnp.zeros(pivot.shape[1:], F32)
    gain = jnp.ones(pivot.shape[1:], F32)
    for z in range(chunks * per):
        c, s = cos_refs[z // per], sin_refs[z // per]
        q = z % per
        d, m = pivot[z], lower[z]
        re = d * (c[q, 0] + s[q, 1]) + m * re
        im = d * (c[q, 1] - s[q, 0]) + m * im
        gain = m * gain
        low[z, 0] = re
        low[z, 1] = im
    summary[0] = gain
    summary[1] = re
    summary[2] = im


def up_summary_kernel(levels, low, lower, upper, enter, summary):
    er, ei = enter[0, 0], enter[0, 1]
    re = im = jnp.zeros(lower.shape[1:], F32)
    gain = jnp.ones(lower.shape[1:], F32)
    carried = jnp.ones(lower.shape[1:], F32)
    for z in range(levels):
        carried = carried * lower[z]
        re = re + gain * (low[z, 0] + carried * er)
        im = im + gain * (low[z, 1] + carried * ei)
        gain = gain * upper[z]
    summary[0] = gain
    summary[1] = re
    summary[2] = im


def solve_kernel(levels, per, low, lower, upper, enter, above, *outs):
    er, ei = enter[0, 0], enter[0, 1]
    gains = []
    carried = jnp.ones(lower.shape[1:], F32)
    for z in range(levels):
        carried = carried * lower[z]
        gains.append(carried)
    re, im = above[0, 0], above[0, 1]
    for z in range(levels - 1, -1, -1):
        re = low[z, 0] + gains[z] * er + upper[z] * re
        im = low[z, 1] + gains[z] * ei + upper[z] * im
        outs[z // per][z % per, 0] = re
        outs[z // per][z % per, 1] = im


def entering(summary, reverse):
    count = lax.axis_size("gz")
    _, width, span = summary.shape
    parts = summary.reshape(3, count, width // count, span)
    got = lax.all_to_all(parts, "gz", split_axis=1, concat_axis=1, tiled=True)
    order = list(range(count))
    if reverse:
        order.reverse()
    states = [None] * count
    state = jnp.zeros((2, width // count, span), F32)
    for at in order:
        states[at] = state
        state = got[1:, at] + got[0, at][None] * state
    return lax.all_to_all(jnp.stack(states), "gz", split_axis=0, concat_axis=0, tiled=True)


def on_device(
    pressure_cotangent,
    velocity_cotangent,
    inverse_spacing,
    inverse_pivot,
    lower_factor,
    upper_factor,
):
    levels, rows, nx = pressure_cotangent.shape
    level_above = passed_along(velocity_cotangent[:1], "gz", -1)
    gy = lax.axis_size("gy")
    gz = lax.axis_size("gz")
    ny = rows * gy
    half = nx // gy
    per = 2 if levels % 2 == 0 else 1
    chunks = levels // per
    velocity = velocity_cotangent.astype(F32)
    shifted = jnp.concatenate([velocity[1:], level_above.astype(F32)], 0)
    source = pressure_cotangent.astype(F32) + inverse_spacing[:, None, None] * (shifted - velocity)

    table = lax.optimization_barrier(split_table(nx, half))
    cy, sy = lax.optimization_barrier(circle_table(ny))

    cos_parts, sin_parts = [], []
    for i in range(chunks):
        piece = source[i * per : (i + 1) * per]
        spec = jnp.einsum("zyn,nc->zyc", piece, table, precision=PREC)
        spec = jnp.transpose(spec.reshape(per, rows, gy, 2 * half), (2, 0, 1, 3))
        if i >= 2:
            spec, cos_parts[i - 2], sin_parts[i - 2] = lax.optimization_barrier(
                (spec, cos_parts[i - 2], sin_parts[i - 2])
            )
        got = lax.all_to_all(spec, "gy", split_axis=0, concat_axis=0, tiled=True)
        got = jnp.transpose(got, (1, 0, 2, 3)).reshape(per, ny, 2 * half)
        c = jnp.einsum("zyc,yk->zck", got, cy, precision=PREC)
        s = jnp.einsum("zyc,yk->zck", got, sy, precision=PREC)
        cos_parts.append(c.reshape(per, 2, half, ny))
        sin_parts.append(s.reshape(per, 2, half, ny))

    quarter = half // gz
    kb = min(16, quarter)
    in_quarter = quarter // kb
    grid = (half // kb,)
    chunk_spec = pl.BlockSpec((per, 2, kb, ny), lambda i: (0, 0, i, 0))
    factor_spec = pl.BlockSpec((levels, kb, ny), lambda i: (0, i, 0))
    low_spec = pl.BlockSpec((levels, 2, kb, ny), lambda i: (0, 0, i, 0))
    summary_spec = pl.BlockSpec((3, kb, ny), lambda i: (0, i, 0))
    state_spec = pl.BlockSpec((1, 2, kb, ny), lambda i: (i // in_quarter, 0, i % in_quarter, 0))
    summary_shape = jax.ShapeDtypeStruct((3, half, ny), F32)

    low, summary = pl.pallas_call(
        functools.partial(down_kernel, chunks, per),
        grid=grid,
        in_specs=[chunk_spec] * (2 * chunks) + [factor_spec] * 2,
        out_specs=[low_spec, summary_spec],
        out_shape=[jax.ShapeDtypeStruct((levels, 2, half, ny), F32), summary_shape],
    )(*cos_parts, *sin_parts, inverse_pivot, lower_factor)
    enter = entering(summary, False)
    summary = pl.pallas_call(
        functools.partial(up_summary_kernel, levels),
        grid=grid,
        in_specs=[low_spec, factor_spec, factor_spec, state_spec],
        out_specs=summary_spec,
        out_shape=summary_shape,
    )(low, lower_factor, upper_factor, enter)
    above = entering(summary, True)
    solved = pl.pallas_call(
        functools.partial(solve_kernel, levels, per),
        grid=grid,
        in_specs=[low_spec, factor_spec, factor_spec, state_spec, state_spec],
        out_specs=[chunk_spec] * chunks,
        out_shape=[jax.ShapeDtypeStruct((per, 2, half, ny), F32)] * chunks,
    )(low, lower_factor, upper_factor, enter, above)

    normalizer = 1.0 / (nx * ny)
    fields = []
    for i in range(chunks):
        flat = solved[i].reshape(per, 2 * half, ny)
        c = jnp.einsum("ky,zck->zyc", cy, flat, precision=PREC)
        s = jnp.einsum("ky,zck->zyc", sy, flat, precision=PREC)
        back = jnp.concatenate([c[..., :half] - s[..., half:], c[..., half:] + s[..., :half]], 2)
        back = jnp.transpose(back.reshape(per, gy, rows, 2 * half), (1, 0, 2, 3))
        if i >= 2:
            back, fields[i - 2] = lax.optimization_barrier((back, fields[i - 2]))
        got = lax.all_to_all(back, "gy", split_axis=0, concat_axis=0, tiled=True)
        got = jnp.transpose(got, (1, 2, 0, 3)).reshape(per, rows, 2 * nx)
        field = jnp.einsum("zyc,nc->zyn", got, table, precision=PREC) * normalizer
        fields.append(field.astype(jnp.bfloat16))
    return jnp.concatenate(fields, 0)


BF16 = jnp.bfloat16
MESH = pl.DeviceIdType.MESH
TINY = 1e-36
PEAK = 2.0**14
ROWS = 32
NT = (((1,), (1,)), ((), ()))
NN = (((1,), (0,)), ((), ()))


def split(x):
    high = x.astype(BF16)
    return high, (x - high.astype(F32)).astype(BF16)


def split_host(x):
    high = x.astype(np.float32).astype(ml_dtypes.bfloat16)
    low = (x - high.astype(np.float64)).astype(np.float32).astype(ml_dtypes.bfloat16)
    return high, low


def along_table(nx, gy):
    width = nx // gy
    chunk, g, j = np.meshgrid(np.arange(width // ROWS), np.arange(gy), np.arange(8), indexing="ij")
    parts = []
    for q in (0, 2, 1, 3):
        kx = g * width + ROWS * chunk + 4 * j + q
        turn = 2 * np.pi * ((kx[..., None] * np.arange(nx // 4)) % nx) / nx
        c, s = np.cos(turn), np.sin(turn)
        pair = np.stack([c, -s], 2)
        if q == 1:
            pair = np.concatenate([pair, np.stack([-s, -c], 2)], -1)
        if q == 3:
            pair = np.concatenate([pair, np.stack([s, c], 2)], -1)
        parts.append(pair.reshape(-1, pair.shape[-1]))
    return split_host(np.concatenate(parts, 1))


def across_table(ny):
    quarter = ny // 4
    lane = np.arange(quarter)
    block, inner = lane // 128, lane % 128
    tables = []
    for q in range(4):
        ky = 512 * block + 128 * (inner % 4) + 4 * (inner // 4) + q
        turn = 2 * np.pi * ((np.arange(quarter)[:, None] * ky) % ny) / ny
        c, s = np.cos(turn), np.sin(turn)
        tables.append(np.block([[c, -s], [s, c]]))
    return split_host(np.stack(tables))


def exchange_lanes(vs):
    lane = lax.broadcasted_iota(jnp.int32, vs[0].shape, 1)
    odd, upper = lane % 2 == 1, lane % 4 >= 2

    def turned(xs, sign):
        xs = [jnp.where(odd, xs[(d + sign) % 4], xs[d]) for d in range(4)]
        return [jnp.where(upper, xs[(d + 2) % 4], xs[d]) for d in range(4)]

    ds = turned([vs[-d % 4] for d in range(4)], -1)
    es = [ds[0]] + [
        jnp.take_along_axis(ds[d], lane // 4 * 4 + (lane + d) % 4, axis=1) for d in range(1, 4)
    ]
    return turned(es, -1)


def encode(v):
    v2 = v * v
    v4 = v2 * v2
    return (v4 * v4 * v).astype(BF16)


def decode(w, scale):
    w = w.astype(F32)
    size = jnp.maximum(jnp.abs(w), 2.0**-126)
    return w * jnp.exp2(jnp.log(size) * (-8.0 / (9.0 * math.log(2.0)))) * scale


def dot3(ah, al, bh, bl, dims):
    def one(a, b):
        return lax.dot_general(a, b, dims, preferred_element_type=F32)

    return one(ah, bh) + one(al, bh) + one(ah, bl)


def greet(devices):
    barrier = pltpu.get_barrier_semaphore()
    for device in devices:
        pl.semaphore_signal(barrier, inc=1, device_id=device, device_id_type=MESH)


def forward_kernel(
    n, levels, nx,
    p_hbm, v_hbm, spacing, th_hbm, tl_hbm, yh_hbm, yl_hbm, pivot_hbm, lower_hbm,
    low_hbm, top, gain,
    p_ref, v_all, th, tl, yh, yl, ah, al, stage, got, bh, bl, spec, pivot, lower,
    in_sem, edge_send, edge_recv, send_sem, recv_sem, own_sem, factor_sem, low_sem,
):
    me, z, zs = lax.axis_index("gy"), lax.axis_index("gz"), lax.axis_size("gz")
    rows = p_hbm.shape[1]
    x4 = nx // 4
    width = nx // n
    chunks = width // ROWS
    y4 = n * rows // 4
    pairs = levels // 2
    per = 2
    turns = chunks // per
    piece = 4 * per * ROWS
    half = width // 2

    inputs = [
        pltpu.make_async_copy(source, to, in_sem.at[i])
        for i, (source, to) in enumerate((
            (p_hbm, p_ref), (v_hbm, v_all.at[pl.ds(0, levels)]),
            (th_hbm, th), (tl_hbm, tl), (yh_hbm, yh), (yl_hbm, yl),
        ))
    ]
    for copy in inputs:
        copy.start()
    barrier = pltpu.get_barrier_semaphore()
    greet([{"gy": lax.rem(me + d, n)} for d in range(1, n)])

    @pl.when(z < zs - 1)
    def _():
        greet([{"gz": z + 1}])

    pl.semaphore_wait(barrier, n - 1 + jnp.minimum(z, 1))

    def edge():
        return pltpu.make_async_remote_copy(
            src_ref=v_hbm.at[pl.ds(0, 1)], dst_ref=v_all.at[pl.ds(levels, 1)],
            send_sem=edge_send, recv_sem=edge_recv, device_id={"gz": z - 1}, device_id_type=MESH,
        )

    @pl.when(z > 0)
    def _():
        edge().start()

    @pl.when(z == zs - 1)
    def _():
        v_all[levels] = jnp.zeros((rows, nx), BF16)

    top[...] = jnp.zeros_like(top)
    gain[...] = jnp.ones_like(gain)

    def factors(lp):
        return [
            pltpu.make_async_copy(
                hbm.at[pl.ds(2 * lp, 2), :, pl.ds(128 * k, 128)], ref.at[k], factor_sem.at[i, k]
            )
            for i, (hbm, ref) in enumerate(((pivot_hbm, pivot), (lower_hbm, lower)))
            for k in range(y4 // 32)
        ]

    for copy in factors(0):
        copy.start()
    for copy in inputs[:2]:
        copy.wait()

    def own(lp):
        return pltpu.make_async_copy(stage.at[lax.rem(lp, 2), me], got.at[lp, me], own_sem.at[lp])

    def transfer(lp, i, d, source, first):
        peer = lax.rem(me + d, n)
        r = pl.ds(0, 16 + piece) if first else pl.ds(pl.multiple_of(16 + i * piece, 16), piece)
        return pltpu.make_async_remote_copy(
            src_ref=stage.at[lax.rem(lp, 2), peer, r, :], dst_ref=got.at[lp, source, r, :],
            send_sem=send_sem.at[lp, i, d], recv_sem=recv_sem.at[lp, i, source],
            device_id={"gy": peer}, device_id_type=MESH,
        )

    def send(lp, i, d, first):
        return transfer(lp, i, d, me, first)

    def arrival(lp, i, d, first):
        return transfer(lp, i, d, lax.rem(me + d, n), first)

    def sent(lp):
        for d in range(1, n):
            for i in range(turns):
                send(lp, i, d, i == 0).wait_send()

    def low_copy(lp):
        return pltpu.make_async_copy(spec, low_hbm.at[lp], low_sem)

    def spectra(lp):
        @pl.when(lp >= 2)
        def _():
            sent(lp - 2)

        @pl.when((lp == pairs - 1) & (z < zs - 1))
        def _():
            edge().wait_recv()

        tile = 16
        peak = jnp.zeros((8, 128), F32)
        for lev in range(2):
            at = 2 * lp + lev
            factor = spacing[at]

            def source(i, peak, lev=lev, at=at, factor=factor):
                r = pl.ds(pl.multiple_of(i * tile, tile), tile)
                q = [pl.ds(k * x4, x4) for k in range(4)]
                xs = [
                    p_ref[at, r, s].astype(F32)
                    + factor * (v_all[at + 1, r, s].astype(F32) - v_all[at, r, s].astype(F32))
                    for s in q
                ]
                size = functools.reduce(jnp.maximum, [jnp.abs(x) for x in xs])
                e, o = xs[0] + xs[2], xs[1] + xs[3]
                to = pl.ds(pl.multiple_of(lev * rows + i * tile, tile), tile)
                for s, a in zip(q, (e + o, e - o, xs[0] - xs[2], xs[1] - xs[3])):
                    ah[to, s], al[to, s] = split(a)
                for k in range(x4 // 128):
                    part = size[:, k * 128 : (k + 1) * 128]
                    peak = jnp.maximum(peak, jnp.maximum(part[:8], part[8:]))
                return peak

            peak = lax.fori_loop(0, rows // tile, source, peak)
        peak = jnp.maximum(jnp.max(peak), TINY)
        held = jnp.full((16, 128), peak, F32).astype(BF16)
        shrink = PEAK / (nx * held.astype(F32)[:1, :1])
        slot = lax.rem(lp, 2)
        for g in range(n):
            stage[slot, g, pl.ds(0, 16), :] = held

        tall = per * 16 * n

        @pl.when(lp == 0)
        def _():
            for copy in inputs[2:4]:
                copy.wait()

        def transform(i, _):
            m = pl.ds(pl.multiple_of(i * tall, tall), tall)
            outs, at = [None] * 4, 0
            for q in (0, 2, 1, 3):
                wide = x4 if q % 2 == 0 else 2 * x4
                start = (0, 2 * x4, x4, 2 * x4)[q]
                t, a = pl.ds(at, wide), pl.ds(start, wide)
                outs[q] = dot3(th[m, t], tl[m, t], ah[:, a], al[:, a], NT) * shrink
                at += wide
            for k in range(per):
                for g in range(n):
                    for c in range(2):
                        s = (k * n + g) * 16 + c * 8
                        block = encode(jnp.concatenate([o[s : s + 8] for o in outs], 0))
                        for lev in range(2):
                            r = 16 + i * piece + ((lev * 2 + c) * per + k) * ROWS
                            stage[slot, g, pl.ds(pl.multiple_of(r, 16), ROWS), :] = block[
                                :, lev * rows : (lev + 1) * rows
                            ]

            @pl.when(i == 0)
            def _():
                for d in range(1, n):
                    send(lp, 0, d, True).start()

            @pl.when(i > 0)
            def _():
                for d in range(1, n):
                    send(lp, i, d, False).start()

            return 0

        lax.fori_loop(0, turns, transform, 0)
        own(lp).start()

    def substitute(lp):
        own(lp).wait()
        for d in range(1, n):
            arrival(lp, 0, d, True).wait_recv()

        @pl.when(lp == 0)
        def _():
            for copy in inputs[4:]:
                copy.wait()

        @pl.when(lp > 0)
        def _():
            low_copy(lp - 1).wait()

        for copy in factors(lp):
            copy.wait()
        scales = [got[lp, s, pl.ds(0, 16), :].astype(F32)[:1, :] * (nx / PEAK) for s in range(n)]

        def one_half(h, _):
            for k in range(turns // 2):
                for d in range(1, n):
                    if k == 0:
                        @pl.when(h > 0)
                        def _(d=d):
                            arrival(lp, turns // 2, d, False).wait_recv()
                    else:
                        arrival(lp, h * (turns // 2) + k, d, False).wait_recv()
            substitute_half(lp, h, scales)
            return 0

        lax.fori_loop(0, 2, one_half, 0)
        low_copy(lp).start()

        @pl.when(lp < pairs - 1)
        def _():
            for copy in factors(lp + 1):
                copy.start()

    def substitute_half(lp, h, scales):
        tile = 16
        quads = n // 4

        def unpack(i, _):
            row = h * half + i * tile
            turn, inner = row // (per * ROWS), lax.rem(row, per * ROWS)
            for lev in range(2):
                for o in range(quads):
                    xs = []
                    for c in range(2):
                        r = 16 + turn * piece + (lev * 2 + c) * per * ROWS + inner
                        r = pl.ds(pl.multiple_of(r, tile), tile)
                        xs.append([decode(got[lp, k * quads + o, r, :], scales[k * quads + o]) for k in range(4)])
                    (r0, r1, r2, r3), (i0, i1, i2, i3) = xs
                    er, fr, ei, fi = r0 + r2, r0 - r2, i0 + i2, i0 - i2
                    gr, hr, gi, hi = r1 + r3, r1 - r3, i1 + i3, i1 - i3
                    real = (er + gr, fr + hi, er - gr, fr - hi)
                    imag = (ei + gi, fi - hr, ei - gi, fi + hr)
                    to = pl.ds(pl.multiple_of(lev * half + i * tile, tile), tile)
                    for q in range(4):
                        for c, x in enumerate((real[q], imag[q])):
                            s = pl.ds(c * y4 + o * 128, 128)
                            bh[q, to, s], bl[q, to, s] = split(x)
            return 0

        lax.fori_loop(0, half // tile, unpack, 0)
        tall = min(width, 256)

        def transform(i, _):
            r = pl.ds(pl.multiple_of(i * tall, tall), tall)
            ro = pl.ds(pl.multiple_of(h * width + i * tall, tall), tall)
            for k in range(2 * y4 // 256):
                w = pl.ds(k * 256, 256)
                parts = [dot3(bh[q, r, :], bl[q, r, :], yh[q, :, w], yl[q, :, w], NN) for q in range(4)]
                for j in range(2):
                    for t, x in enumerate(exchange_lanes([x[:, j * 128 : (j + 1) * 128] for x in parts])):
                        spec[t, ro, pl.ds(k * 256 + j * 128, 128)] = x
            return 0

        lax.fori_loop(0, width // tall, transform, 0)

        def solve(inner, _):
            i = h * (chunks // 2) + inner
            r = pl.ds(pl.multiple_of(i * ROWS, ROWS), ROWS)
            strided = [pl.ds(i * ROWS + q, 8, stride=4) for q in range(4)]
            for b in range(y4 // 128):
                for t in range(4):
                    s = pl.ds(512 * b + 128 * t, 128)
                    lanes = [pl.ds(c * y4 + b * 128, 128) for c in range(2)]
                    rl = [
                        pl.ds(pl.multiple_of(h * width + lev * half + inner * ROWS, ROWS), ROWS)
                        for lev in range(2)
                    ]
                    ms, ds = [
                        [jnp.concatenate([f[4 * b + t, lev, x, :] for x in strided], 0) for lev in range(2)]
                        for f in (lower, pivot)
                    ]
                    xs = [[spec[t, rl[lev], lanes[c]] for c in range(2)] for lev in range(2)]
                    held, run = [top[c, r, s] for c in range(2)], gain[r, s]
                    first = [ds[0] * xs[0][c] + ms[0] * held[c] for c in range(2)]
                    second = [ds[1] * xs[1][c] + ms[1] * first[c] for c in range(2)]
                    gain[r, s] = run * ms[0] * ms[1]
                    for c in range(2):
                        spec[t, rl[0], lanes[c]] = first[c]
                        spec[t, rl[1], lanes[c]] = second[c]
                        top[c, r, s] = second[c]
            return 0

        lax.fori_loop(0, chunks // 2, solve, 0)

    def step(t, _):
        @pl.when(t < pairs)
        def _():
            spectra(t)

        @pl.when(t >= 1)
        def _():
            substitute(t - 1)

        return 0

    lax.fori_loop(0, pairs + 1, step, 0)
    low_copy(pairs - 1).wait()
    for lp in range(max(pairs - 2, 0), pairs):
        sent(lp)

    @pl.when(z > 0)
    def _():
        edge().wait_send()


def backward_kernel(
    n, levels, nx,
    low_hbm, top_hbm, gain_hbm, lower_hbm, upper_hbm, th_hbm, tl_hbm, yh_hbm, yl_hbm,
    out_hbm,
    th, tl, yh, yl, low, lower, upper, top, gain, enter, above, d_send, u_send, sh, sl, yo, stage, got, xh, xl, acc, out,
    in_sem, low_sem, load_sem, sum_sem, ds_sem, dr_sem, us_sem, ur_sem, send_sem, recv_sem, own_sem, out_sem,
):
    me, z, zs = lax.axis_index("gy"), lax.axis_index("gz"), lax.axis_size("gz")
    width = nx // n
    chunks = width // ROWS
    rows = out_hbm.shape[1]
    ny = n * rows
    y4, x4 = ny // 4, nx // 4
    body = levels * 2 * ROWS
    per = 2 if chunks % 2 == 0 else 1

    inputs = [
        pltpu.make_async_copy(source, to, in_sem.at[i])
        for i, (source, to) in enumerate(((yh_hbm, yh), (yl_hbm, yl), (th_hbm, th), (tl_hbm, tl)))
    ]

    def loads(c):
        slot = lax.rem(c, 2)
        r = pl.ds(pl.multiple_of(c * ROWS, ROWS), ROWS)
        rh = pl.ds(pl.multiple_of(lax.rem(c, chunks // 2) * ROWS, ROWS), ROWS)
        return [
            pltpu.make_async_copy(
                low_hbm.at[:, :, c // (chunks // 2), :, rh, :], low.at[slot], low_sem.at[slot]
            ),
        ] + [
            pltpu.make_async_copy(hbm.at[:, r, pl.ds(128 * k, 128)], ref.at[slot, k], load_sem.at[slot, i, k])
            for i, (hbm, ref) in enumerate(((lower_hbm, lower), (upper_hbm, upper)))
            for k in range(ny // 128)
        ]

    def sums(c):
        slot = lax.rem(c, 2)
        r = pl.ds(pl.multiple_of(c * ROWS, ROWS), ROWS)
        return [
            pltpu.make_async_copy(top_hbm.at[:, r, :], top.at[slot], sum_sem.at[slot, 0]),
            pltpu.make_async_copy(gain_hbm.at[r, :], gain.at[slot], sum_sem.at[slot, 1]),
        ]

    for copy in sums(0) + loads(0) + inputs:
        copy.start()
    barrier = pltpu.get_barrier_semaphore()
    greet([{"gy": lax.rem(me + d, n)} for d in range(1, n)])

    @pl.when(z < zs - 1)
    def _():
        greet([{"gz": z + 1}])

    @pl.when(z > 0)
    def _():
        greet([{"gz": z - 1}])

    pl.semaphore_wait(barrier, n - 1 + jnp.minimum(z, 1) + jnp.minimum(zs - 1 - z, 1))

    @pl.when(z == 0)
    def _():
        enter[...] = jnp.zeros_like(enter)

    @pl.when(z == zs - 1)
    def _():
        above[...] = jnp.zeros_like(above)

    def state_rows(q):
        return pl.ds(pl.multiple_of(q * 8, 8), 8)

    def pass_down(c, q):
        return pltpu.make_async_remote_copy(
            src_ref=d_send.at[lax.rem(c, 2), :, state_rows(q), :], dst_ref=enter.at[c, :, state_rows(q), :],
            send_sem=ds_sem.at[c, q], recv_sem=dr_sem.at[c, q],
            device_id={"gz": z + 1}, device_id_type=MESH,
        )

    def pass_up(c, q):
        return pltpu.make_async_remote_copy(
            src_ref=u_send.at[lax.rem(c, 2), :, state_rows(q), :], dst_ref=above.at[c, :, state_rows(q), :],
            send_sem=us_sem.at[c, q], recv_sem=ur_sem.at[c, q],
            device_id={"gz": z - 1}, device_id_type=MESH,
        )

    def own(c):
        return pltpu.make_async_copy(stage.at[lax.rem(c, 2), me], got.at[c, me], own_sem.at[c])

    def send(c, d):
        peer = lax.rem(me + d, n)
        return pltpu.make_async_remote_copy(
            src_ref=stage.at[lax.rem(c, 2), peer], dst_ref=got.at[c, me],
            send_sem=send_sem.at[c, d], recv_sem=recv_sem.at[c, me],
            device_id={"gy": peer}, device_id_type=MESH,
        )

    def arrival(c, d):
        peer = lax.rem(me + d, n)
        return pltpu.make_async_remote_copy(
            src_ref=stage.at[lax.rem(c, 2), peer], dst_ref=got.at[c, peer],
            send_sem=send_sem.at[c, d], recv_sem=recv_sem.at[c, peer],
            device_id={"gy": peer}, device_id_type=MESH,
        )

    def relay(c):
        for copy in sums(c):
            copy.wait()

        @pl.when(c + 1 < chunks)
        def _():
            for copy in sums(c + 1):
                copy.start()

        slot = lax.rem(c, 2)

        @pl.when((z < zs - 1) & (c >= 2))
        def _():
            for q in range(4):
                pass_down(c - 2, q).wait_send()

        def carry(q, _):
            r = state_rows(q)

            @pl.when(z > 0)
            def _():
                pass_down(c, q).wait_recv()

            @pl.when(z < zs - 1)
            def _():
                new = [top[slot, k, r, :] + gain[slot, r, :] * enter[c, k, r, :] for k in range(2)]
                for k in range(2):
                    d_send[slot, k, r, :] = new[k]
                pass_down(c, q).start()

            return 0

        lax.fori_loop(0, 4, carry, 0)

    def solve(c):
        slot = lax.rem(c, 2)
        for copy in loads(c):
            copy.wait()

        @pl.when(c + 1 < chunks)
        def _():
            for copy in loads(c + 1):
                copy.start()

        @pl.when((z > 0) & (c >= 2))
        def _():
            for q in range(4):
                pass_up(c - 2, q).wait_send()

        def sweep(q, _):
            strided = pl.ds(q, 8, stride=4)
            r = state_rows(q)

            @pl.when(z < zs - 1)
            def _():
                pass_up(c, q).wait_recv()

            for b in range(y4 // 128):
                natural = [pl.ds(512 * b + 128 * t, 128) for t in range(4)]
                gains = [[] for _ in range(4)]
                for t in range(4):
                    for lev in range(levels):
                        m = lower[slot, 4 * b + t, lev, strided, :]
                        gains[t].append(m if lev == 0 else gains[t][-1] * m)
                state = [[above[c, k, r, s] for s in natural] for k in range(2)]
                entry = [[enter[c, k, r, s] for s in natural] for k in range(2)]
                for lev in range(levels - 1, -1, -1):
                    ups = [upper[slot, 4 * b + t, lev, strided, :] for t in range(4)]
                    for k in range(2):
                        lanes = pl.ds(k * y4 + b * 128, 128)
                        state[k] = [
                            low[slot, lev // 2, t, lev % 2, r, lanes] + gains[t][lev] * entry[k][t] + ups[t] * state[k][t]
                            for t in range(4)
                        ]
                        to = pl.ds(pl.multiple_of(lev * ROWS + q * 8, 8), 8)
                        for t in range(4):
                            yo[t, to, lanes] = state[k][t]
                for k in range(2):
                    for t in range(4):
                        u_send[slot, k, r, natural[t]] = state[k][t]

            @pl.when(z > 0)
            def _():
                pass_up(c, q).start()

            return 0

        lax.fori_loop(0, 4, sweep, 0)

        @pl.when(c == 0)
        def _():
            acc[...] = jnp.zeros_like(acc)
            for copy in inputs:
                copy.wait()

        @pl.when(c >= 2)
        def _():
            own(c - 2).wait()
            for d in range(1, n):
                send(c - 2, d).wait_send()

        count = levels * ROWS

        def halve(i, _):
            r = pl.ds(pl.multiple_of(i * ROWS, ROWS), ROWS)
            for k in range(2 * y4 // 128):
                s = pl.ds(k * 128, 128)
                for q, x in enumerate(exchange_lanes([yo[t, r, s] for t in range(4)])):
                    sh[q, r, s], sl[q, r, s] = split(x)
            return 0

        lax.fori_loop(0, levels, halve, 0)

        def transform(q, _):
            yo[q] = dot3(sh[q], sl[q], yh[q], yl[q], NT)
            return 0

        lax.fori_loop(0, 4, transform, 0)

        def combine(i, peak):
            r = pl.ds(pl.multiple_of(i * 8, 8), 8)
            for h in range(y4 // 128):
                rs = pl.ds(h * 128, 128)
                cs = pl.ds(y4 + h * 128, 128)
                r0, r1, r2, r3 = [yo[q, r, rs] for q in range(4)]
                i0, i1, i2, i3 = [yo[q, r, cs] for q in range(4)]
                er, fr, ei, fi = r0 + r2, r0 - r2, i0 + i2, i0 - i2
                gr, hr, gi, hi = r1 + r3, r1 - r3, i1 + i3, i1 - i3
                real = (er + gr, fr - hi, er - gr, fr + hi)
                imag = (ei + gi, fi + hr, ei - gi, fi - hr)
                for q in range(4):
                    yo[q, r, rs] = real[q]
                    yo[q, r, cs] = imag[q]
                    peak = jnp.maximum(peak, jnp.maximum(jnp.abs(real[q]), jnp.abs(imag[q])))
            return peak

        peak = lax.fori_loop(0, count // 8, combine, jnp.zeros((8, 128), F32))
        held = jnp.full((16, 128), jnp.maximum(jnp.max(peak), TINY), F32).astype(BF16)
        shrink = PEAK / held.astype(F32)[:1, :1]
        quads = n // 4
        for g in range(n):
            stage[slot, g, pl.ds(body, 16), :] = held

        def pack(lev, _):
            r = pl.ds(pl.multiple_of(lev * ROWS, ROWS), ROWS)
            for g in range(n):
                for k in range(2):
                    x = yo[g // quads, r, pl.ds(k * y4 + (g % quads) * 128, 128)]
                    to = pl.ds(pl.multiple_of((lev * 2 + k) * ROWS, ROWS), ROWS)
                    stage[slot, g, to, :] = encode(x * shrink)
            return 0

        lax.fori_loop(0, levels, pack, 0)
        own(c).start()
        for d in range(1, n):
            send(c, d).start()

    def gather(pair):
        for k in range(per):
            c = pair * per + k

            for d in range(1, n):
                arrival(c, d).wait_recv()

        scales = [
            [got[pair * per + k, s, pl.ds(body, 16), :].astype(F32)[:1, :] * (1.0 / (PEAK * nx * ny)) for s in range(n)]
            for k in range(per)
        ]
        deep = per * 16 * n

        def two_levels(lp, _):
            for lev in range(2):
                for k in range(per):
                    parts = []
                    for s in range(n):
                        for j in range(2):
                            r = ((lp * 2 + lev) * 2 + j) * ROWS
                            r = pl.ds(pl.multiple_of(r, ROWS), ROWS)
                            parts.append(decode(got[pair * per + k, s, r, :], scales[k][s]))
                    for q in range(4):
                        block = jnp.concatenate([x[q * 8 : q * 8 + 8] for x in parts], 0)
                        high, low_part = split(block.T)
                        lanes = pl.ds(k * 16 * n, 16 * n)
                        xh[q, pl.ds(lev * rows, rows), lanes] = high
                        xl[q, pl.ds(lev * rows, rows), lanes] = low_part
            m = pl.ds(pl.multiple_of(pair * deep, deep), deep)
            to = pl.ds(pl.multiple_of(lp * 2 * rows, 2 * rows), 2 * rows)

            def part(q, start, wide):
                t = pl.ds(start, wide)
                return dot3(xh[q], xl[q], th[m, t], tl[m, t], NN)

            acc[to, pl.ds(0, x4)] += part(0, 0, x4)
            acc[to, pl.ds(x4, x4)] += part(2, x4, x4)
            acc[to, pl.ds(2 * x4, 2 * x4)] += part(1, 2 * x4, 2 * x4) + part(3, 4 * x4, 2 * x4)
            return 0

        lax.fori_loop(0, levels // 2, two_levels, 0)

    lag = 2 * (zs - 1)
    halves = chunks // per

    def step(t, _):
        down = t - z

        @pl.when((down >= 0) & (down < chunks))
        def _():
            relay(down)

        c = t - lag + z

        @pl.when((c >= 0) & (c < chunks))
        def _():
            solve(c)

        @pl.when((c >= 2 * per - 1) & (c < chunks) & (lax.rem(c + 1 + 2 * per, per) == 0))
        def _():
            gather((c + 1) // per - 2)

        return 0

    last = chunks - 1
    lax.fori_loop(0, chunks + lag, step, 0)
    for c in range(max(chunks - 2, 0), chunks):
        own(c).wait()
        for d in range(1, n):
            send(c, d).wait_send()

        @pl.when(z < zs - 1)
        def _():
            for q in range(4):
                pass_down(c, q).wait_send()

        @pl.when(z > 0)
        def _():
            for q in range(4):
                pass_up(c, q).wait_send()

    gather(halves - 1)

    def finish(i, _):
        lev = i
        r = pl.ds(pl.multiple_of(lev * rows, rows), rows)
        slot = lax.rem(lev, 2)

        @pl.when(lev >= 2)
        def _():
            pltpu.make_async_copy(out.at[slot], out_hbm.at[lev], out_sem.at[slot]).wait()

        def emit(k, _):
            r = pl.ds(pl.multiple_of(lev * rows + k * 16, 16), 16)
            ro = pl.ds(pl.multiple_of(k * 16, 16), 16)
            a0, a2, u, w = [acc[r, pl.ds(s * x4, x4)] for s in range(4)]
            e, o = a0 + a2, a0 - a2
            for s, x in enumerate((e + u, o + w, e - u, o - w)):
                out[slot, ro, pl.ds(s * x4, x4)] = x.astype(BF16)
            return 0

        lax.fori_loop(0, rows // 16, emit, 0)
        pltpu.make_async_copy(out.at[slot], out_hbm.at[lev], out_sem.at[slot]).start()
        return 0

    lax.fori_loop(0, levels, finish, 0)
    for lev in range(levels - min(2, levels), levels):
        pltpu.make_async_copy(out.at[lev % 2], out_hbm.at[lev], out_sem.at[lev % 2]).wait()


def fast_device(p, v, inverse_spacing, inverse_pivot, lower_factor, upper_factor):
    levels, rows, nx = p.shape
    n = lax.axis_size("gy")
    width, ny = nx // n, n * rows
    y4 = ny // 4
    pairs, chunks = levels // 2, nx // n // ROWS
    th, tl = [jnp.asarray(t) for t in along_table(nx, n)]
    yh, yl = [jnp.asarray(t) for t in across_table(ny)]
    anyspace = pl.BlockSpec(memory_space=pl.ANY)
    vmem = pl.BlockSpec(memory_space=pltpu.VMEM)
    dma = pltpu.SemaphoreType.DMA
    message = 4 * width + 16
    tables = [pltpu.VMEM(t.shape, BF16) for t in (th, tl, yh, yl)]
    low, top, gain = pl.pallas_call(
        functools.partial(forward_kernel, n, levels, nx),
        out_shape=[
            jax.ShapeDtypeStruct((pairs, 4, 2 * width, 2 * y4), F32),
            jax.ShapeDtypeStruct((2, width, ny), F32),
            jax.ShapeDtypeStruct((width, ny), F32),
        ],
        in_specs=[anyspace] * 2 + [pl.BlockSpec(memory_space=pltpu.SMEM)] + [anyspace] * 6,
        out_specs=[anyspace, vmem, vmem],
        scratch_shapes=[
            pltpu.VMEM((levels, rows, nx), BF16),
            pltpu.VMEM((levels + 1, rows, nx), BF16),
            *tables,
            pltpu.VMEM((2 * rows, nx), BF16),
            pltpu.VMEM((2 * rows, nx), BF16),
            pltpu.VMEM((2, n, message, 128), BF16),
            pltpu.VMEM((pairs, n, message, 128), BF16),
            pltpu.VMEM((4, 2 * width, 2 * y4), BF16),
            pltpu.VMEM((4, 2 * width, 2 * y4), BF16),
            pltpu.VMEM((4, 2 * width, 2 * y4), F32),
            pltpu.VMEM((ny // 128, 2, width, 128), F32),
            pltpu.VMEM((ny // 128, 2, width, 128), F32),
            dma((6,)), dma, dma,
            dma((pairs, chunks // 2, n)), dma((pairs, chunks // 2, n)), dma((pairs,)), dma((2, ny // 128)), dma,
        ],
        compiler_params=pltpu.CompilerParams(
            collective_id=0, has_side_effects=True, vmem_limit_bytes=62 * 2**20
        ),
        name="forward",
    )(p, v, inverse_spacing, th, tl, yh, yl, inverse_pivot, lower_factor)

    low = low.reshape(pairs, 4, 2, 2, width // 2, 2 * y4)
    message = levels * 2 * ROWS + 16
    per = 2 if chunks % 2 == 0 else 1
    count = levels * ROWS
    return pl.pallas_call(
        functools.partial(backward_kernel, n, levels, nx),
        out_shape=jax.ShapeDtypeStruct((levels, rows, nx), BF16),
        in_specs=[anyspace] * 9,
        out_specs=anyspace,
        scratch_shapes=[
            *tables,
            pltpu.VMEM((2, pairs, 4, 2, ROWS, 2 * y4), F32),
            pltpu.VMEM((2, ny // 128, levels, ROWS, 128), F32),
            pltpu.VMEM((2, ny // 128, levels, ROWS, 128), F32),
            pltpu.VMEM((2, 2, ROWS, ny), F32),
            pltpu.VMEM((2, ROWS, ny), F32),
            pltpu.VMEM((chunks, 2, ROWS, ny), F32),
            pltpu.VMEM((chunks, 2, ROWS, ny), F32),
            pltpu.VMEM((2, 2, ROWS, ny), F32),
            pltpu.VMEM((2, 2, ROWS, ny), F32),
            pltpu.VMEM((4, count, 2 * y4), BF16),
            pltpu.VMEM((4, count, 2 * y4), BF16),
            pltpu.VMEM((4, count, 2 * y4), F32),
            pltpu.VMEM((2, n, message, 128), BF16),
            pltpu.VMEM((chunks, n, message, 128), BF16),
            pltpu.VMEM((4, 2 * rows, per * 16 * n), BF16),
            pltpu.VMEM((4, 2 * rows, per * 16 * n), BF16),
            pltpu.VMEM((levels * rows, nx), F32),
            pltpu.VMEM((2, rows, nx), BF16),
            dma((4,)), dma((2,)), dma((2, 2, ny // 128)), dma((2, 2)),
            dma((chunks, 4)), dma((chunks, 4)), dma((chunks, 4)), dma((chunks, 4)),
            dma((chunks, n)), dma((chunks, n)), dma((chunks,)), dma((2,)),
        ],
        compiler_params=pltpu.CompilerParams(
            collective_id=1, has_side_effects=True, vmem_limit_bytes=62 * 2**20
        ),
        name="backward",
    )(low, top, gain, lower_factor, upper_factor, th, tl, yh, yl)


def solution(mesh):
    spec = P("gz", "gy", None)

    def program(*arrays):
        levels, ny, nx = arrays[0].shape
        gy, gz = mesh.shape["gy"], mesh.shape["gz"]
        fast = ny // gy == 128 and gy % 4 == 0 and levels // gz % 2 == 0 and nx // gy % (4 * ROWS) == 0
        return jax.shard_map(
            fast_device if fast else on_device,
            mesh=mesh,
            in_specs=(spec, spec, P("gz"), spec, spec, spec),
            out_specs=spec,
            check_vma=False,
        )(*arrays)

    return program
```

```python
import functools
import math

import jax
import jax.numpy as jnp
import ml_dtypes
import numpy as np
from jax import lax
from jax.experimental import pallas as pl
from jax.experimental.pallas import tpu as pltpu
from jax.sharding import PartitionSpec as P

PREC = lax.Precision.HIGH
F32 = jnp.float32


def passed_along(x, axis, by):
    size = lax.axis_size(axis)
    pairs = [(i, i + by) for i in range(size) if 0 <= i + by < size]
    return lax.ppermute(x, axis, pairs)


def unit_circle(phase, count):
    angle = (phase % count).astype(F32) * (2.0 * math.pi / count)
    return jnp.cos(angle), jnp.sin(angle)


def circle_table(count):
    low = 32
    high = count // low
    k = jnp.arange(count, dtype=jnp.int32)[None, :]
    ch, sh = unit_circle(jnp.arange(high, dtype=jnp.int32)[:, None] * low * k, count)
    cl, sl = unit_circle(jnp.arange(low, dtype=jnp.int32)[:, None] * k, count)
    ch, sh, cl, sl = lax.optimization_barrier((ch, sh, cl, sl))
    ch, sh, cl, sl = ch[:, None], sh[:, None], cl[None], sl[None]
    cosine = (ch * cl - sh * sl).reshape(count, count)
    sine = (sh * cl + ch * sl).reshape(count, count)
    return cosine, sine


def split_table(count, half):
    low = 32
    column = jnp.arange(2 * count, dtype=jnp.int32)[None, :]
    k = column // (2 * half) * half + column % half
    quarter = jnp.where(column % (2 * half) < half, 0, count // 4)
    ch, sh = unit_circle(jnp.arange(count // low, dtype=jnp.int32)[:, None] * low * k, count)
    cl, sl = unit_circle(jnp.arange(low, dtype=jnp.int32)[:, None] * k + quarter, count)
    ch, sh, cl, sl = lax.optimization_barrier((ch, sh, cl, sl))
    return (ch[:, None] * cl[None] - sh[:, None] * sl[None]).reshape(count, 2 * count)


def down_kernel(chunks, per, *refs):
    cos_refs, sin_refs = refs[:chunks], refs[chunks : 2 * chunks]
    pivot, lower, low, summary = refs[2 * chunks :]
    re = im = jnp.zeros(pivot.shape[1:], F32)
    gain = jnp.ones(pivot.shape[1:], F32)
    for z in range(chunks * per):
        c, s = cos_refs[z // per], sin_refs[z // per]
        q = z % per
        d, m = pivot[z], lower[z]
        re = d * (c[q, 0] + s[q, 1]) + m * re
        im = d * (c[q, 1] - s[q, 0]) + m * im
        gain = m * gain
        low[z, 0] = re
        low[z, 1] = im
    summary[0] = gain
    summary[1] = re
    summary[2] = im


def up_summary_kernel(levels, low, lower, upper, enter, summary):
    er, ei = enter[0, 0], enter[0, 1]
    re = im = jnp.zeros(lower.shape[1:], F32)
    gain = jnp.ones(lower.shape[1:], F32)
    carried = jnp.ones(lower.shape[1:], F32)
    for z in range(levels):
        carried = carried * lower[z]
        re = re + gain * (low[z, 0] + carried * er)
        im = im + gain * (low[z, 1] + carried * ei)
        gain = gain * upper[z]
    summary[0] = gain
    summary[1] = re
    summary[2] = im


def solve_kernel(levels, per, low, lower, upper, enter, above, *outs):
    er, ei = enter[0, 0], enter[0, 1]
    gains = []
    carried = jnp.ones(lower.shape[1:], F32)
    for z in range(levels):
        carried = carried * lower[z]
        gains.append(carried)
    re, im = above[0, 0], above[0, 1]
    for z in range(levels - 1, -1, -1):
        re = low[z, 0] + gains[z] * er + upper[z] * re
        im = low[z, 1] + gains[z] * ei + upper[z] * im
        outs[z // per][z % per, 0] = re
        outs[z // per][z % per, 1] = im


def entering(summary, reverse):
    count = lax.axis_size("gz")
    _, width, span = summary.shape
    parts = summary.reshape(3, count, width // count, span)
    got = lax.all_to_all(parts, "gz", split_axis=1, concat_axis=1, tiled=True)
    order = list(range(count))
    if reverse:
        order.reverse()
    states = [None] * count
    state = jnp.zeros((2, width // count, span), F32)
    for at in order:
        states[at] = state
        state = got[1:, at] + got[0, at][None] * state
    return lax.all_to_all(jnp.stack(states), "gz", split_axis=0, concat_axis=0, tiled=True)


def on_device(
    pressure_cotangent,
    velocity_cotangent,
    inverse_spacing,
    inverse_pivot,
    lower_factor,
    upper_factor,
):
    levels, rows, nx = pressure_cotangent.shape
    level_above = passed_along(velocity_cotangent[:1], "gz", -1)
    gy = lax.axis_size("gy")
    gz = lax.axis_size("gz")
    ny = rows * gy
    half = nx // gy
    per = 2 if levels % 2 == 0 else 1
    chunks = levels // per
    velocity = velocity_cotangent.astype(F32)
    shifted = jnp.concatenate([velocity[1:], level_above.astype(F32)], 0)
    source = pressure_cotangent.astype(F32) + inverse_spacing[:, None, None] * (shifted - velocity)

    table = lax.optimization_barrier(split_table(nx, half))
    cy, sy = lax.optimization_barrier(circle_table(ny))

    cos_parts, sin_parts = [], []
    for i in range(chunks):
        piece = source[i * per : (i + 1) * per]
        spec = jnp.einsum("zyn,nc->zyc", piece, table, precision=PREC)
        spec = jnp.transpose(spec.reshape(per, rows, gy, 2 * half), (2, 0, 1, 3))
        if i >= 2:
            spec, cos_parts[i - 2], sin_parts[i - 2] = lax.optimization_barrier(
                (spec, cos_parts[i - 2], sin_parts[i - 2])
            )
        got = lax.all_to_all(spec, "gy", split_axis=0, concat_axis=0, tiled=True)
        got = jnp.transpose(got, (1, 0, 2, 3)).reshape(per, ny, 2 * half)
        c = jnp.einsum("zyc,yk->zck", got, cy, precision=PREC)
        s = jnp.einsum("zyc,yk->zck", got, sy, precision=PREC)
        cos_parts.append(c.reshape(per, 2, half, ny))
        sin_parts.append(s.reshape(per, 2, half, ny))

    quarter = half // gz
    kb = min(16, quarter)
    in_quarter = quarter // kb
    grid = (half // kb,)
    chunk_spec = pl.BlockSpec((per, 2, kb, ny), lambda i: (0, 0, i, 0))
    factor_spec = pl.BlockSpec((levels, kb, ny), lambda i: (0, i, 0))
    low_spec = pl.BlockSpec((levels, 2, kb, ny), lambda i: (0, 0, i, 0))
    summary_spec = pl.BlockSpec((3, kb, ny), lambda i: (0, i, 0))
    state_spec = pl.BlockSpec((1, 2, kb, ny), lambda i: (i // in_quarter, 0, i % in_quarter, 0))
    summary_shape = jax.ShapeDtypeStruct((3, half, ny), F32)

    low, summary = pl.pallas_call(
        functools.partial(down_kernel, chunks, per),
        grid=grid,
        in_specs=[chunk_spec] * (2 * chunks) + [factor_spec] * 2,
        out_specs=[low_spec, summary_spec],
        out_shape=[jax.ShapeDtypeStruct((levels, 2, half, ny), F32), summary_shape],
    )(*cos_parts, *sin_parts, inverse_pivot, lower_factor)
    enter = entering(summary, False)
    summary = pl.pallas_call(
        functools.partial(up_summary_kernel, levels),
        grid=grid,
        in_specs=[low_spec, factor_spec, factor_spec, state_spec],
        out_specs=summary_spec,
        out_shape=summary_shape,
    )(low, lower_factor, upper_factor, enter)
    above = entering(summary, True)
    solved = pl.pallas_call(
        functools.partial(solve_kernel, levels, per),
        grid=grid,
        in_specs=[low_spec, factor_spec, factor_spec, state_spec, state_spec],
        out_specs=[chunk_spec] * chunks,
        out_shape=[jax.ShapeDtypeStruct((per, 2, half, ny), F32)] * chunks,
    )(low, lower_factor, upper_factor, enter, above)

    normalizer = 1.0 / (nx * ny)
    fields = []
    for i in range(chunks):
        flat = solved[i].reshape(per, 2 * half, ny)
        c = jnp.einsum("ky,zck->zyc", cy, flat, precision=PREC)
        s = jnp.einsum("ky,zck->zyc", sy, flat, precision=PREC)
        back = jnp.concatenate([c[..., :half] - s[..., half:], c[..., half:] + s[..., :half]], 2)
        back = jnp.transpose(back.reshape(per, gy, rows, 2 * half), (1, 0, 2, 3))
        if i >= 2:
            back, fields[i - 2] = lax.optimization_barrier((back, fields[i - 2]))
        got = lax.all_to_all(back, "gy", split_axis=0, concat_axis=0, tiled=True)
        got = jnp.transpose(got, (1, 2, 0, 3)).reshape(per, rows, 2 * nx)
        field = jnp.einsum("zyc,nc->zyn", got, table, precision=PREC) * normalizer
        fields.append(field.astype(jnp.bfloat16))
    return jnp.concatenate(fields, 0)


BF16 = jnp.bfloat16
MESH = pl.DeviceIdType.MESH
TINY = 1e-36
PEAK = 2.0**14
ROWS = 32
NT = (((1,), (1,)), ((), ()))
NN = (((1,), (0,)), ((), ()))


def split(x):
    high = x.astype(BF16)
    return high, (x - high.astype(F32)).astype(BF16)


def split_host(x):
    high = x.astype(np.float32).astype(ml_dtypes.bfloat16)
    low = (x - high.astype(np.float64)).astype(np.float32).astype(ml_dtypes.bfloat16)
    return high, low


def along_table(nx, gy):
    width = nx // gy
    chunk, g, j = np.meshgrid(np.arange(width // ROWS), np.arange(gy), np.arange(8), indexing="ij")
    parts = []
    for q in (0, 2, 1, 3):
        kx = g * width + ROWS * chunk + 4 * j + q
        turn = 2 * np.pi * ((kx[..., None] * np.arange(nx // 4)) % nx) / nx
        c, s = np.cos(turn), np.sin(turn)
        pair = np.stack([c, -s], 2)
        if q == 1:
            pair = np.concatenate([pair, np.stack([-s, -c], 2)], -1)
        if q == 3:
            pair = np.concatenate([pair, np.stack([s, c], 2)], -1)
        parts.append(pair.reshape(-1, pair.shape[-1]))
    return split_host(np.concatenate(parts, 1))


def across_table(ny):
    quarter = ny // 4
    lane = np.arange(quarter)
    block, inner = lane // 128, lane % 128
    tables = []
    for q in range(4):
        ky = 512 * block + 128 * (inner % 4) + 4 * (inner // 4) + q
        turn = 2 * np.pi * ((np.arange(quarter)[:, None] * ky) % ny) / ny
        c, s = np.cos(turn), np.sin(turn)
        tables.append(np.block([[c, -s], [s, c]]))
    return split_host(np.stack(tables))


def exchange_lanes(vs):
    lane = lax.broadcasted_iota(jnp.int32, vs[0].shape, 1)
    odd, upper = lane % 2 == 1, lane % 4 >= 2

    def turned(xs, sign):
        xs = [jnp.where(odd, xs[(d + sign) % 4], xs[d]) for d in range(4)]
        return [jnp.where(upper, xs[(d + 2) % 4], xs[d]) for d in range(4)]

    ds = turned([vs[-d % 4] for d in range(4)], -1)
    es = [ds[0]] + [
        jnp.take_along_axis(ds[d], lane // 4 * 4 + (lane + d) % 4, axis=1) for d in range(1, 4)
    ]
    return turned(es, -1)


def encode(v):
    v2 = v * v
    v4 = v2 * v2
    return (v4 * v4 * v).astype(BF16)


def decode(w, scale):
    w = w.astype(F32)
    size = jnp.maximum(jnp.abs(w), 2.0**-126)
    return w * jnp.exp2(jnp.log(size) * (-8.0 / (9.0 * math.log(2.0)))) * scale


def dot3(ah, al, bh, bl, dims):
    def one(a, b):
        return lax.dot_general(a, b, dims, preferred_element_type=F32)

    return one(ah, bh) + one(al, bh) + one(ah, bl)


def greet(devices):
    barrier = pltpu.get_barrier_semaphore()
    for device in devices:
        pl.semaphore_signal(barrier, inc=1, device_id=device, device_id_type=MESH)


def forward_kernel(
    n, levels, nx,
    p_hbm, v_hbm, spacing, th_hbm, tl_hbm, yh_hbm, yl_hbm, pivot_hbm, lower_hbm,
    low_hbm, top, gain,
    p_ref, v_all, th, tl, yh, yl, ah, al, stage, got, bh, bl, spec, pivot, lower,
    in_sem, table_sem, edge_send, edge_recv, send_sem, recv_sem, own_sem, factor_sem, low_sem,
):
    me, z, zs = lax.axis_index("gy"), lax.axis_index("gz"), lax.axis_size("gz")
    rows = p_hbm.shape[1]
    x4 = nx // 4
    width = nx // n
    chunks = width // ROWS
    y4 = n * rows // 4
    pairs = levels // 2
    per = 2
    turns = chunks // per
    piece = 4 * per * ROWS
    half = width // 2

    tall = per * 16 * n

    def part(source, to, start, stop, sem):
        r = pl.ds(start, stop - start)
        return pltpu.make_async_copy(source.at[r], to.at[r], sem)

    def table_part(i):
        m = pl.ds(pl.multiple_of(i * tall, tall), tall)
        return [
            pltpu.make_async_copy(source.at[m, :], to.at[m, :], table_sem.at[k, i])
            for k, (source, to) in enumerate(((th_hbm, th), (tl_hbm, tl)))
        ]

    ahead = min(3, levels)
    early = [part(p_hbm, p_ref, 0, 2, in_sem.at[0]), part(v_hbm, v_all, 0, ahead, in_sem.at[1])]
    late = []
    if levels > 2:
        late.append(part(p_hbm, p_ref, 2, levels, in_sem.at[2]))
    if levels > ahead:
        late.append(part(v_hbm, v_all, ahead, levels, in_sem.at[3]))
    across = [
        pltpu.make_async_copy(source, to, in_sem.at[4 + i])
        for i, (source, to) in enumerate(((yh_hbm, yh), (yl_hbm, yl)))
    ]
    for copy in early + [c for i in range(turns) for c in table_part(i)] + late + across:
        copy.start()
    barrier = pltpu.get_barrier_semaphore()
    greet([{"gy": lax.rem(me + d, n)} for d in range(1, n)])

    @pl.when(z < zs - 1)
    def _():
        greet([{"gz": z + 1}])

    pl.semaphore_wait(barrier, n - 1 + jnp.minimum(z, 1))

    def edge():
        return pltpu.make_async_remote_copy(
            src_ref=v_hbm.at[pl.ds(0, 1)], dst_ref=v_all.at[pl.ds(levels, 1)],
            send_sem=edge_send, recv_sem=edge_recv, device_id={"gz": z - 1}, device_id_type=MESH,
        )

    @pl.when(z > 0)
    def _():
        edge().start()

    @pl.when(z == zs - 1)
    def _():
        v_all[levels] = jnp.zeros((rows, nx), BF16)

    top[...] = jnp.zeros_like(top)
    gain[...] = jnp.ones_like(gain)

    def factors(lp):
        return [
            pltpu.make_async_copy(
                hbm.at[pl.ds(2 * lp, 2), :, pl.ds(128 * k, 128)], ref.at[k], factor_sem.at[i, k]
            )
            for i, (hbm, ref) in enumerate(((pivot_hbm, pivot), (lower_hbm, lower)))
            for k in range(y4 // 32)
        ]

    for copy in factors(0):
        copy.start()
    for copy in early:
        copy.wait()

    def own(lp):
        return pltpu.make_async_copy(stage.at[lax.rem(lp, 2), me], got.at[lp, me], own_sem.at[lp])

    def transfer(lp, i, d, source, first):
        peer = lax.rem(me + d, n)
        r = pl.ds(0, 16 + piece) if first else pl.ds(pl.multiple_of(16 + i * piece, 16), piece)
        return pltpu.make_async_remote_copy(
            src_ref=stage.at[lax.rem(lp, 2), peer, r, :], dst_ref=got.at[lp, source, r, :],
            send_sem=send_sem.at[lp, i, d], recv_sem=recv_sem.at[lp, i, source],
            device_id={"gy": peer}, device_id_type=MESH,
        )

    def send(lp, i, d, first):
        return transfer(lp, i, d, me, first)

    def arrival(lp, i, d, first):
        return transfer(lp, i, d, lax.rem(me + d, n), first)

    def sent(lp):
        for d in range(1, n):
            for i in range(turns):
                send(lp, i, d, i == 0).wait_send()

    def low_copy(lp):
        return pltpu.make_async_copy(spec, low_hbm.at[lp], low_sem)

    def spectra(lp):
        @pl.when(lp >= 2)
        def _():
            sent(lp - 2)

        @pl.when(lp == 1)
        def _():
            for copy in late:
                copy.wait()

        @pl.when((lp == pairs - 1) & (z < zs - 1))
        def _():
            edge().wait_recv()

        tile = 16
        peak = jnp.zeros((8, 128), F32)
        for lev in range(2):
            at = 2 * lp + lev
            factor = spacing[at]

            def source(i, peak, lev=lev, at=at, factor=factor):
                r = pl.ds(pl.multiple_of(i * tile, tile), tile)
                q = [pl.ds(k * x4, x4) for k in range(4)]
                xs = [
                    p_ref[at, r, s].astype(F32)
                    + factor * (v_all[at + 1, r, s].astype(F32) - v_all[at, r, s].astype(F32))
                    for s in q
                ]
                size = functools.reduce(jnp.maximum, [jnp.abs(x) for x in xs])
                e, o = xs[0] + xs[2], xs[1] + xs[3]
                to = pl.ds(pl.multiple_of(lev * rows + i * tile, tile), tile)
                for s, a in zip(q, (e + o, e - o, xs[0] - xs[2], xs[1] - xs[3])):
                    ah[to, s], al[to, s] = split(a)
                for k in range(x4 // 128):
                    part = size[:, k * 128 : (k + 1) * 128]
                    peak = jnp.maximum(peak, jnp.maximum(part[:8], part[8:]))
                return peak

            peak = lax.fori_loop(0, rows // tile, source, peak)
        peak = jnp.maximum(jnp.max(peak), TINY)
        held = jnp.full((16, 128), peak, F32).astype(BF16)
        shrink = PEAK / (nx * held.astype(F32)[:1, :1])
        slot = lax.rem(lp, 2)
        for g in range(n):
            stage[slot, g, pl.ds(0, 16), :] = held

        def transform(i, _):
            @pl.when(lp == 0)
            def _():
                for copy in table_part(i):
                    copy.wait()

            m = pl.ds(pl.multiple_of(i * tall, tall), tall)
            outs, at = [None] * 4, 0
            for q in (0, 2, 1, 3):
                wide = x4 if q % 2 == 0 else 2 * x4
                start = (0, 2 * x4, x4, 2 * x4)[q]
                t, a = pl.ds(at, wide), pl.ds(start, wide)
                outs[q] = dot3(th[m, t], tl[m, t], ah[:, a], al[:, a], NT) * shrink
                at += wide
            for k in range(per):
                for g in range(n):
                    for c in range(2):
                        s = (k * n + g) * 16 + c * 8
                        block = encode(jnp.concatenate([o[s : s + 8] for o in outs], 0))
                        for lev in range(2):
                            r = 16 + i * piece + ((lev * 2 + c) * per + k) * ROWS
                            stage[slot, g, pl.ds(pl.multiple_of(r, 16), ROWS), :] = block[
                                :, lev * rows : (lev + 1) * rows
                            ]

            @pl.when(i == 0)
            def _():
                for d in range(1, n):
                    send(lp, 0, d, True).start()

            @pl.when(i > 0)
            def _():
                for d in range(1, n):
                    send(lp, i, d, False).start()

            return 0

        lax.fori_loop(0, turns, transform, 0)
        own(lp).start()

    def substitute(lp):
        own(lp).wait()
        for d in range(1, n):
            arrival(lp, 0, d, True).wait_recv()

        @pl.when(lp == 0)
        def _():
            for copy in across:
                copy.wait()

        @pl.when(lp > 0)
        def _():
            low_copy(lp - 1).wait()

        for copy in factors(lp):
            copy.wait()
        scales = [got[lp, s, pl.ds(0, 16), :].astype(F32)[:1, :] * (nx / PEAK) for s in range(n)]

        def one_half(h, _):
            for k in range(turns // 2):
                for d in range(1, n):
                    if k == 0:
                        @pl.when(h > 0)
                        def _(d=d):
                            arrival(lp, turns // 2, d, False).wait_recv()
                    else:
                        arrival(lp, h * (turns // 2) + k, d, False).wait_recv()
            substitute_half(lp, h, scales)
            return 0

        lax.fori_loop(0, 2, one_half, 0)
        low_copy(lp).start()

        @pl.when(lp < pairs - 1)
        def _():
            for copy in factors(lp + 1):
                copy.start()

    def substitute_half(lp, h, scales):
        tile = 16
        quads = n // 4

        def unpack(i, _):
            row = h * half + i * tile
            turn, inner = row // (per * ROWS), lax.rem(row, per * ROWS)
            for lev in range(2):
                for o in range(quads):
                    xs = []
                    for c in range(2):
                        r = 16 + turn * piece + (lev * 2 + c) * per * ROWS + inner
                        r = pl.ds(pl.multiple_of(r, tile), tile)
                        xs.append([decode(got[lp, k * quads + o, r, :], scales[k * quads + o]) for k in range(4)])
                    (r0, r1, r2, r3), (i0, i1, i2, i3) = xs
                    er, fr, ei, fi = r0 + r2, r0 - r2, i0 + i2, i0 - i2
                    gr, hr, gi, hi = r1 + r3, r1 - r3, i1 + i3, i1 - i3
                    real = (er + gr, fr + hi, er - gr, fr - hi)
                    imag = (ei + gi, fi - hr, ei - gi, fi + hr)
                    to = pl.ds(pl.multiple_of(lev * half + i * tile, tile), tile)
                    for q in range(4):
                        for c, x in enumerate((real[q], imag[q])):
                            s = pl.ds(c * y4 + o * 128, 128)
                            bh[q, to, s], bl[q, to, s] = split(x)
            return 0

        lax.fori_loop(0, half // tile, unpack, 0)
        tall = min(width, 256)

        def transform(i, _):
            r = pl.ds(pl.multiple_of(i * tall, tall), tall)
            ro = pl.ds(pl.multiple_of(h * width + i * tall, tall), tall)
            for k in range(2 * y4 // 256):
                w = pl.ds(k * 256, 256)
                parts = [dot3(bh[q, r, :], bl[q, r, :], yh[q, :, w], yl[q, :, w], NN) for q in range(4)]
                for j in range(2):
                    for t, x in enumerate(exchange_lanes([x[:, j * 128 : (j + 1) * 128] for x in parts])):
                        spec[t, ro, pl.ds(k * 256 + j * 128, 128)] = x
            return 0

        lax.fori_loop(0, width // tall, transform, 0)

        def solve(inner, _):
            i = h * (chunks // 2) + inner
            r = pl.ds(pl.multiple_of(i * ROWS, ROWS), ROWS)
            strided = [pl.ds(i * ROWS + q, 8, stride=4) for q in range(4)]
            for b in range(y4 // 128):
                for t in range(4):
                    s = pl.ds(512 * b + 128 * t, 128)
                    lanes = [pl.ds(c * y4 + b * 128, 128) for c in range(2)]
                    rl = [
                        pl.ds(pl.multiple_of(h * width + lev * half + inner * ROWS, ROWS), ROWS)
                        for lev in range(2)
                    ]
                    ms, ds = [
                        [jnp.concatenate([f[4 * b + t, lev, x, :] for x in strided], 0) for lev in range(2)]
                        for f in (lower, pivot)
                    ]
                    xs = [[spec[t, rl[lev], lanes[c]] for c in range(2)] for lev in range(2)]
                    held, run = [top[c, r, s] for c in range(2)], gain[r, s]
                    first = [ds[0] * xs[0][c] + ms[0] * held[c] for c in range(2)]
                    second = [ds[1] * xs[1][c] + ms[1] * first[c] for c in range(2)]
                    gain[r, s] = run * ms[0] * ms[1]
                    for c in range(2):
                        spec[t, rl[0], lanes[c]] = first[c]
                        spec[t, rl[1], lanes[c]] = second[c]
                        top[c, r, s] = second[c]
            return 0

        lax.fori_loop(0, chunks // 2, solve, 0)

    def step(t, _):
        @pl.when(t < pairs)
        def _():
            spectra(t)

        @pl.when(t >= 1)
        def _():
            substitute(t - 1)

        return 0

    lax.fori_loop(0, pairs + 1, step, 0)
    low_copy(pairs - 1).wait()
    for lp in range(max(pairs - 2, 0), pairs):
        sent(lp)

    @pl.when(z > 0)
    def _():
        edge().wait_send()


def backward_kernel(
    n, levels, nx,
    low_hbm, top_hbm, gain_hbm, lower_hbm, upper_hbm, th_hbm, tl_hbm, yh_hbm, yl_hbm,
    out_hbm,
    th, tl, yh, yl, low, lower, upper, top, gain, enter, above, d_send, u_send, sh, sl, yo, stage, got, xh, xl, acc,
    in_sem, low_sem, load_sem, sum_sem, ds_sem, dr_sem, us_sem, ur_sem, send_sem, recv_sem, own_sem, out_sem,
):
    me, z, zs = lax.axis_index("gy"), lax.axis_index("gz"), lax.axis_size("gz")
    width = nx // n
    chunks = width // ROWS
    rows = out_hbm.shape[0] // levels
    ny = n * rows
    y4, x4 = ny // 4, nx // 4
    body = levels * 2 * ROWS
    per = 2 if chunks % 2 == 0 else 1

    inputs = [
        pltpu.make_async_copy(source, to, in_sem.at[i])
        for i, (source, to) in enumerate(((yh_hbm, yh), (yl_hbm, yl), (th_hbm, th), (tl_hbm, tl)))
    ]

    def loads(c):
        slot = lax.rem(c, 2)
        r = pl.ds(pl.multiple_of(c * ROWS, ROWS), ROWS)
        rh = pl.ds(pl.multiple_of(lax.rem(c, chunks // 2) * ROWS, ROWS), ROWS)
        return [
            pltpu.make_async_copy(
                low_hbm.at[:, :, c // (chunks // 2), :, rh, :], low.at[slot], low_sem.at[slot]
            ),
        ] + [
            pltpu.make_async_copy(hbm.at[:, r, pl.ds(128 * k, 128)], ref.at[slot, k], load_sem.at[slot, i, k])
            for i, (hbm, ref) in enumerate(((lower_hbm, lower), (upper_hbm, upper)))
            for k in range(ny // 128)
        ]

    def sums(c):
        slot = lax.rem(c, 2)
        r = pl.ds(pl.multiple_of(c * ROWS, ROWS), ROWS)
        return [
            pltpu.make_async_copy(top_hbm.at[:, r, :], top.at[slot], sum_sem.at[slot, 0]),
            pltpu.make_async_copy(gain_hbm.at[r, :], gain.at[slot], sum_sem.at[slot, 1]),
        ]

    for copy in sums(0) + loads(0) + inputs:
        copy.start()
    barrier = pltpu.get_barrier_semaphore()
    greet([{"gy": lax.rem(me + d, n)} for d in range(1, n)])

    @pl.when(z < zs - 1)
    def _():
        greet([{"gz": z + 1}])

    @pl.when(z > 0)
    def _():
        greet([{"gz": z - 1}])

    acc[...] = jnp.zeros_like(acc)
    pl.semaphore_wait(barrier, n - 1 + jnp.minimum(z, 1) + jnp.minimum(zs - 1 - z, 1))

    @pl.when(z == 0)
    def _():
        enter[...] = jnp.zeros_like(enter)

    @pl.when(z == zs - 1)
    def _():
        above[...] = jnp.zeros_like(above)

    def state_rows(q):
        return pl.ds(pl.multiple_of(q * 8, 8), 8)

    def pass_down(c, q):
        return pltpu.make_async_remote_copy(
            src_ref=d_send.at[lax.rem(c, 2), :, state_rows(q), :], dst_ref=enter.at[c, :, state_rows(q), :],
            send_sem=ds_sem.at[c, q], recv_sem=dr_sem.at[c, q],
            device_id={"gz": z + 1}, device_id_type=MESH,
        )

    def pass_up(c, q):
        return pltpu.make_async_remote_copy(
            src_ref=u_send.at[lax.rem(c, 2), :, state_rows(q), :], dst_ref=above.at[c, :, state_rows(q), :],
            send_sem=us_sem.at[c, q], recv_sem=ur_sem.at[c, q],
            device_id={"gz": z - 1}, device_id_type=MESH,
        )

    def own(c):
        return pltpu.make_async_copy(stage.at[lax.rem(c, 2), me], got.at[c, me], own_sem.at[c])

    def send(c, d):
        peer = lax.rem(me + d, n)
        return pltpu.make_async_remote_copy(
            src_ref=stage.at[lax.rem(c, 2), peer], dst_ref=got.at[c, me],
            send_sem=send_sem.at[c, d], recv_sem=recv_sem.at[c, me],
            device_id={"gy": peer}, device_id_type=MESH,
        )

    def arrival(c, d):
        peer = lax.rem(me + d, n)
        return pltpu.make_async_remote_copy(
            src_ref=stage.at[lax.rem(c, 2), peer], dst_ref=got.at[c, peer],
            send_sem=send_sem.at[c, d], recv_sem=recv_sem.at[c, peer],
            device_id={"gy": peer}, device_id_type=MESH,
        )

    def relay(c):
        for copy in sums(c):
            copy.wait()

        @pl.when(c + 1 < chunks)
        def _():
            for copy in sums(c + 1):
                copy.start()

        slot = lax.rem(c, 2)

        @pl.when((z < zs - 1) & (c >= 2))
        def _():
            for q in range(4):
                pass_down(c - 2, q).wait_send()

        def carry(q, _):
            r = state_rows(q)

            @pl.when(z > 0)
            def _():
                pass_down(c, q).wait_recv()

            @pl.when(z < zs - 1)
            def _():
                new = [top[slot, k, r, :] + gain[slot, r, :] * enter[c, k, r, :] for k in range(2)]
                for k in range(2):
                    d_send[slot, k, r, :] = new[k]
                pass_down(c, q).start()

            return 0

        lax.fori_loop(0, 4, carry, 0)

    def solve(c):
        slot = lax.rem(c, 2)
        for copy in loads(c):
            copy.wait()

        @pl.when(c + 1 < chunks)
        def _():
            for copy in loads(c + 1):
                copy.start()

        @pl.when((z > 0) & (c >= 2))
        def _():
            for q in range(4):
                pass_up(c - 2, q).wait_send()

        def sweep(q, _):
            strided = pl.ds(q, 8, stride=4)
            r = state_rows(q)

            @pl.when(z < zs - 1)
            def _():
                pass_up(c, q).wait_recv()

            for b in range(y4 // 128):
                natural = [pl.ds(512 * b + 128 * t, 128) for t in range(4)]
                gains = [[] for _ in range(4)]
                for t in range(4):
                    for lev in range(levels):
                        m = lower[slot, 4 * b + t, lev, strided, :]
                        gains[t].append(m if lev == 0 else gains[t][-1] * m)
                state = [[above[c, k, r, s] for s in natural] for k in range(2)]
                entry = [[enter[c, k, r, s] for s in natural] for k in range(2)]
                for lev in range(levels - 1, -1, -1):
                    ups = [upper[slot, 4 * b + t, lev, strided, :] for t in range(4)]
                    for k in range(2):
                        lanes = pl.ds(k * y4 + b * 128, 128)
                        state[k] = [
                            low[slot, lev // 2, t, lev % 2, r, lanes] + gains[t][lev] * entry[k][t] + ups[t] * state[k][t]
                            for t in range(4)
                        ]
                        to = pl.ds(pl.multiple_of(lev * ROWS + q * 8, 8), 8)
                        for t in range(4):
                            yo[t, to, lanes] = state[k][t]
                for k in range(2):
                    for t in range(4):
                        u_send[slot, k, r, natural[t]] = state[k][t]

            @pl.when(z > 0)
            def _():
                pass_up(c, q).start()

            return 0

        lax.fori_loop(0, 4, sweep, 0)

        @pl.when(c == 0)
        def _():
            for copy in inputs:
                copy.wait()

        @pl.when(c >= 2)
        def _():
            own(c - 2).wait()
            for d in range(1, n):
                send(c - 2, d).wait_send()

        count = levels * ROWS

        def halve(i, _):
            r = pl.ds(pl.multiple_of(i * ROWS, ROWS), ROWS)
            for k in range(2 * y4 // 128):
                s = pl.ds(k * 128, 128)
                for q, x in enumerate(exchange_lanes([yo[t, r, s] for t in range(4)])):
                    sh[q, r, s], sl[q, r, s] = split(x)
            return 0

        lax.fori_loop(0, levels, halve, 0)

        def transform(q, _):
            yo[q] = dot3(sh[q], sl[q], yh[q], yl[q], NT)
            return 0

        lax.fori_loop(0, 4, transform, 0)

        def combine(i, peak):
            r = pl.ds(pl.multiple_of(i * 8, 8), 8)
            for h in range(y4 // 128):
                rs = pl.ds(h * 128, 128)
                cs = pl.ds(y4 + h * 128, 128)
                r0, r1, r2, r3 = [yo[q, r, rs] for q in range(4)]
                i0, i1, i2, i3 = [yo[q, r, cs] for q in range(4)]
                er, fr, ei, fi = r0 + r2, r0 - r2, i0 + i2, i0 - i2
                gr, hr, gi, hi = r1 + r3, r1 - r3, i1 + i3, i1 - i3
                real = (er + gr, fr - hi, er - gr, fr + hi)
                imag = (ei + gi, fi + hr, ei - gi, fi - hr)
                for q in range(4):
                    yo[q, r, rs] = real[q]
                    yo[q, r, cs] = imag[q]
                    peak = jnp.maximum(peak, jnp.maximum(jnp.abs(real[q]), jnp.abs(imag[q])))
            return peak

        peak = lax.fori_loop(0, count // 8, combine, jnp.zeros((8, 128), F32))
        held = jnp.full((16, 128), jnp.maximum(jnp.max(peak), TINY), F32).astype(BF16)
        shrink = PEAK / held.astype(F32)[:1, :1]
        quads = n // 4
        for g in range(n):
            stage[slot, g, pl.ds(body, 16), :] = held

        def pack(lev, _):
            r = pl.ds(pl.multiple_of(lev * ROWS, ROWS), ROWS)
            for g in range(n):
                for k in range(2):
                    x = yo[g // quads, r, pl.ds(k * y4 + (g % quads) * 128, 128)]
                    to = pl.ds(pl.multiple_of((lev * 2 + k) * ROWS, ROWS), ROWS)
                    stage[slot, g, to, :] = encode(x * shrink)
            return 0

        lax.fori_loop(0, levels, pack, 0)
        own(c).start()
        for d in range(1, n):
            send(c, d).start()

    def done(lp):
        r = pl.ds(pl.multiple_of(lp * 2 * rows, 2 * rows), 2 * rows)
        return pltpu.make_async_copy(acc.at[r, :], out_hbm.at[r, :], out_sem.at[lp])

    def gather(pair, final=False):
        for k in range(per):
            c = pair * per + k

            for d in range(1, n):
                arrival(c, d).wait_recv()

        scales = [
            [got[pair * per + k, s, pl.ds(body, 16), :].astype(F32)[:1, :] * (1.0 / (PEAK * nx * ny)) for s in range(n)]
            for k in range(per)
        ]
        deep = per * 16 * n

        def two_levels(lp, _):
            for lev in range(2):
                for k in range(per):
                    parts = []
                    for s in range(n):
                        for j in range(2):
                            r = ((lp * 2 + lev) * 2 + j) * ROWS
                            r = pl.ds(pl.multiple_of(r, ROWS), ROWS)
                            parts.append(decode(got[pair * per + k, s, r, :], scales[k][s]))
                    for q in range(4):
                        block = jnp.concatenate([x[q * 8 : q * 8 + 8] for x in parts], 0)
                        high, low_part = split(block.T)
                        lanes = pl.ds(k * 16 * n, 16 * n)
                        xh[q, pl.ds(lev * rows, rows), lanes] = high
                        xl[q, pl.ds(lev * rows, rows), lanes] = low_part
            m = pl.ds(pl.multiple_of(pair * deep, deep), deep)
            to = pl.ds(pl.multiple_of(lp * 2 * rows, 2 * rows), 2 * rows)

            def part(q, start, wide):
                t = pl.ds(start, wide)
                return dot3(xh[q], xl[q], th[m, t], tl[m, t], NN)

            acc[to, pl.ds(0, x4)] += part(0, 0, x4)
            acc[to, pl.ds(x4, x4)] += part(2, x4, x4)
            acc[to, pl.ds(2 * x4, 2 * x4)] += part(1, 2 * x4, 2 * x4) + part(3, 4 * x4, 2 * x4)
            if final:
                done(lp).start()
            return 0

        lax.fori_loop(0, levels // 2, two_levels, 0)

    lag = zs - 1
    halves = chunks // per

    def step(t, _):
        @pl.when(t < chunks)
        def _():
            relay(t)

        c = t - lag + z

        @pl.when((c >= 0) & (c < chunks))
        def _():
            solve(c)

        @pl.when((c >= 2 * per - 1) & (c < chunks) & (lax.rem(c + 1 + 2 * per, per) == 0))
        def _():
            gather((c + 1) // per - 2)

        return 0

    last = chunks - 1
    lax.fori_loop(0, chunks + lag, step, 0)
    for c in range(max(chunks - 2, 0), chunks):
        own(c).wait()
        for d in range(1, n):
            send(c, d).wait_send()

        @pl.when(z < zs - 1)
        def _():
            for q in range(4):
                pass_down(c, q).wait_send()

        @pl.when(z > 0)
        def _():
            for q in range(4):
                pass_up(c, q).wait_send()

    gather(halves - 1, final=True)
    for lp in range(levels // 2):
        done(lp).wait()


def finish_kernel(acc, out):
    x4 = acc.shape[1] // 4
    a0, a2, u, w = [acc[:, s * x4 : (s + 1) * x4] for s in range(4)]
    e, o = a0 + a2, a0 - a2
    for s, x in enumerate((e + u, o + w, e - u, o - w)):
        out[0, :, s * x4 : (s + 1) * x4] = x.astype(BF16)


def fast_device(p, v, inverse_spacing, inverse_pivot, lower_factor, upper_factor):
    levels, rows, nx = p.shape
    n = lax.axis_size("gy")
    width, ny = nx // n, n * rows
    y4 = ny // 4
    pairs, chunks = levels // 2, nx // n // ROWS
    th, tl = [jnp.asarray(t) for t in along_table(nx, n)]
    yh, yl = [jnp.asarray(t) for t in across_table(ny)]
    anyspace = pl.BlockSpec(memory_space=pl.ANY)
    vmem = pl.BlockSpec(memory_space=pltpu.VMEM)
    dma = pltpu.SemaphoreType.DMA
    message = 4 * width + 16
    tables = [pltpu.VMEM(t.shape, BF16) for t in (th, tl, yh, yl)]
    low, top, gain = pl.pallas_call(
        functools.partial(forward_kernel, n, levels, nx),
        out_shape=[
            jax.ShapeDtypeStruct((pairs, 4, 2 * width, 2 * y4), F32),
            jax.ShapeDtypeStruct((2, width, ny), F32),
            jax.ShapeDtypeStruct((width, ny), F32),
        ],
        in_specs=[anyspace] * 2 + [pl.BlockSpec(memory_space=pltpu.SMEM)] + [anyspace] * 6,
        out_specs=[anyspace, vmem, vmem],
        scratch_shapes=[
            pltpu.VMEM((levels, rows, nx), BF16),
            pltpu.VMEM((levels + 1, rows, nx), BF16),
            *tables,
            pltpu.VMEM((2 * rows, nx), BF16),
            pltpu.VMEM((2 * rows, nx), BF16),
            pltpu.VMEM((2, n, message, 128), BF16),
            pltpu.VMEM((pairs, n, message, 128), BF16),
            pltpu.VMEM((4, 2 * width, 2 * y4), BF16),
            pltpu.VMEM((4, 2 * width, 2 * y4), BF16),
            pltpu.VMEM((4, 2 * width, 2 * y4), F32),
            pltpu.VMEM((ny // 128, 2, width, 128), F32),
            pltpu.VMEM((ny // 128, 2, width, 128), F32),
            dma((6,)), dma((2, chunks // 2)), dma, dma,
            dma((pairs, chunks // 2, n)), dma((pairs, chunks // 2, n)), dma((pairs,)), dma((2, ny // 128)), dma,
        ],
        compiler_params=pltpu.CompilerParams(
            collective_id=0, has_side_effects=True, vmem_limit_bytes=62 * 2**20
        ),
        name="forward",
    )(p, v, inverse_spacing, th, tl, yh, yl, inverse_pivot, lower_factor)

    low = low.reshape(pairs, 4, 2, 2, width // 2, 2 * y4)
    message = levels * 2 * ROWS + 16
    per = 2 if chunks % 2 == 0 else 1
    count = levels * ROWS
    acc = pl.pallas_call(
        functools.partial(backward_kernel, n, levels, nx),
        out_shape=jax.ShapeDtypeStruct((levels * rows, nx), F32),
        in_specs=[anyspace] * 9,
        out_specs=anyspace,
        scratch_shapes=[
            *tables,
            pltpu.VMEM((2, pairs, 4, 2, ROWS, 2 * y4), F32),
            pltpu.VMEM((2, ny // 128, levels, ROWS, 128), F32),
            pltpu.VMEM((2, ny // 128, levels, ROWS, 128), F32),
            pltpu.VMEM((2, 2, ROWS, ny), F32),
            pltpu.VMEM((2, ROWS, ny), F32),
            pltpu.VMEM((chunks, 2, ROWS, ny), F32),
            pltpu.VMEM((chunks, 2, ROWS, ny), F32),
            pltpu.VMEM((2, 2, ROWS, ny), F32),
            pltpu.VMEM((2, 2, ROWS, ny), F32),
            pltpu.VMEM((4, count, 2 * y4), BF16),
            pltpu.VMEM((4, count, 2 * y4), BF16),
            pltpu.VMEM((4, count, 2 * y4), F32),
            pltpu.VMEM((2, n, message, 128), BF16),
            pltpu.VMEM((chunks, n, message, 128), BF16),
            pltpu.VMEM((4, 2 * rows, per * 16 * n), BF16),
            pltpu.VMEM((4, 2 * rows, per * 16 * n), BF16),
            pltpu.VMEM((levels * rows, nx), F32),
            dma((4,)), dma((2,)), dma((2, 2, ny // 128)), dma((2, 2)),
            dma((chunks, 4)), dma((chunks, 4)), dma((chunks, 4)), dma((chunks, 4)),
            dma((chunks, n)), dma((chunks, n)), dma((chunks,)), dma((pairs,)),
        ],
        compiler_params=pltpu.CompilerParams(
            collective_id=1, has_side_effects=True, vmem_limit_bytes=62 * 2**20
        ),
        name="backward",
    )(low, top, gain, lower_factor, upper_factor, th, tl, yh, yl)
    return pl.pallas_call(
        finish_kernel,
        grid=(levels,),
        out_shape=jax.ShapeDtypeStruct((levels, rows, nx), BF16),
        in_specs=[pl.BlockSpec((rows, nx), lambda i: (i, 0))],
        out_specs=pl.BlockSpec((1, rows, nx), lambda i: (i, 0, 0)),
        name="finish",
    )(acc)


def solution(mesh):
    spec = P("gz", "gy", None)

    def program(*arrays):
        levels, ny, nx = arrays[0].shape
        gy, gz = mesh.shape["gy"], mesh.shape["gz"]
        fast = ny // gy == 128 and gy % 4 == 0 and levels // gz % 2 == 0 and nx // gy % (4 * ROWS) == 0
        return jax.shard_map(
            fast_device if fast else on_device,
            mesh=mesh,
            in_specs=(spec, spec, P("gz"), spec, spec, spec),
            out_specs=spec,
            check_vma=False,
        )(*arrays)

    return program
```

```python
import functools
import math

import jax
import jax.numpy as jnp
import ml_dtypes
import numpy as np
from jax import lax
from jax.experimental import pallas as pl
from jax.experimental.pallas import tpu as pltpu
from jax.sharding import PartitionSpec as P

PREC = lax.Precision.HIGH
F32 = jnp.float32


def passed_along(x, axis, by):
    size = lax.axis_size(axis)
    pairs = [(i, i + by) for i in range(size) if 0 <= i + by < size]
    return lax.ppermute(x, axis, pairs)


def unit_circle(phase, count):
    angle = (phase % count).astype(F32) * (2.0 * math.pi / count)
    return jnp.cos(angle), jnp.sin(angle)


def circle_table(count):
    low = 32
    high = count // low
    k = jnp.arange(count, dtype=jnp.int32)[None, :]
    ch, sh = unit_circle(jnp.arange(high, dtype=jnp.int32)[:, None] * low * k, count)
    cl, sl = unit_circle(jnp.arange(low, dtype=jnp.int32)[:, None] * k, count)
    ch, sh, cl, sl = lax.optimization_barrier((ch, sh, cl, sl))
    ch, sh, cl, sl = ch[:, None], sh[:, None], cl[None], sl[None]
    cosine = (ch * cl - sh * sl).reshape(count, count)
    sine = (sh * cl + ch * sl).reshape(count, count)
    return cosine, sine


def split_table(count, half):
    low = 32
    column = jnp.arange(2 * count, dtype=jnp.int32)[None, :]
    k = column // (2 * half) * half + column % half
    quarter = jnp.where(column % (2 * half) < half, 0, count // 4)
    ch, sh = unit_circle(jnp.arange(count // low, dtype=jnp.int32)[:, None] * low * k, count)
    cl, sl = unit_circle(jnp.arange(low, dtype=jnp.int32)[:, None] * k + quarter, count)
    ch, sh, cl, sl = lax.optimization_barrier((ch, sh, cl, sl))
    return (ch[:, None] * cl[None] - sh[:, None] * sl[None]).reshape(count, 2 * count)


def down_kernel(chunks, per, *refs):
    cos_refs, sin_refs = refs[:chunks], refs[chunks : 2 * chunks]
    pivot, lower, low, summary = refs[2 * chunks :]
    re = im = jnp.zeros(pivot.shape[1:], F32)
    gain = jnp.ones(pivot.shape[1:], F32)
    for z in range(chunks * per):
        c, s = cos_refs[z // per], sin_refs[z // per]
        q = z % per
        d, m = pivot[z], lower[z]
        re = d * (c[q, 0] + s[q, 1]) + m * re
        im = d * (c[q, 1] - s[q, 0]) + m * im
        gain = m * gain
        low[z, 0] = re
        low[z, 1] = im
    summary[0] = gain
    summary[1] = re
    summary[2] = im


def up_summary_kernel(levels, low, lower, upper, enter, summary):
    er, ei = enter[0, 0], enter[0, 1]
    re = im = jnp.zeros(lower.shape[1:], F32)
    gain = jnp.ones(lower.shape[1:], F32)
    carried = jnp.ones(lower.shape[1:], F32)
    for z in range(levels):
        carried = carried * lower[z]
        re = re + gain * (low[z, 0] + carried * er)
        im = im + gain * (low[z, 1] + carried * ei)
        gain = gain * upper[z]
    summary[0] = gain
    summary[1] = re
    summary[2] = im


def solve_kernel(levels, per, low, lower, upper, enter, above, *outs):
    er, ei = enter[0, 0], enter[0, 1]
    gains = []
    carried = jnp.ones(lower.shape[1:], F32)
    for z in range(levels):
        carried = carried * lower[z]
        gains.append(carried)
    re, im = above[0, 0], above[0, 1]
    for z in range(levels - 1, -1, -1):
        re = low[z, 0] + gains[z] * er + upper[z] * re
        im = low[z, 1] + gains[z] * ei + upper[z] * im
        outs[z // per][z % per, 0] = re
        outs[z // per][z % per, 1] = im


def entering(summary, reverse):
    count = lax.axis_size("gz")
    _, width, span = summary.shape
    parts = summary.reshape(3, count, width // count, span)
    got = lax.all_to_all(parts, "gz", split_axis=1, concat_axis=1, tiled=True)
    order = list(range(count))
    if reverse:
        order.reverse()
    states = [None] * count
    state = jnp.zeros((2, width // count, span), F32)
    for at in order:
        states[at] = state
        state = got[1:, at] + got[0, at][None] * state
    return lax.all_to_all(jnp.stack(states), "gz", split_axis=0, concat_axis=0, tiled=True)


def on_device(
    pressure_cotangent,
    velocity_cotangent,
    inverse_spacing,
    inverse_pivot,
    lower_factor,
    upper_factor,
):
    levels, rows, nx = pressure_cotangent.shape
    level_above = passed_along(velocity_cotangent[:1], "gz", -1)
    gy = lax.axis_size("gy")
    gz = lax.axis_size("gz")
    ny = rows * gy
    half = nx // gy
    per = 2 if levels % 2 == 0 else 1
    chunks = levels // per
    velocity = velocity_cotangent.astype(F32)
    shifted = jnp.concatenate([velocity[1:], level_above.astype(F32)], 0)
    source = pressure_cotangent.astype(F32) + inverse_spacing[:, None, None] * (shifted - velocity)

    table = lax.optimization_barrier(split_table(nx, half))
    cy, sy = lax.optimization_barrier(circle_table(ny))

    cos_parts, sin_parts = [], []
    for i in range(chunks):
        piece = source[i * per : (i + 1) * per]
        spec = jnp.einsum("zyn,nc->zyc", piece, table, precision=PREC)
        spec = jnp.transpose(spec.reshape(per, rows, gy, 2 * half), (2, 0, 1, 3))
        if i >= 2:
            spec, cos_parts[i - 2], sin_parts[i - 2] = lax.optimization_barrier(
                (spec, cos_parts[i - 2], sin_parts[i - 2])
            )
        got = lax.all_to_all(spec, "gy", split_axis=0, concat_axis=0, tiled=True)
        got = jnp.transpose(got, (1, 0, 2, 3)).reshape(per, ny, 2 * half)
        c = jnp.einsum("zyc,yk->zck", got, cy, precision=PREC)
        s = jnp.einsum("zyc,yk->zck", got, sy, precision=PREC)
        cos_parts.append(c.reshape(per, 2, half, ny))
        sin_parts.append(s.reshape(per, 2, half, ny))

    quarter = half // gz
    kb = min(16, quarter)
    in_quarter = quarter // kb
    grid = (half // kb,)
    chunk_spec = pl.BlockSpec((per, 2, kb, ny), lambda i: (0, 0, i, 0))
    factor_spec = pl.BlockSpec((levels, kb, ny), lambda i: (0, i, 0))
    low_spec = pl.BlockSpec((levels, 2, kb, ny), lambda i: (0, 0, i, 0))
    summary_spec = pl.BlockSpec((3, kb, ny), lambda i: (0, i, 0))
    state_spec = pl.BlockSpec((1, 2, kb, ny), lambda i: (i // in_quarter, 0, i % in_quarter, 0))
    summary_shape = jax.ShapeDtypeStruct((3, half, ny), F32)

    low, summary = pl.pallas_call(
        functools.partial(down_kernel, chunks, per),
        grid=grid,
        in_specs=[chunk_spec] * (2 * chunks) + [factor_spec] * 2,
        out_specs=[low_spec, summary_spec],
        out_shape=[jax.ShapeDtypeStruct((levels, 2, half, ny), F32), summary_shape],
    )(*cos_parts, *sin_parts, inverse_pivot, lower_factor)
    enter = entering(summary, False)
    summary = pl.pallas_call(
        functools.partial(up_summary_kernel, levels),
        grid=grid,
        in_specs=[low_spec, factor_spec, factor_spec, state_spec],
        out_specs=summary_spec,
        out_shape=summary_shape,
    )(low, lower_factor, upper_factor, enter)
    above = entering(summary, True)
    solved = pl.pallas_call(
        functools.partial(solve_kernel, levels, per),
        grid=grid,
        in_specs=[low_spec, factor_spec, factor_spec, state_spec, state_spec],
        out_specs=[chunk_spec] * chunks,
        out_shape=[jax.ShapeDtypeStruct((per, 2, half, ny), F32)] * chunks,
    )(low, lower_factor, upper_factor, enter, above)

    normalizer = 1.0 / (nx * ny)
    fields = []
    for i in range(chunks):
        flat = solved[i].reshape(per, 2 * half, ny)
        c = jnp.einsum("ky,zck->zyc", cy, flat, precision=PREC)
        s = jnp.einsum("ky,zck->zyc", sy, flat, precision=PREC)
        back = jnp.concatenate([c[..., :half] - s[..., half:], c[..., half:] + s[..., :half]], 2)
        back = jnp.transpose(back.reshape(per, gy, rows, 2 * half), (1, 0, 2, 3))
        if i >= 2:
            back, fields[i - 2] = lax.optimization_barrier((back, fields[i - 2]))
        got = lax.all_to_all(back, "gy", split_axis=0, concat_axis=0, tiled=True)
        got = jnp.transpose(got, (1, 2, 0, 3)).reshape(per, rows, 2 * nx)
        field = jnp.einsum("zyc,nc->zyn", got, table, precision=PREC) * normalizer
        fields.append(field.astype(jnp.bfloat16))
    return jnp.concatenate(fields, 0)


BF16 = jnp.bfloat16
MESH = pl.DeviceIdType.MESH
TINY = 1e-36
PEAK = 2.0**14
ROWS = 32
NT = (((1,), (1,)), ((), ()))
NN = (((1,), (0,)), ((), ()))


def split(x):
    high = x.astype(BF16)
    return high, (x - high.astype(F32)).astype(BF16)


def split_host(x):
    high = x.astype(np.float32).astype(ml_dtypes.bfloat16)
    low = (x - high.astype(np.float64)).astype(np.float32).astype(ml_dtypes.bfloat16)
    return high, low


def along_table(nx, gy):
    width = nx // gy
    chunk, g, j = np.meshgrid(np.arange(width // ROWS), np.arange(gy), np.arange(8), indexing="ij")
    parts = []
    for q in (0, 2, 1, 3):
        kx = g * width + ROWS * chunk + 4 * j + q
        turn = 2 * np.pi * ((kx[..., None] * np.arange(nx // 4)) % nx) / nx
        c, s = np.cos(turn), np.sin(turn)
        pair = np.stack([c, -s], 2)
        if q == 1:
            pair = np.concatenate([pair, np.stack([-s, -c], 2)], -1)
        if q == 3:
            pair = np.concatenate([pair, np.stack([s, c], 2)], -1)
        parts.append(pair.reshape(-1, pair.shape[-1]))
    return split_host(np.concatenate(parts, 1))


def across_table(ny):
    quarter = ny // 4
    lane = np.arange(quarter)
    block, inner = lane // 128, lane % 128
    tables = []
    for q in range(4):
        ky = 512 * block + 128 * (inner % 4) + 4 * (inner // 4) + q
        turn = 2 * np.pi * ((np.arange(quarter)[:, None] * ky) % ny) / ny
        c, s = np.cos(turn), np.sin(turn)
        tables.append(np.block([[c, -s], [s, c]]))
    return split_host(np.stack(tables))


def exchange_lanes(vs):
    lane = lax.broadcasted_iota(jnp.int32, vs[0].shape, 1)
    odd, upper = lane % 2 == 1, lane % 4 >= 2

    def turned(xs, sign):
        xs = [jnp.where(odd, xs[(d + sign) % 4], xs[d]) for d in range(4)]
        return [jnp.where(upper, xs[(d + 2) % 4], xs[d]) for d in range(4)]

    ds = turned([vs[-d % 4] for d in range(4)], -1)
    es = [ds[0]] + [
        jnp.take_along_axis(ds[d], lane // 4 * 4 + (lane + d) % 4, axis=1) for d in range(1, 4)
    ]
    return turned(es, -1)


def encode(v):
    v2 = v * v
    v4 = v2 * v2
    return (v4 * v4 * v).astype(BF16)


def decode(w, scale):
    w = w.astype(F32)
    size = jnp.maximum(jnp.abs(w), 2.0**-126)
    return w * jnp.exp2(jnp.log(size) * (-8.0 / (9.0 * math.log(2.0)))) * scale


def dot3(ah, al, bh, bl, dims):
    def one(a, b):
        return lax.dot_general(a, b, dims, preferred_element_type=F32)

    return one(ah, bh) + one(al, bh) + one(ah, bl)


def greet(devices):
    barrier = pltpu.get_barrier_semaphore()
    for device in devices:
        pl.semaphore_signal(barrier, inc=1, device_id=device, device_id_type=MESH)


def forward_kernel(
    n, levels, nx,
    p_hbm, v_hbm, spacing, th_hbm, tl_hbm, yh_hbm, yl_hbm, pivot_hbm, lower_hbm,
    low_hbm, top, gain,
    p_ref, v_all, th, tl, yh, yl, ah, al, stage, got, note, notes, bh, bl, spec, pivot, lower,
    in_sem, table_sem, edge_send, edge_recv, send_sem, recv_sem, note_send, note_recv, own_sem, factor_sem, low_sem,
):
    me, z, zs = lax.axis_index("gy"), lax.axis_index("gz"), lax.axis_size("gz")
    rows = p_hbm.shape[1]
    x4 = nx // 4
    width = nx // n
    chunks = width // ROWS
    y4 = n * rows // 4
    pairs = levels // 2
    per = 2
    turns = chunks // per
    piece = 4 * per * ROWS
    half = width // 2

    tall = per * 16 * n

    def part(source, to, start, stop, sem):
        r = pl.ds(start, stop - start)
        return pltpu.make_async_copy(source.at[r], to.at[r], sem)

    def table_part(i):
        m = pl.ds(pl.multiple_of(i * tall, tall), tall)
        return [
            pltpu.make_async_copy(source.at[m, :], to.at[m, :], table_sem.at[k, i])
            for k, (source, to) in enumerate(((th_hbm, th), (tl_hbm, tl)))
        ]

    ahead = min(3, levels)
    early = [part(p_hbm, p_ref, 0, 2, in_sem.at[0]), part(v_hbm, v_all, 0, ahead, in_sem.at[1])]
    late = []
    if levels > 2:
        late.append(part(p_hbm, p_ref, 2, levels, in_sem.at[2]))
    if levels > ahead:
        late.append(part(v_hbm, v_all, ahead, levels, in_sem.at[3]))
    across = [
        pltpu.make_async_copy(source, to, in_sem.at[4 + i])
        for i, (source, to) in enumerate(((yh_hbm, yh), (yl_hbm, yl)))
    ]
    for copy in early + [c for i in range(turns) for c in table_part(i)] + late + across:
        copy.start()
    barrier = pltpu.get_barrier_semaphore()
    greet([{"gy": lax.rem(me + d, n)} for d in range(1, n)])

    @pl.when(z < zs - 1)
    def _():
        greet([{"gz": z + 1}])

    pl.semaphore_wait(barrier, n - 1 + jnp.minimum(z, 1))

    def edge():
        return pltpu.make_async_remote_copy(
            src_ref=v_hbm.at[pl.ds(0, 1)], dst_ref=v_all.at[pl.ds(levels, 1)],
            send_sem=edge_send, recv_sem=edge_recv, device_id={"gz": z - 1}, device_id_type=MESH,
        )

    @pl.when(z > 0)
    def _():
        edge().start()

    @pl.when(z == zs - 1)
    def _():
        v_all[levels] = jnp.zeros((rows, nx), BF16)

    top[...] = jnp.zeros_like(top)
    gain[...] = jnp.ones_like(gain)

    def factors(lp):
        return [
            pltpu.make_async_copy(
                hbm.at[pl.ds(2 * lp, 2), :, pl.ds(128 * k, 128)], ref.at[k], factor_sem.at[i, k]
            )
            for i, (hbm, ref) in enumerate(((pivot_hbm, pivot), (lower_hbm, lower)))
            for k in range(y4 // 32)
        ]

    for copy in factors(0):
        copy.start()
    for copy in early:
        copy.wait()

    def own(lp):
        return pltpu.make_async_copy(stage.at[lax.rem(lp, 2), me], got.at[lp, me], own_sem.at[lp])

    def transfer(lp, i, d, source):
        peer = lax.rem(me + d, n)
        r = pl.ds(pl.multiple_of(i * piece, piece), piece)
        return pltpu.make_async_remote_copy(
            src_ref=stage.at[lax.rem(lp, 2), peer, r, :], dst_ref=got.at[lp, source, r, :],
            send_sem=send_sem.at[lp, i, d], recv_sem=recv_sem.at[lp, i, source],
            device_id={"gy": peer}, device_id_type=MESH,
        )

    def tell(lp, d, source):
        return pltpu.make_async_remote_copy(
            src_ref=note.at[lax.rem(lp, 2)], dst_ref=notes.at[lp, source],
            send_sem=note_send.at[lp, d], recv_sem=note_recv.at[lp, source],
            device_id={"gy": lax.rem(me + d, n)}, device_id_type=MESH,
        )

    def send(lp, i, d):
        return transfer(lp, i, d, me)

    def arrival(lp, i, d):
        return transfer(lp, i, d, lax.rem(me + d, n))

    def sent(lp):
        for d in range(1, n):
            tell(lp, d, me).wait_send()
            for i in range(turns):
                send(lp, i, d).wait_send()

    def low_copy(lp):
        return pltpu.make_async_copy(spec, low_hbm.at[lp], low_sem)

    def spectra(lp):
        @pl.when(lp >= 2)
        def _():
            sent(lp - 2)

        @pl.when(lp == 1)
        def _():
            for copy in late:
                copy.wait()

        @pl.when((lp == pairs - 1) & (z < zs - 1))
        def _():
            edge().wait_recv()

        tile = 16
        peak = jnp.zeros((8, 128), F32)
        for lev in range(2):
            at = 2 * lp + lev
            factor = spacing[at]

            def source(i, peak, lev=lev, at=at, factor=factor):
                r = pl.ds(pl.multiple_of(i * tile, tile), tile)
                q = [pl.ds(k * x4, x4) for k in range(4)]
                xs = [
                    p_ref[at, r, s].astype(F32)
                    + factor * (v_all[at + 1, r, s].astype(F32) - v_all[at, r, s].astype(F32))
                    for s in q
                ]
                size = functools.reduce(jnp.maximum, [jnp.abs(x) for x in xs])
                e, o = xs[0] + xs[2], xs[1] + xs[3]
                to = pl.ds(pl.multiple_of(lev * rows + i * tile, tile), tile)
                for s, a in zip(q, (e + o, e - o, xs[0] - xs[2], xs[1] - xs[3])):
                    ah[to, s], al[to, s] = split(a)
                for k in range(x4 // 128):
                    part = size[:, k * 128 : (k + 1) * 128]
                    peak = jnp.maximum(peak, jnp.maximum(part[:8], part[8:]))
                return peak

            peak = lax.fori_loop(0, rows // tile, source, peak)
        peak = jnp.maximum(jnp.max(peak), TINY)
        held = jnp.full((1, 128), peak, F32)
        shrink = PEAK / (nx * held[:1, :1])
        slot = lax.rem(lp, 2)
        note[slot] = held
        notes[lp, me] = held
        for d in range(1, n):
            tell(lp, d, me).start()

        def transform(i, _):
            @pl.when(lp == 0)
            def _():
                for copy in table_part(i):
                    copy.wait()

            m = pl.ds(pl.multiple_of(i * tall, tall), tall)
            outs, at = [None] * 4, 0
            for q in (0, 2, 1, 3):
                wide = x4 if q % 2 == 0 else 2 * x4
                start = (0, 2 * x4, x4, 2 * x4)[q]
                t, a = pl.ds(at, wide), pl.ds(start, wide)
                outs[q] = dot3(th[m, t], tl[m, t], ah[:, a], al[:, a], NT) * shrink
                at += wide
            for k in range(per):
                for g in range(n):
                    for c in range(2):
                        s = (k * n + g) * 16 + c * 8
                        block = encode(jnp.concatenate([o[s : s + 8] for o in outs], 0))
                        for lev in range(2):
                            r = i * piece + ((lev * 2 + c) * per + k) * ROWS
                            stage[slot, g, pl.ds(pl.multiple_of(r, ROWS), ROWS), :] = block[
                                :, lev * rows : (lev + 1) * rows
                            ]

            for d in range(1, n):
                send(lp, i, d).start()
            return 0

        lax.fori_loop(0, turns, transform, 0)
        own(lp).start()

    def substitute(lp):
        own(lp).wait()
        for d in range(1, n):
            tell(lp, d, lax.rem(me + d, n)).wait_recv()

        @pl.when(lp == 0)
        def _():
            for copy in across:
                copy.wait()

        @pl.when(lp > 0)
        def _():
            low_copy(lp - 1).wait()

        for copy in factors(lp):
            copy.wait()
        scales = [notes[lp, s] * (nx / PEAK) for s in range(n)]

        def one_half(h, _):
            for k in range(turns // 2):
                for d in range(1, n):
                    arrival(lp, h * (turns // 2) + k, d).wait_recv()
            substitute_half(lp, h, scales)
            return 0

        lax.fori_loop(0, 2, one_half, 0)
        low_copy(lp).start()

        @pl.when(lp < pairs - 1)
        def _():
            for copy in factors(lp + 1):
                copy.start()

    def substitute_half(lp, h, scales):
        tile = 16
        quads = n // 4

        def unpack(i, _):
            row = h * half + i * tile
            turn, inner = row // (per * ROWS), lax.rem(row, per * ROWS)
            for lev in range(2):
                for o in range(quads):
                    xs = []
                    for c in range(2):
                        r = turn * piece + (lev * 2 + c) * per * ROWS + inner
                        r = pl.ds(pl.multiple_of(r, tile), tile)
                        xs.append([decode(got[lp, k * quads + o, r, :], scales[k * quads + o]) for k in range(4)])
                    (r0, r1, r2, r3), (i0, i1, i2, i3) = xs
                    er, fr, ei, fi = r0 + r2, r0 - r2, i0 + i2, i0 - i2
                    gr, hr, gi, hi = r1 + r3, r1 - r3, i1 + i3, i1 - i3
                    real = (er + gr, fr + hi, er - gr, fr - hi)
                    imag = (ei + gi, fi - hr, ei - gi, fi + hr)
                    to = pl.ds(pl.multiple_of(lev * half + i * tile, tile), tile)
                    for q in range(4):
                        for c, x in enumerate((real[q], imag[q])):
                            s = pl.ds(c * y4 + o * 128, 128)
                            bh[q, to, s], bl[q, to, s] = split(x)
            return 0

        lax.fori_loop(0, half // tile, unpack, 0)
        tall = min(width, 256)

        def transform(i, _):
            r = pl.ds(pl.multiple_of(i * tall, tall), tall)
            ro = pl.ds(pl.multiple_of(h * width + i * tall, tall), tall)
            for k in range(2 * y4 // 256):
                w = pl.ds(k * 256, 256)
                parts = [dot3(bh[q, r, :], bl[q, r, :], yh[q, :, w], yl[q, :, w], NN) for q in range(4)]
                for j in range(2):
                    for t, x in enumerate(exchange_lanes([x[:, j * 128 : (j + 1) * 128] for x in parts])):
                        spec[t, ro, pl.ds(k * 256 + j * 128, 128)] = x
            return 0

        lax.fori_loop(0, width // tall, transform, 0)

        def solve(inner, _):
            i = h * (chunks // 2) + inner
            r = pl.ds(pl.multiple_of(i * ROWS, ROWS), ROWS)
            strided = [pl.ds(i * ROWS + q, 8, stride=4) for q in range(4)]
            for b in range(y4 // 128):
                for t in range(4):
                    s = pl.ds(512 * b + 128 * t, 128)
                    lanes = [pl.ds(c * y4 + b * 128, 128) for c in range(2)]
                    rl = [
                        pl.ds(pl.multiple_of(h * width + lev * half + inner * ROWS, ROWS), ROWS)
                        for lev in range(2)
                    ]
                    ms, ds = [
                        [jnp.concatenate([f[4 * b + t, lev, x, :] for x in strided], 0) for lev in range(2)]
                        for f in (lower, pivot)
                    ]
                    xs = [[spec[t, rl[lev], lanes[c]] for c in range(2)] for lev in range(2)]
                    held, run = [top[c, r, s] for c in range(2)], gain[r, s]
                    first = [ds[0] * xs[0][c] + ms[0] * held[c] for c in range(2)]
                    second = [ds[1] * xs[1][c] + ms[1] * first[c] for c in range(2)]
                    gain[r, s] = run * ms[0] * ms[1]
                    for c in range(2):
                        spec[t, rl[0], lanes[c]] = first[c]
                        spec[t, rl[1], lanes[c]] = second[c]
                        top[c, r, s] = second[c]
            return 0

        lax.fori_loop(0, chunks // 2, solve, 0)

    def step(t, _):
        @pl.when(t < pairs)
        def _():
            spectra(t)

        @pl.when(t >= 1)
        def _():
            substitute(t - 1)

        return 0

    lax.fori_loop(0, pairs + 1, step, 0)
    low_copy(pairs - 1).wait()
    for lp in range(max(pairs - 2, 0), pairs):
        sent(lp)

    @pl.when(z > 0)
    def _():
        edge().wait_send()


def backward_kernel(
    n, levels, nx,
    low_hbm, top_hbm, gain_hbm, lower_hbm, upper_hbm, th_hbm, tl_hbm, yh_hbm, yl_hbm,
    out_hbm,
    th, tl, yh, yl, low, lower, upper, top, gain, enter, above, d_send, u_send, sh, sl, yo, stage, got, note, notes, out, xh, xl, acc,
    in_sem, low_sem, load_sem, sum_sem, ds_sem, dr_sem, us_sem, ur_sem, send_sem, recv_sem, note_send, note_recv, own_sem, out_sem,
):
    me, z, zs = lax.axis_index("gy"), lax.axis_index("gz"), lax.axis_size("gz")
    width = nx // n
    chunks = width // ROWS
    rows = out_hbm.shape[1]
    ny = n * rows
    y4, x4 = ny // 4, nx // 4
    per = 2 if chunks % 2 == 0 else 1

    inputs = [
        pltpu.make_async_copy(source, to, in_sem.at[i])
        for i, (source, to) in enumerate(((yh_hbm, yh), (yl_hbm, yl), (th_hbm, th), (tl_hbm, tl)))
    ]

    def loads(c):
        slot = lax.rem(c, 2)
        r = pl.ds(pl.multiple_of(c * ROWS, ROWS), ROWS)
        rh = pl.ds(pl.multiple_of(lax.rem(c, chunks // 2) * ROWS, ROWS), ROWS)
        return [
            pltpu.make_async_copy(
                low_hbm.at[:, :, c // (chunks // 2), :, rh, :], low.at[slot], low_sem.at[slot]
            ),
        ] + [
            pltpu.make_async_copy(hbm.at[:, r, pl.ds(128 * k, 128)], ref.at[slot, k], load_sem.at[slot, i, k])
            for i, (hbm, ref) in enumerate(((lower_hbm, lower), (upper_hbm, upper)))
            for k in range(ny // 128)
        ]

    def sums(c):
        slot = lax.rem(c, 2)
        r = pl.ds(pl.multiple_of(c * ROWS, ROWS), ROWS)
        return [
            pltpu.make_async_copy(top_hbm.at[:, r, :], top.at[slot], sum_sem.at[slot, 0]),
            pltpu.make_async_copy(gain_hbm.at[r, :], gain.at[slot], sum_sem.at[slot, 1]),
        ]

    for copy in sums(0) + loads(0) + inputs:
        copy.start()
    barrier = pltpu.get_barrier_semaphore()
    greet([{"gy": lax.rem(me + d, n)} for d in range(1, n)])

    @pl.when(z < zs - 1)
    def _():
        greet([{"gz": z + 1}])

    @pl.when(z > 0)
    def _():
        greet([{"gz": z - 1}])

    acc[...] = jnp.zeros_like(acc)
    pl.semaphore_wait(barrier, n - 1 + jnp.minimum(z, 1) + jnp.minimum(zs - 1 - z, 1))

    @pl.when(z == 0)
    def _():
        enter[...] = jnp.zeros_like(enter)

    @pl.when(z == zs - 1)
    def _():
        above[...] = jnp.zeros_like(above)

    def state_rows(q):
        return pl.ds(pl.multiple_of(q * 8, 8), 8)

    def pass_down(c, q):
        return pltpu.make_async_remote_copy(
            src_ref=d_send.at[lax.rem(c, 2), :, state_rows(q), :], dst_ref=enter.at[c, :, state_rows(q), :],
            send_sem=ds_sem.at[c, q], recv_sem=dr_sem.at[c, q],
            device_id={"gz": z + 1}, device_id_type=MESH,
        )

    def pass_up(c, q):
        return pltpu.make_async_remote_copy(
            src_ref=u_send.at[lax.rem(c, 2), :, state_rows(q), :], dst_ref=above.at[c, :, state_rows(q), :],
            send_sem=us_sem.at[c, q], recv_sem=ur_sem.at[c, q],
            device_id={"gz": z - 1}, device_id_type=MESH,
        )

    def own(c):
        return pltpu.make_async_copy(stage.at[lax.rem(c, 2), me], got.at[c, me], own_sem.at[c])

    def send(c, d):
        peer = lax.rem(me + d, n)
        return pltpu.make_async_remote_copy(
            src_ref=stage.at[lax.rem(c, 2), peer], dst_ref=got.at[c, me],
            send_sem=send_sem.at[c, d], recv_sem=recv_sem.at[c, me],
            device_id={"gy": peer}, device_id_type=MESH,
        )

    def arrival(c, d):
        peer = lax.rem(me + d, n)
        return pltpu.make_async_remote_copy(
            src_ref=stage.at[lax.rem(c, 2), peer], dst_ref=got.at[c, peer],
            send_sem=send_sem.at[c, d], recv_sem=recv_sem.at[c, peer],
            device_id={"gy": peer}, device_id_type=MESH,
        )

    def tell(c, d, source):
        return pltpu.make_async_remote_copy(
            src_ref=note.at[lax.rem(c, 2)], dst_ref=notes.at[c, source],
            send_sem=note_send.at[c, d], recv_sem=note_recv.at[c, source],
            device_id={"gy": lax.rem(me + d, n)}, device_id_type=MESH,
        )

    def relay(c):
        for copy in sums(c):
            copy.wait()

        @pl.when(c + 1 < chunks)
        def _():
            for copy in sums(c + 1):
                copy.start()

        slot = lax.rem(c, 2)

        @pl.when((z < zs - 1) & (c >= 2))
        def _():
            for q in range(4):
                pass_down(c - 2, q).wait_send()

        def carry(q, _):
            r = state_rows(q)

            @pl.when(z > 0)
            def _():
                pass_down(c, q).wait_recv()

            @pl.when(z < zs - 1)
            def _():
                new = [top[slot, k, r, :] + gain[slot, r, :] * enter[c, k, r, :] for k in range(2)]
                for k in range(2):
                    d_send[slot, k, r, :] = new[k]
                pass_down(c, q).start()

            return 0

        lax.fori_loop(0, 4, carry, 0)

    def solve(c):
        slot = lax.rem(c, 2)
        for copy in loads(c):
            copy.wait()

        @pl.when(c + 1 < chunks)
        def _():
            for copy in loads(c + 1):
                copy.start()

        @pl.when((z > 0) & (c >= 2))
        def _():
            for q in range(4):
                pass_up(c - 2, q).wait_send()

        def sweep(q, _):
            strided = pl.ds(q, 8, stride=4)
            r = state_rows(q)

            @pl.when(z < zs - 1)
            def _():
                pass_up(c, q).wait_recv()

            for b in range(y4 // 128):
                natural = [pl.ds(512 * b + 128 * t, 128) for t in range(4)]
                gains = [[] for _ in range(4)]
                for t in range(4):
                    for lev in range(levels):
                        m = lower[slot, 4 * b + t, lev, strided, :]
                        gains[t].append(m if lev == 0 else gains[t][-1] * m)
                state = [[above[c, k, r, s] for s in natural] for k in range(2)]
                entry = [[enter[c, k, r, s] for s in natural] for k in range(2)]
                for lev in range(levels - 1, -1, -1):
                    ups = [upper[slot, 4 * b + t, lev, strided, :] for t in range(4)]
                    for k in range(2):
                        lanes = pl.ds(k * y4 + b * 128, 128)
                        state[k] = [
                            low[slot, lev // 2, t, lev % 2, r, lanes] + gains[t][lev] * entry[k][t] + ups[t] * state[k][t]
                            for t in range(4)
                        ]
                        to = pl.ds(pl.multiple_of(lev * ROWS + q * 8, 8), 8)
                        for t in range(4):
                            yo[t, to, lanes] = state[k][t]
                for k in range(2):
                    for t in range(4):
                        u_send[slot, k, r, natural[t]] = state[k][t]

            @pl.when(z > 0)
            def _():
                pass_up(c, q).start()

            return 0

        lax.fori_loop(0, 4, sweep, 0)

        @pl.when(c == 0)
        def _():
            for copy in inputs:
                copy.wait()

        @pl.when(c >= 2)
        def _():
            own(c - 2).wait()
            for d in range(1, n):
                tell(c - 2, d, me).wait_send()
                send(c - 2, d).wait_send()

        count = levels * ROWS

        def halve(i, _):
            r = pl.ds(pl.multiple_of(i * ROWS, ROWS), ROWS)
            for k in range(2 * y4 // 128):
                s = pl.ds(k * 128, 128)
                for q, x in enumerate(exchange_lanes([yo[t, r, s] for t in range(4)])):
                    sh[q, r, s], sl[q, r, s] = split(x)
            return 0

        lax.fori_loop(0, levels, halve, 0)

        def transform(q, _):
            yo[q] = dot3(sh[q], sl[q], yh[q], yl[q], NT)
            return 0

        lax.fori_loop(0, 4, transform, 0)

        def combine(i, peak):
            r = pl.ds(pl.multiple_of(i * 8, 8), 8)
            for h in range(y4 // 128):
                rs = pl.ds(h * 128, 128)
                cs = pl.ds(y4 + h * 128, 128)
                r0, r1, r2, r3 = [yo[q, r, rs] for q in range(4)]
                i0, i1, i2, i3 = [yo[q, r, cs] for q in range(4)]
                er, fr, ei, fi = r0 + r2, r0 - r2, i0 + i2, i0 - i2
                gr, hr, gi, hi = r1 + r3, r1 - r3, i1 + i3, i1 - i3
                real = (er + gr, fr - hi, er - gr, fr + hi)
                imag = (ei + gi, fi + hr, ei - gi, fi - hr)
                for q in range(4):
                    yo[q, r, rs] = real[q]
                    yo[q, r, cs] = imag[q]
                    peak = jnp.maximum(peak, jnp.maximum(jnp.abs(real[q]), jnp.abs(imag[q])))
            return peak

        peak = lax.fori_loop(0, count // 8, combine, jnp.zeros((8, 128), F32))
        held = jnp.full((1, 128), jnp.maximum(jnp.max(peak), TINY), F32)
        shrink = PEAK / held[:1, :1]
        quads = n // 4
        note[slot] = held
        notes[c, me] = held
        for d in range(1, n):
            tell(c, d, me).start()

        def pack(lev, _):
            r = pl.ds(pl.multiple_of(lev * ROWS, ROWS), ROWS)
            for g in range(n):
                for k in range(2):
                    x = yo[g // quads, r, pl.ds(k * y4 + (g % quads) * 128, 128)]
                    to = pl.ds(pl.multiple_of((lev * 2 + k) * ROWS, ROWS), ROWS)
                    stage[slot, g, to, :] = encode(x * shrink)
            return 0

        lax.fori_loop(0, levels, pack, 0)
        own(c).start()
        for d in range(1, n):
            send(c, d).start()

    def done(lp):
        return pltpu.make_async_copy(out.at[pl.ds(2 * lp, 2)], out_hbm.at[pl.ds(2 * lp, 2)], out_sem.at[lp])

    def emit(lp):
        def tile(i, _):
            lev = 2 * lp + i // (rows // 16)
            ro = pl.ds(pl.multiple_of(lax.rem(i, rows // 16) * 16, 16), 16)
            r = pl.ds(pl.multiple_of(lp * 2 * rows + i * 16, 16), 16)
            a0, a2, u, w = [acc[r, pl.ds(s * x4, x4)] for s in range(4)]
            e, o = a0 + a2, a0 - a2
            for s, x in enumerate((e + u, o + w, e - u, o - w)):
                out[lev, ro, pl.ds(s * x4, x4)] = x.astype(BF16)
            return 0

        lax.fori_loop(0, 2 * rows // 16, tile, 0)
        done(lp).start()

    def gather(pair, ks, final=False):
        for k in ks:
            for d in range(1, n):
                tell(pair * per + k, d, lax.rem(me + d, n)).wait_recv()
                arrival(pair * per + k, d).wait_recv()

        scales = {k: [notes[pair * per + k, s] * (1.0 / (PEAK * nx * ny)) for s in range(n)] for k in ks}
        deep = 16 * n
        mine = pl.ds(ks[0] * deep, len(ks) * deep)

        def two_levels(lp, _):
            for lev in range(2):
                for k in ks:
                    parts = []
                    for s in range(n):
                        for j in range(2):
                            r = ((lp * 2 + lev) * 2 + j) * ROWS
                            r = pl.ds(pl.multiple_of(r, ROWS), ROWS)
                            parts.append(decode(got[pair * per + k, s, r, :], scales[k][s]))
                    for q in range(4):
                        block = jnp.concatenate([x[q * 8 : q * 8 + 8] for x in parts], 0)
                        high, low_part = split(block.T)
                        lanes = pl.ds(k * deep, deep)
                        xh[q, pl.ds(lev * rows, rows), lanes] = high
                        xl[q, pl.ds(lev * rows, rows), lanes] = low_part
            m = pl.ds(pl.multiple_of((pair * per + ks[0]) * deep, deep), len(ks) * deep)
            to = pl.ds(pl.multiple_of(lp * 2 * rows, 2 * rows), 2 * rows)

            def part(q, start, wide):
                t = pl.ds(start, wide)
                return dot3(xh[q, :, mine], xl[q, :, mine], th[m, t], tl[m, t], NN)

            acc[to, pl.ds(0, x4)] += part(0, 0, x4)
            acc[to, pl.ds(x4, x4)] += part(2, x4, x4)
            acc[to, pl.ds(2 * x4, 2 * x4)] += part(1, 2 * x4, 2 * x4) + part(3, 4 * x4, 2 * x4)
            if final:
                emit(lp)
            return 0

        lax.fori_loop(0, levels // 2, two_levels, 0)

    lag = zs - 1
    halves = chunks // per

    def step(t, _):
        @pl.when(t < chunks)
        def _():
            relay(t)

        c = t - lag + z

        @pl.when((c >= 0) & (c < chunks))
        def _():
            solve(c)

        @pl.when((c >= 2 * per - 1) & (c < chunks) & (lax.rem(c + 1 + 2 * per, per) == 0))
        def _():
            gather((c + 1) // per - 2, range(per))

        return 0

    lax.fori_loop(0, chunks + lag, step, 0)
    for c in range(max(chunks - 2, 0), chunks):
        own(c).wait()
    for k in range(per - 1):
        gather(halves - 1, (k,))
    for c in range(max(chunks - 2, 0), chunks):
        for d in range(1, n):
            tell(c, d, me).wait_send()
            send(c, d).wait_send()

        @pl.when(z < zs - 1)
        def _():
            for q in range(4):
                pass_down(c, q).wait_send()

        @pl.when(z > 0)
        def _():
            for q in range(4):
                pass_up(c, q).wait_send()

    gather(halves - 1, (per - 1,), final=True)
    for lp in range(levels // 2):
        done(lp).wait()


def fast_device(p, v, inverse_spacing, inverse_pivot, lower_factor, upper_factor):
    levels, rows, nx = p.shape
    n = lax.axis_size("gy")
    width, ny = nx // n, n * rows
    y4 = ny // 4
    pairs, chunks = levels // 2, nx // n // ROWS
    th, tl = [jnp.asarray(t) for t in along_table(nx, n)]
    yh, yl = [jnp.asarray(t) for t in across_table(ny)]
    anyspace = pl.BlockSpec(memory_space=pl.ANY)
    vmem = pl.BlockSpec(memory_space=pltpu.VMEM)
    dma = pltpu.SemaphoreType.DMA
    message = 4 * width
    tables = [pltpu.VMEM(t.shape, BF16) for t in (th, tl, yh, yl)]
    low, top, gain = pl.pallas_call(
        functools.partial(forward_kernel, n, levels, nx),
        out_shape=[
            jax.ShapeDtypeStruct((pairs, 4, 2 * width, 2 * y4), F32),
            jax.ShapeDtypeStruct((2, width, ny), F32),
            jax.ShapeDtypeStruct((width, ny), F32),
        ],
        in_specs=[anyspace] * 2 + [pl.BlockSpec(memory_space=pltpu.SMEM)] + [anyspace] * 6,
        out_specs=[anyspace, vmem, vmem],
        scratch_shapes=[
            pltpu.VMEM((levels, rows, nx), BF16),
            pltpu.VMEM((levels + 1, rows, nx), BF16),
            *tables,
            pltpu.VMEM((2 * rows, nx), BF16),
            pltpu.VMEM((2 * rows, nx), BF16),
            pltpu.VMEM((2, n, message, 128), BF16),
            pltpu.VMEM((pairs, n, message, 128), BF16),
            pltpu.VMEM((2, 1, 128), F32),
            pltpu.VMEM((pairs, n, 1, 128), F32),
            pltpu.VMEM((4, 2 * width, 2 * y4), BF16),
            pltpu.VMEM((4, 2 * width, 2 * y4), BF16),
            pltpu.VMEM((4, 2 * width, 2 * y4), F32),
            pltpu.VMEM((ny // 128, 2, width, 128), F32),
            pltpu.VMEM((ny // 128, 2, width, 128), F32),
            dma((6,)), dma((2, chunks // 2)), dma, dma,
            dma((pairs, chunks // 2, n)), dma((pairs, chunks // 2, n)), dma((pairs, n)), dma((pairs, n)), dma((pairs,)), dma((2, ny // 128)), dma,
        ],
        compiler_params=pltpu.CompilerParams(
            collective_id=0, has_side_effects=True, vmem_limit_bytes=62 * 2**20
        ),
        name="forward",
    )(p, v, inverse_spacing, th, tl, yh, yl, inverse_pivot, lower_factor)

    low = low.reshape(pairs, 4, 2, 2, width // 2, 2 * y4)
    message = levels * 2 * ROWS
    per = 2 if chunks % 2 == 0 else 1
    count = levels * ROWS
    return pl.pallas_call(
        functools.partial(backward_kernel, n, levels, nx),
        out_shape=jax.ShapeDtypeStruct((levels, rows, nx), BF16),
        in_specs=[anyspace] * 9,
        out_specs=anyspace,
        scratch_shapes=[
            *tables,
            pltpu.VMEM((2, pairs, 4, 2, ROWS, 2 * y4), F32),
            pltpu.VMEM((2, ny // 128, levels, ROWS, 128), F32),
            pltpu.VMEM((2, ny // 128, levels, ROWS, 128), F32),
            pltpu.VMEM((2, 2, ROWS, ny), F32),
            pltpu.VMEM((2, ROWS, ny), F32),
            pltpu.VMEM((chunks, 2, ROWS, ny), F32),
            pltpu.VMEM((chunks, 2, ROWS, ny), F32),
            pltpu.VMEM((2, 2, ROWS, ny), F32),
            pltpu.VMEM((2, 2, ROWS, ny), F32),
            pltpu.VMEM((4, count, 2 * y4), BF16),
            pltpu.VMEM((4, count, 2 * y4), BF16),
            pltpu.VMEM((4, count, 2 * y4), F32),
            pltpu.VMEM((2, n, message, 128), BF16),
            pltpu.VMEM((chunks, n, message, 128), BF16),
            pltpu.VMEM((2, 1, 128), F32),
            pltpu.VMEM((chunks, n, 1, 128), F32),
            pltpu.VMEM((levels, rows, nx), BF16),
            pltpu.VMEM((4, 2 * rows, per * 16 * n), BF16),
            pltpu.VMEM((4, 2 * rows, per * 16 * n), BF16),
            pltpu.VMEM((levels * rows, nx), F32),
            dma((4,)), dma((2,)), dma((2, 2, ny // 128)), dma((2, 2)),
            dma((chunks, 4)), dma((chunks, 4)), dma((chunks, 4)), dma((chunks, 4)),
            dma((chunks, n)), dma((chunks, n)), dma((chunks, n)), dma((chunks, n)), dma((chunks,)), dma((pairs,)),
        ],
        compiler_params=pltpu.CompilerParams(
            collective_id=1, has_side_effects=True, vmem_limit_bytes=62 * 2**20
        ),
        name="backward",
    )(low, top, gain, lower_factor, upper_factor, th, tl, yh, yl)


def solution(mesh):
    spec = P("gz", "gy", None)

    def program(*arrays):
        levels, ny, nx = arrays[0].shape
        gy, gz = mesh.shape["gy"], mesh.shape["gz"]
        fast = ny // gy == 128 and gy % 4 == 0 and levels // gz % 2 == 0 and nx // gy % (4 * ROWS) == 0
        return jax.shard_map(
            fast_device if fast else on_device,
            mesh=mesh,
            in_specs=(spec, spec, P("gz"), spec, spec, spec),
            out_specs=spec,
            check_vma=False,
        )(*arrays)

    return program
```

```python
import functools
import math

import jax
import jax.numpy as jnp
import ml_dtypes
import numpy as np
from jax import lax
from jax.experimental import pallas as pl
from jax.experimental.pallas import tpu as pltpu
from jax.sharding import PartitionSpec as P

PREC = lax.Precision.HIGH
F32 = jnp.float32


def passed_along(x, axis, by):
    size = lax.axis_size(axis)
    pairs = [(i, i + by) for i in range(size) if 0 <= i + by < size]
    return lax.ppermute(x, axis, pairs)


def unit_circle(phase, count):
    angle = (phase % count).astype(F32) * (2.0 * math.pi / count)
    return jnp.cos(angle), jnp.sin(angle)


def circle_table(count):
    low = 32
    high = count // low
    k = jnp.arange(count, dtype=jnp.int32)[None, :]
    ch, sh = unit_circle(jnp.arange(high, dtype=jnp.int32)[:, None] * low * k, count)
    cl, sl = unit_circle(jnp.arange(low, dtype=jnp.int32)[:, None] * k, count)
    ch, sh, cl, sl = lax.optimization_barrier((ch, sh, cl, sl))
    ch, sh, cl, sl = ch[:, None], sh[:, None], cl[None], sl[None]
    cosine = (ch * cl - sh * sl).reshape(count, count)
    sine = (sh * cl + ch * sl).reshape(count, count)
    return cosine, sine


def split_table(count, half):
    low = 32
    column = jnp.arange(2 * count, dtype=jnp.int32)[None, :]
    k = column // (2 * half) * half + column % half
    quarter = jnp.where(column % (2 * half) < half, 0, count // 4)
    ch, sh = unit_circle(jnp.arange(count // low, dtype=jnp.int32)[:, None] * low * k, count)
    cl, sl = unit_circle(jnp.arange(low, dtype=jnp.int32)[:, None] * k + quarter, count)
    ch, sh, cl, sl = lax.optimization_barrier((ch, sh, cl, sl))
    return (ch[:, None] * cl[None] - sh[:, None] * sl[None]).reshape(count, 2 * count)


def down_kernel(chunks, per, *refs):
    cos_refs, sin_refs = refs[:chunks], refs[chunks : 2 * chunks]
    pivot, lower, low, summary = refs[2 * chunks :]
    re = im = jnp.zeros(pivot.shape[1:], F32)
    gain = jnp.ones(pivot.shape[1:], F32)
    for z in range(chunks * per):
        c, s = cos_refs[z // per], sin_refs[z // per]
        q = z % per
        d, m = pivot[z], lower[z]
        re = d * (c[q, 0] + s[q, 1]) + m * re
        im = d * (c[q, 1] - s[q, 0]) + m * im
        gain = m * gain
        low[z, 0] = re
        low[z, 1] = im
    summary[0] = gain
    summary[1] = re
    summary[2] = im


def up_summary_kernel(levels, low, lower, upper, enter, summary):
    er, ei = enter[0, 0], enter[0, 1]
    re = im = jnp.zeros(lower.shape[1:], F32)
    gain = jnp.ones(lower.shape[1:], F32)
    carried = jnp.ones(lower.shape[1:], F32)
    for z in range(levels):
        carried = carried * lower[z]
        re = re + gain * (low[z, 0] + carried * er)
        im = im + gain * (low[z, 1] + carried * ei)
        gain = gain * upper[z]
    summary[0] = gain
    summary[1] = re
    summary[2] = im


def solve_kernel(levels, per, low, lower, upper, enter, above, *outs):
    er, ei = enter[0, 0], enter[0, 1]
    gains = []
    carried = jnp.ones(lower.shape[1:], F32)
    for z in range(levels):
        carried = carried * lower[z]
        gains.append(carried)
    re, im = above[0, 0], above[0, 1]
    for z in range(levels - 1, -1, -1):
        re = low[z, 0] + gains[z] * er + upper[z] * re
        im = low[z, 1] + gains[z] * ei + upper[z] * im
        outs[z // per][z % per, 0] = re
        outs[z // per][z % per, 1] = im


def entering(summary, reverse):
    count = lax.axis_size("gz")
    _, width, span = summary.shape
    parts = summary.reshape(3, count, width // count, span)
    got = lax.all_to_all(parts, "gz", split_axis=1, concat_axis=1, tiled=True)
    order = list(range(count))
    if reverse:
        order.reverse()
    states = [None] * count
    state = jnp.zeros((2, width // count, span), F32)
    for at in order:
        states[at] = state
        state = got[1:, at] + got[0, at][None] * state
    return lax.all_to_all(jnp.stack(states), "gz", split_axis=0, concat_axis=0, tiled=True)


def on_device(
    pressure_cotangent,
    velocity_cotangent,
    inverse_spacing,
    inverse_pivot,
    lower_factor,
    upper_factor,
):
    levels, rows, nx = pressure_cotangent.shape
    level_above = passed_along(velocity_cotangent[:1], "gz", -1)
    gy = lax.axis_size("gy")
    gz = lax.axis_size("gz")
    ny = rows * gy
    half = nx // gy
    per = 2 if levels % 2 == 0 else 1
    chunks = levels // per
    velocity = velocity_cotangent.astype(F32)
    shifted = jnp.concatenate([velocity[1:], level_above.astype(F32)], 0)
    source = pressure_cotangent.astype(F32) + inverse_spacing[:, None, None] * (shifted - velocity)

    table = lax.optimization_barrier(split_table(nx, half))
    cy, sy = lax.optimization_barrier(circle_table(ny))

    cos_parts, sin_parts = [], []
    for i in range(chunks):
        piece = source[i * per : (i + 1) * per]
        spec = jnp.einsum("zyn,nc->zyc", piece, table, precision=PREC)
        spec = jnp.transpose(spec.reshape(per, rows, gy, 2 * half), (2, 0, 1, 3))
        if i >= 2:
            spec, cos_parts[i - 2], sin_parts[i - 2] = lax.optimization_barrier(
                (spec, cos_parts[i - 2], sin_parts[i - 2])
            )
        got = lax.all_to_all(spec, "gy", split_axis=0, concat_axis=0, tiled=True)
        got = jnp.transpose(got, (1, 0, 2, 3)).reshape(per, ny, 2 * half)
        c = jnp.einsum("zyc,yk->zck", got, cy, precision=PREC)
        s = jnp.einsum("zyc,yk->zck", got, sy, precision=PREC)
        cos_parts.append(c.reshape(per, 2, half, ny))
        sin_parts.append(s.reshape(per, 2, half, ny))

    quarter = half // gz
    kb = min(16, quarter)
    in_quarter = quarter // kb
    grid = (half // kb,)
    chunk_spec = pl.BlockSpec((per, 2, kb, ny), lambda i: (0, 0, i, 0))
    factor_spec = pl.BlockSpec((levels, kb, ny), lambda i: (0, i, 0))
    low_spec = pl.BlockSpec((levels, 2, kb, ny), lambda i: (0, 0, i, 0))
    summary_spec = pl.BlockSpec((3, kb, ny), lambda i: (0, i, 0))
    state_spec = pl.BlockSpec((1, 2, kb, ny), lambda i: (i // in_quarter, 0, i % in_quarter, 0))
    summary_shape = jax.ShapeDtypeStruct((3, half, ny), F32)

    low, summary = pl.pallas_call(
        functools.partial(down_kernel, chunks, per),
        grid=grid,
        in_specs=[chunk_spec] * (2 * chunks) + [factor_spec] * 2,
        out_specs=[low_spec, summary_spec],
        out_shape=[jax.ShapeDtypeStruct((levels, 2, half, ny), F32), summary_shape],
    )(*cos_parts, *sin_parts, inverse_pivot, lower_factor)
    enter = entering(summary, False)
    summary = pl.pallas_call(
        functools.partial(up_summary_kernel, levels),
        grid=grid,
        in_specs=[low_spec, factor_spec, factor_spec, state_spec],
        out_specs=summary_spec,
        out_shape=summary_shape,
    )(low, lower_factor, upper_factor, enter)
    above = entering(summary, True)
    solved = pl.pallas_call(
        functools.partial(solve_kernel, levels, per),
        grid=grid,
        in_specs=[low_spec, factor_spec, factor_spec, state_spec, state_spec],
        out_specs=[chunk_spec] * chunks,
        out_shape=[jax.ShapeDtypeStruct((per, 2, half, ny), F32)] * chunks,
    )(low, lower_factor, upper_factor, enter, above)

    normalizer = 1.0 / (nx * ny)
    fields = []
    for i in range(chunks):
        flat = solved[i].reshape(per, 2 * half, ny)
        c = jnp.einsum("ky,zck->zyc", cy, flat, precision=PREC)
        s = jnp.einsum("ky,zck->zyc", sy, flat, precision=PREC)
        back = jnp.concatenate([c[..., :half] - s[..., half:], c[..., half:] + s[..., :half]], 2)
        back = jnp.transpose(back.reshape(per, gy, rows, 2 * half), (1, 0, 2, 3))
        if i >= 2:
            back, fields[i - 2] = lax.optimization_barrier((back, fields[i - 2]))
        got = lax.all_to_all(back, "gy", split_axis=0, concat_axis=0, tiled=True)
        got = jnp.transpose(got, (1, 2, 0, 3)).reshape(per, rows, 2 * nx)
        field = jnp.einsum("zyc,nc->zyn", got, table, precision=PREC) * normalizer
        fields.append(field.astype(jnp.bfloat16))
    return jnp.concatenate(fields, 0)


BF16 = jnp.bfloat16
MESH = pl.DeviceIdType.MESH
TINY = 1e-36
PEAK = 2.0**14
ROWS = 32
NT = (((1,), (1,)), ((), ()))
NN = (((1,), (0,)), ((), ()))


def split(x):
    high = x.astype(BF16)
    return high, (x - high.astype(F32)).astype(BF16)


def split_host(x):
    high = x.astype(np.float32).astype(ml_dtypes.bfloat16)
    low = (x - high.astype(np.float64)).astype(np.float32).astype(ml_dtypes.bfloat16)
    return high, low


def along_table(nx, gy):
    width = nx // gy
    chunk, g, j = np.meshgrid(np.arange(width // ROWS), np.arange(gy), np.arange(8), indexing="ij")
    parts = []
    for q in (0, 2, 1, 3):
        kx = g * width + ROWS * chunk + 4 * j + q
        turn = 2 * np.pi * ((kx[..., None] * np.arange(nx // 4)) % nx) / nx
        c, s = np.cos(turn), np.sin(turn)
        pair = np.stack([c, -s], 2)
        if q == 1:
            pair = np.concatenate([pair, np.stack([-s, -c], 2)], -1)
        if q == 3:
            pair = np.concatenate([pair, np.stack([s, c], 2)], -1)
        parts.append(pair.reshape(-1, pair.shape[-1]))
    return split_host(np.concatenate(parts, 1))


def across_table(ny):
    quarter = ny // 4
    lane = np.arange(quarter)
    block, inner = lane // 128, lane % 128
    tables = []
    for q in range(4):
        ky = 512 * block + 128 * (inner % 4) + 4 * (inner // 4) + q
        turn = 2 * np.pi * ((np.arange(quarter)[:, None] * ky) % ny) / ny
        c, s = np.cos(turn), np.sin(turn)
        tables.append(np.block([[c, -s], [s, c]]))
    return split_host(np.stack(tables))


def exchange_lanes(vs):
    lane = lax.broadcasted_iota(jnp.int32, vs[0].shape, 1)
    odd, upper = lane % 2 == 1, lane % 4 >= 2

    def turned(xs, sign):
        xs = [jnp.where(odd, xs[(d + sign) % 4], xs[d]) for d in range(4)]
        return [jnp.where(upper, xs[(d + 2) % 4], xs[d]) for d in range(4)]

    ds = turned([vs[-d % 4] for d in range(4)], -1)
    es = [ds[0]] + [
        jnp.take_along_axis(ds[d], lane // 4 * 4 + (lane + d) % 4, axis=1) for d in range(1, 4)
    ]
    return turned(es, -1)


def encode(v):
    v2 = v * v
    v4 = v2 * v2
    return (v4 * v4 * v).astype(BF16)


def decode(w, scale):
    w = w.astype(F32)
    size = jnp.maximum(jnp.abs(w), 2.0**-126)
    return w * jnp.exp2(jnp.log(size) * (-8.0 / (9.0 * math.log(2.0)))) * scale


def dot3(ah, al, bh, bl, dims):
    def one(a, b):
        return lax.dot_general(a, b, dims, preferred_element_type=F32)

    return one(ah, bh) + one(al, bh) + one(ah, bl)


def greet(devices):
    barrier = pltpu.get_barrier_semaphore()
    for device in devices:
        pl.semaphore_signal(barrier, inc=1, device_id=device, device_id_type=MESH)


def forward_kernel(
    n, levels, nx,
    p_hbm, v_hbm, spacing, th_hbm, tl_hbm, yh_hbm, yl_hbm, pivot_hbm, lower_hbm,
    low_hbm, top, gain,
    p_ref, v_all, th, tl, yh, yl, ah, al, stage, got, note, notes, bh, bl, spec, pivot, lower,
    in_sem, table_sem, edge_send, edge_recv, send_sem, recv_sem, note_send, note_recv, own_sem, factor_sem, low_sem,
):
    me, z, zs = lax.axis_index("gy"), lax.axis_index("gz"), lax.axis_size("gz")
    rows = p_hbm.shape[1]
    x4 = nx // 4
    width = nx // n
    chunks = width // ROWS
    y4 = n * rows // 4
    pairs = levels // 2
    per = 2
    turns = chunks // per
    piece = 4 * per * ROWS
    half = width // 2

    tall = per * 16 * n

    def part(source, to, start, stop, sem):
        r = pl.ds(start, stop - start)
        return pltpu.make_async_copy(source.at[r], to.at[r], sem)

    def table_part(i):
        m = pl.ds(pl.multiple_of(i * tall, tall), tall)
        return [
            pltpu.make_async_copy(source.at[m, :], to.at[m, :], table_sem.at[k, i])
            for k, (source, to) in enumerate(((th_hbm, th), (tl_hbm, tl)))
        ]

    ahead = min(3, levels)
    early = [part(p_hbm, p_ref, 0, 2, in_sem.at[0]), part(v_hbm, v_all, 0, ahead, in_sem.at[1])]
    late = []
    if levels > 2:
        late.append(part(p_hbm, p_ref, 2, levels, in_sem.at[2]))
    if levels > ahead:
        late.append(part(v_hbm, v_all, ahead, levels, in_sem.at[3]))
    across = [
        pltpu.make_async_copy(source, to, in_sem.at[4 + i])
        for i, (source, to) in enumerate(((yh_hbm, yh), (yl_hbm, yl)))
    ]
    for copy in early + table_part(0):
        copy.start()
    barrier = pltpu.get_barrier_semaphore()
    greet([{"gy": lax.rem(me + d, n)} for d in range(1, n)])

    @pl.when(z < zs - 1)
    def _():
        greet([{"gz": z + 1}])

    pl.semaphore_wait(barrier, n - 1 + jnp.minimum(z, 1))

    def edge():
        return pltpu.make_async_remote_copy(
            src_ref=v_hbm.at[pl.ds(0, 1)], dst_ref=v_all.at[pl.ds(levels, 1)],
            send_sem=edge_send, recv_sem=edge_recv, device_id={"gz": z - 1}, device_id_type=MESH,
        )

    @pl.when(z > 0)
    def _():
        edge().start()

    @pl.when(z == zs - 1)
    def _():
        v_all[levels] = jnp.zeros((rows, nx), BF16)

    top[...] = jnp.zeros_like(top)
    gain[...] = jnp.ones_like(gain)

    def factors(lp):
        return [
            pltpu.make_async_copy(
                hbm.at[pl.ds(2 * lp, 2), :, pl.ds(128 * k, 128)], ref.at[k], factor_sem.at[i, k]
            )
            for i, (hbm, ref) in enumerate(((pivot_hbm, pivot), (lower_hbm, lower)))
            for k in range(y4 // 32)
        ]

    for copy in early:
        copy.wait()
    for copy in table_part(1):
        copy.start()

    def own(lp):
        return pltpu.make_async_copy(stage.at[lax.rem(lp, 2), me], got.at[lp, me], own_sem.at[lp])

    def transfer(lp, i, d, source):
        peer = lax.rem(me + d, n)
        r = pl.ds(pl.multiple_of(i * piece, piece), piece)
        return pltpu.make_async_remote_copy(
            src_ref=stage.at[lax.rem(lp, 2), peer, r, :], dst_ref=got.at[lp, source, r, :],
            send_sem=send_sem.at[lp, i, d], recv_sem=recv_sem.at[lp, i, source],
            device_id={"gy": peer}, device_id_type=MESH,
        )

    def tell(lp, d, source):
        return pltpu.make_async_remote_copy(
            src_ref=note.at[lax.rem(lp, 2)], dst_ref=notes.at[lp, source],
            send_sem=note_send.at[lp, d], recv_sem=note_recv.at[lp, source],
            device_id={"gy": lax.rem(me + d, n)}, device_id_type=MESH,
        )

    def send(lp, i, d):
        return transfer(lp, i, d, me)

    def arrival(lp, i, d):
        return transfer(lp, i, d, lax.rem(me + d, n))

    def sent(lp):
        for d in range(1, n):
            tell(lp, d, me).wait_send()
            for i in range(turns):
                send(lp, i, d).wait_send()

    def low_copy(lp, h):
        r = pl.ds(pl.multiple_of(h * width, width), width)
        return pltpu.make_async_copy(spec.at[:, r, :], low_hbm.at[lp, :, r, :], low_sem.at[h])

    def spectra(lp):
        @pl.when(lp >= 2)
        def _():
            sent(lp - 2)

        @pl.when(lp == 1)
        def _():
            for copy in late:
                copy.wait()

        @pl.when((lp == pairs - 1) & (z < zs - 1))
        def _():
            edge().wait_recv()

        tile = 16
        peak = jnp.zeros((8, 128), F32)
        for lev in range(2):
            at = 2 * lp + lev
            factor = spacing[at]

            def source(i, peak, lev=lev, at=at, factor=factor):
                r = pl.ds(pl.multiple_of(i * tile, tile), tile)
                q = [pl.ds(k * x4, x4) for k in range(4)]
                xs = [
                    p_ref[at, r, s].astype(F32)
                    + factor * (v_all[at + 1, r, s].astype(F32) - v_all[at, r, s].astype(F32))
                    for s in q
                ]
                size = functools.reduce(jnp.maximum, [jnp.abs(x) for x in xs])
                e, o = xs[0] + xs[2], xs[1] + xs[3]
                to = pl.ds(pl.multiple_of(lev * rows + i * tile, tile), tile)
                for s, a in zip(q, (e + o, e - o, xs[0] - xs[2], xs[1] - xs[3])):
                    ah[to, s], al[to, s] = split(a)
                for k in range(x4 // 128):
                    part = size[:, k * 128 : (k + 1) * 128]
                    peak = jnp.maximum(peak, jnp.maximum(part[:8], part[8:]))
                return peak

            peak = lax.fori_loop(0, rows // tile, source, peak)
        peak = jnp.maximum(jnp.max(peak), TINY)
        held = jnp.full((1, 128), peak, F32)
        shrink = PEAK / (nx * held[:1, :1])
        slot = lax.rem(lp, 2)
        note[slot] = held
        notes[lp, me] = held
        for d in range(1, n):
            tell(lp, d, me).start()

        def transform(i, _):
            @pl.when(lp == 0)
            def _():
                for copy in table_part(i):
                    copy.wait()

                @pl.when(i + 2 < turns)
                def _():
                    for copy in table_part(i + 2):
                        copy.start()

            m = pl.ds(pl.multiple_of(i * tall, tall), tall)
            outs, at = [None] * 4, 0
            for q in (0, 2, 1, 3):
                wide = x4 if q % 2 == 0 else 2 * x4
                start = (0, 2 * x4, x4, 2 * x4)[q]
                t, a = pl.ds(at, wide), pl.ds(start, wide)
                outs[q] = dot3(th[m, t], tl[m, t], ah[:, a], al[:, a], NT) * shrink
                at += wide
            for k in range(per):
                for g in range(n):
                    for c in range(2):
                        s = (k * n + g) * 16 + c * 8
                        block = encode(jnp.concatenate([o[s : s + 8] for o in outs], 0))
                        for lev in range(2):
                            r = i * piece + ((lev * 2 + c) * per + k) * ROWS
                            stage[slot, g, pl.ds(pl.multiple_of(r, ROWS), ROWS), :] = block[
                                :, lev * rows : (lev + 1) * rows
                            ]

            for d in range(1, n):
                send(lp, i, d).start()
            return 0

        lax.fori_loop(0, turns, transform, 0)
        own(lp).start()

        @pl.when(lp == 0)
        def _():
            for copy in late + across + factors(0):
                copy.start()

    def substitute(lp):
        own(lp).wait()
        for d in range(1, n):
            tell(lp, d, lax.rem(me + d, n)).wait_recv()

        @pl.when(lp == 0)
        def _():
            for copy in across:
                copy.wait()

        @pl.when(lp > 0)
        def _():
            for h in range(2):
                low_copy(lp - 1, h).wait()

        for copy in factors(lp):
            copy.wait()
        scales = [notes[lp, s] * (nx / PEAK) for s in range(n)]

        def one_half(h, _):
            for k in range(turns // 2):
                for d in range(1, n):
                    arrival(lp, h * (turns // 2) + k, d).wait_recv()
            substitute_half(lp, h, scales)
            low_copy(lp, h).start()
            return 0

        lax.fori_loop(0, 2, one_half, 0)

        @pl.when(lp < pairs - 1)
        def _():
            for copy in factors(lp + 1):
                copy.start()

    def substitute_half(lp, h, scales):
        tile = 16
        quads = n // 4

        def unpack(i, _):
            row = h * half + i * tile
            turn, inner = row // (per * ROWS), lax.rem(row, per * ROWS)
            for lev in range(2):
                for o in range(quads):
                    xs = []
                    for c in range(2):
                        r = turn * piece + (lev * 2 + c) * per * ROWS + inner
                        r = pl.ds(pl.multiple_of(r, tile), tile)
                        xs.append([decode(got[lp, k * quads + o, r, :], scales[k * quads + o]) for k in range(4)])
                    (r0, r1, r2, r3), (i0, i1, i2, i3) = xs
                    er, fr, ei, fi = r0 + r2, r0 - r2, i0 + i2, i0 - i2
                    gr, hr, gi, hi = r1 + r3, r1 - r3, i1 + i3, i1 - i3
                    real = (er + gr, fr + hi, er - gr, fr - hi)
                    imag = (ei + gi, fi - hr, ei - gi, fi + hr)
                    to = pl.ds(pl.multiple_of(lev * half + i * tile, tile), tile)
                    for q in range(4):
                        for c, x in enumerate((real[q], imag[q])):
                            s = pl.ds(c * y4 + o * 128, 128)
                            bh[q, to, s], bl[q, to, s] = split(x)
            return 0

        lax.fori_loop(0, half // tile, unpack, 0)
        tall = min(width, 256)

        def transform(i, _):
            r = pl.ds(pl.multiple_of(i * tall, tall), tall)
            ro = pl.ds(pl.multiple_of(h * width + i * tall, tall), tall)
            for k in range(2 * y4 // 256):
                w = pl.ds(k * 256, 256)
                parts = [dot3(bh[q, r, :], bl[q, r, :], yh[q, :, w], yl[q, :, w], NN) for q in range(4)]
                for j in range(2):
                    for t, x in enumerate(exchange_lanes([x[:, j * 128 : (j + 1) * 128] for x in parts])):
                        spec[t, ro, pl.ds(k * 256 + j * 128, 128)] = x
            return 0

        lax.fori_loop(0, width // tall, transform, 0)

        def solve(inner, _):
            i = h * (chunks // 2) + inner
            r = pl.ds(pl.multiple_of(i * ROWS, ROWS), ROWS)
            strided = [pl.ds(i * ROWS + q, 8, stride=4) for q in range(4)]
            for b in range(y4 // 128):
                for t in range(4):
                    s = pl.ds(512 * b + 128 * t, 128)
                    lanes = [pl.ds(c * y4 + b * 128, 128) for c in range(2)]
                    rl = [
                        pl.ds(pl.multiple_of(h * width + lev * half + inner * ROWS, ROWS), ROWS)
                        for lev in range(2)
                    ]
                    ms, ds = [
                        [jnp.concatenate([f[4 * b + t, lev, x, :] for x in strided], 0) for lev in range(2)]
                        for f in (lower, pivot)
                    ]
                    xs = [[spec[t, rl[lev], lanes[c]] for c in range(2)] for lev in range(2)]
                    held, run = [top[c, r, s] for c in range(2)], gain[r, s]
                    first = [ds[0] * xs[0][c] + ms[0] * held[c] for c in range(2)]
                    second = [ds[1] * xs[1][c] + ms[1] * first[c] for c in range(2)]
                    gain[r, s] = run * ms[0] * ms[1]
                    for c in range(2):
                        spec[t, rl[0], lanes[c]] = first[c]
                        spec[t, rl[1], lanes[c]] = second[c]
                        top[c, r, s] = second[c]
            return 0

        lax.fori_loop(0, chunks // 2, solve, 0)

    def step(t, _):
        @pl.when(t < pairs)
        def _():
            spectra(t)

        @pl.when(t >= 1)
        def _():
            substitute(t - 1)

        return 0

    lax.fori_loop(0, pairs + 1, step, 0)
    for h in range(2):
        low_copy(pairs - 1, h).wait()
    for lp in range(max(pairs - 2, 0), pairs):
        sent(lp)

    @pl.when(z > 0)
    def _():
        edge().wait_send()


def backward_kernel(
    n, levels, nx,
    low_hbm, top_hbm, gain_hbm, lower_hbm, upper_hbm, th_hbm, tl_hbm, yh_hbm, yl_hbm,
    out_hbm,
    th, tl, yh, yl, low, lower, upper, top, gain, enter, above, d_send, u_send, sh, sl, yo, stage, got, note, notes, out, xh, xl, acc,
    in_sem, low_sem, load_sem, sum_sem, ds_sem, dr_sem, us_sem, ur_sem, send_sem, recv_sem, note_send, note_recv, own_sem, out_sem,
):
    me, z, zs = lax.axis_index("gy"), lax.axis_index("gz"), lax.axis_size("gz")
    width = nx // n
    chunks = width // ROWS
    rows = out_hbm.shape[1]
    ny = n * rows
    y4, x4 = ny // 4, nx // 4
    per = 2 if chunks % 2 == 0 else 1

    inputs = [
        pltpu.make_async_copy(source, to, in_sem.at[i])
        for i, (source, to) in enumerate(((yh_hbm, yh), (yl_hbm, yl), (th_hbm, th), (tl_hbm, tl)))
    ]

    def loads(c):
        slot = lax.rem(c, 2)
        r = pl.ds(pl.multiple_of(c * ROWS, ROWS), ROWS)
        rh = pl.ds(pl.multiple_of(lax.rem(c, chunks // 2) * ROWS, ROWS), ROWS)
        return [
            pltpu.make_async_copy(
                low_hbm.at[:, :, c // (chunks // 2), :, rh, :], low.at[slot], low_sem.at[slot]
            ),
        ] + [
            pltpu.make_async_copy(hbm.at[:, r, pl.ds(128 * k, 128)], ref.at[slot, k], load_sem.at[slot, i, k])
            for i, (hbm, ref) in enumerate(((lower_hbm, lower), (upper_hbm, upper)))
            for k in range(ny // 128)
        ]

    def sums(c):
        slot = lax.rem(c, 2)
        r = pl.ds(pl.multiple_of(c * ROWS, ROWS), ROWS)
        return [
            pltpu.make_async_copy(top_hbm.at[:, r, :], top.at[slot], sum_sem.at[slot, 0]),
            pltpu.make_async_copy(gain_hbm.at[r, :], gain.at[slot], sum_sem.at[slot, 1]),
        ]

    for copy in sums(0) + loads(0) + inputs[:2]:
        copy.start()
    barrier = pltpu.get_barrier_semaphore()
    greet([{"gy": lax.rem(me + d, n)} for d in range(1, n)])

    @pl.when(z < zs - 1)
    def _():
        greet([{"gz": z + 1}])

    @pl.when(z > 0)
    def _():
        greet([{"gz": z - 1}])

    acc[...] = jnp.zeros_like(acc)
    pl.semaphore_wait(barrier, n - 1 + jnp.minimum(z, 1) + jnp.minimum(zs - 1 - z, 1))

    @pl.when(z == 0)
    def _():
        enter[...] = jnp.zeros_like(enter)

    @pl.when(z == zs - 1)
    def _():
        above[...] = jnp.zeros_like(above)

    def state_rows(q):
        return pl.ds(pl.multiple_of(q * 8, 8), 8)

    def pass_down(c, q):
        return pltpu.make_async_remote_copy(
            src_ref=d_send.at[lax.rem(c, 2), :, state_rows(q), :], dst_ref=enter.at[c, :, state_rows(q), :],
            send_sem=ds_sem.at[c, q], recv_sem=dr_sem.at[c, q],
            device_id={"gz": z + 1}, device_id_type=MESH,
        )

    def pass_up(c, q):
        return pltpu.make_async_remote_copy(
            src_ref=u_send.at[lax.rem(c, 2), :, state_rows(q), :], dst_ref=above.at[c, :, state_rows(q), :],
            send_sem=us_sem.at[c, q], recv_sem=ur_sem.at[c, q],
            device_id={"gz": z - 1}, device_id_type=MESH,
        )

    def own(c):
        return pltpu.make_async_copy(stage.at[lax.rem(c, 2), me], got.at[c, me], own_sem.at[c])

    def send(c, d):
        peer = lax.rem(me + d, n)
        return pltpu.make_async_remote_copy(
            src_ref=stage.at[lax.rem(c, 2), peer], dst_ref=got.at[c, me],
            send_sem=send_sem.at[c, d], recv_sem=recv_sem.at[c, me],
            device_id={"gy": peer}, device_id_type=MESH,
        )

    def arrival(c, d):
        peer = lax.rem(me + d, n)
        return pltpu.make_async_remote_copy(
            src_ref=stage.at[lax.rem(c, 2), peer], dst_ref=got.at[c, peer],
            send_sem=send_sem.at[c, d], recv_sem=recv_sem.at[c, peer],
            device_id={"gy": peer}, device_id_type=MESH,
        )

    def tell(c, d, source):
        return pltpu.make_async_remote_copy(
            src_ref=note.at[lax.rem(c, 2)], dst_ref=notes.at[c, source],
            send_sem=note_send.at[c, d], recv_sem=note_recv.at[c, source],
            device_id={"gy": lax.rem(me + d, n)}, device_id_type=MESH,
        )

    def relay(c):
        for copy in sums(c):
            copy.wait()

        @pl.when(c + 1 < chunks)
        def _():
            for copy in sums(c + 1):
                copy.start()

        slot = lax.rem(c, 2)

        @pl.when((z < zs - 1) & (c >= 2))
        def _():
            for q in range(4):
                pass_down(c - 2, q).wait_send()

        def carry(q, _):
            r = state_rows(q)

            @pl.when(z > 0)
            def _():
                pass_down(c, q).wait_recv()

            @pl.when(z < zs - 1)
            def _():
                new = [top[slot, k, r, :] + gain[slot, r, :] * enter[c, k, r, :] for k in range(2)]
                for k in range(2):
                    d_send[slot, k, r, :] = new[k]
                pass_down(c, q).start()

            return 0

        lax.fori_loop(0, 4, carry, 0)

    def solve(c):
        slot = lax.rem(c, 2)
        for copy in loads(c):
            copy.wait()

        @pl.when(c + 1 < chunks)
        def _():
            for copy in loads(c + 1):
                copy.start()

        @pl.when((z > 0) & (c >= 2))
        def _():
            for q in range(4):
                pass_up(c - 2, q).wait_send()

        def sweep(q, _):
            strided = pl.ds(q, 8, stride=4)
            r = state_rows(q)

            @pl.when(z < zs - 1)
            def _():
                pass_up(c, q).wait_recv()

            for b in range(y4 // 128):
                natural = [pl.ds(512 * b + 128 * t, 128) for t in range(4)]
                gains = [[] for _ in range(4)]
                for t in range(4):
                    for lev in range(levels):
                        m = lower[slot, 4 * b + t, lev, strided, :]
                        gains[t].append(m if lev == 0 else gains[t][-1] * m)
                state = [[above[c, k, r, s] for s in natural] for k in range(2)]
                entry = [[enter[c, k, r, s] for s in natural] for k in range(2)]
                for lev in range(levels - 1, -1, -1):
                    ups = [upper[slot, 4 * b + t, lev, strided, :] for t in range(4)]
                    for k in range(2):
                        lanes = pl.ds(k * y4 + b * 128, 128)
                        state[k] = [
                            low[slot, lev // 2, t, lev % 2, r, lanes] + gains[t][lev] * entry[k][t] + ups[t] * state[k][t]
                            for t in range(4)
                        ]
                        to = pl.ds(pl.multiple_of(lev * ROWS + q * 8, 8), 8)
                        for t in range(4):
                            yo[t, to, lanes] = state[k][t]
                for k in range(2):
                    for t in range(4):
                        u_send[slot, k, r, natural[t]] = state[k][t]

            @pl.when(z > 0)
            def _():
                pass_up(c, q).start()

            return 0

        lax.fori_loop(0, 4, sweep, 0)

        @pl.when(c == 0)
        def _():
            for copy in inputs[2:]:
                copy.start()
            for copy in inputs[:2]:
                copy.wait()

        @pl.when(c == 1)
        def _():
            for copy in inputs[2:]:
                copy.wait()

        @pl.when(c >= 2)
        def _():
            own(c - 2).wait()
            for d in range(1, n):
                tell(c - 2, d, me).wait_send()
                send(c - 2, d).wait_send()

        count = levels * ROWS

        def halve(i, _):
            r = pl.ds(pl.multiple_of(i * ROWS, ROWS), ROWS)
            for k in range(2 * y4 // 128):
                s = pl.ds(k * 128, 128)
                for q, x in enumerate(exchange_lanes([yo[t, r, s] for t in range(4)])):
                    sh[q, r, s], sl[q, r, s] = split(x)
            return 0

        lax.fori_loop(0, levels, halve, 0)

        def transform(q, _):
            yo[q] = dot3(sh[q], sl[q], yh[q], yl[q], NT)
            return 0

        lax.fori_loop(0, 4, transform, 0)

        def combine(i, peak):
            r = pl.ds(pl.multiple_of(i * 8, 8), 8)
            for h in range(y4 // 128):
                rs = pl.ds(h * 128, 128)
                cs = pl.ds(y4 + h * 128, 128)
                r0, r1, r2, r3 = [yo[q, r, rs] for q in range(4)]
                i0, i1, i2, i3 = [yo[q, r, cs] for q in range(4)]
                er, fr, ei, fi = r0 + r2, r0 - r2, i0 + i2, i0 - i2
                gr, hr, gi, hi = r1 + r3, r1 - r3, i1 + i3, i1 - i3
                real = (er + gr, fr - hi, er - gr, fr + hi)
                imag = (ei + gi, fi + hr, ei - gi, fi - hr)
                for q in range(4):
                    yo[q, r, rs] = real[q]
                    yo[q, r, cs] = imag[q]
                    peak = jnp.maximum(peak, jnp.maximum(jnp.abs(real[q]), jnp.abs(imag[q])))
            return peak

        peak = lax.fori_loop(0, count // 8, combine, jnp.zeros((8, 128), F32))
        held = jnp.full((1, 128), jnp.maximum(jnp.max(peak), TINY), F32)
        shrink = PEAK / held[:1, :1]
        quads = n // 4
        note[slot] = held
        notes[c, me] = held
        for d in range(1, n):
            tell(c, d, me).start()

        def pack(lev, _):
            r = pl.ds(pl.multiple_of(lev * ROWS, ROWS), ROWS)
            for g in range(n):
                for k in range(2):
                    x = yo[g // quads, r, pl.ds(k * y4 + (g % quads) * 128, 128)]
                    to = pl.ds(pl.multiple_of((lev * 2 + k) * ROWS, ROWS), ROWS)
                    stage[slot, g, to, :] = encode(x * shrink)
            return 0

        lax.fori_loop(0, levels, pack, 0)
        own(c).start()
        for d in range(1, n):
            send(c, d).start()

    def done(lp):
        return pltpu.make_async_copy(out.at[pl.ds(2 * lp, 2)], out_hbm.at[pl.ds(2 * lp, 2)], out_sem.at[lp])

    def emit(lp):
        def tile(i, _):
            lev = 2 * lp + i // (rows // 16)
            ro = pl.ds(pl.multiple_of(lax.rem(i, rows // 16) * 16, 16), 16)
            r = pl.ds(pl.multiple_of(lp * 2 * rows + i * 16, 16), 16)
            a0, a2, u, w = [acc[r, pl.ds(s * x4, x4)] for s in range(4)]
            e, o = a0 + a2, a0 - a2
            for s, x in enumerate((e + u, o + w, e - u, o - w)):
                out[lev, ro, pl.ds(s * x4, x4)] = x.astype(BF16)
            return 0

        lax.fori_loop(0, 2 * rows // 16, tile, 0)
        done(lp).start()

    def gather(pair, ks, final=False):
        for k in ks:
            for d in range(1, n):
                tell(pair * per + k, d, lax.rem(me + d, n)).wait_recv()
                arrival(pair * per + k, d).wait_recv()

        scales = {k: [notes[pair * per + k, s] * (1.0 / (PEAK * nx * ny)) for s in range(n)] for k in ks}
        deep = 16 * n
        mine = pl.ds(ks[0] * deep, len(ks) * deep)

        def two_levels(lp, _):
            for lev in range(2):
                for k in ks:
                    parts = []
                    for s in range(n):
                        for j in range(2):
                            r = ((lp * 2 + lev) * 2 + j) * ROWS
                            r = pl.ds(pl.multiple_of(r, ROWS), ROWS)
                            parts.append(decode(got[pair * per + k, s, r, :], scales[k][s]))
                    for q in range(4):
                        block = jnp.concatenate([x[q * 8 : q * 8 + 8] for x in parts], 0)
                        high, low_part = split(block.T)
                        lanes = pl.ds(k * deep, deep)
                        xh[q, pl.ds(lev * rows, rows), lanes] = high
                        xl[q, pl.ds(lev * rows, rows), lanes] = low_part
            m = pl.ds(pl.multiple_of((pair * per + ks[0]) * deep, deep), len(ks) * deep)
            to = pl.ds(pl.multiple_of(lp * 2 * rows, 2 * rows), 2 * rows)

            def part(q, start, wide):
                t = pl.ds(start, wide)
                return dot3(xh[q, :, mine], xl[q, :, mine], th[m, t], tl[m, t], NN)

            acc[to, pl.ds(0, x4)] += part(0, 0, x4)
            acc[to, pl.ds(x4, x4)] += part(2, x4, x4)
            acc[to, pl.ds(2 * x4, 2 * x4)] += part(1, 2 * x4, 2 * x4) + part(3, 4 * x4, 2 * x4)
            if final:
                emit(lp)
            return 0

        lax.fori_loop(0, levels // 2, two_levels, 0)

    lag = zs - 1
    halves = chunks // per

    def step(t, _):
        @pl.when(t < chunks)
        def _():
            relay(t)

        c = t - lag + z

        @pl.when((c >= 0) & (c < chunks))
        def _():
            solve(c)

        @pl.when((c >= 2 * per - 1) & (c < chunks) & (lax.rem(c + 1 + 2 * per, per) == 0))
        def _():
            gather((c + 1) // per - 2, range(per))

        return 0

    lax.fori_loop(0, chunks + lag, step, 0)
    for c in range(max(chunks - 2, 0), chunks):
        own(c).wait()
    for k in range(per - 1):
        gather(halves - 1, (k,))
    for c in range(max(chunks - 2, 0), chunks):
        for d in range(1, n):
            tell(c, d, me).wait_send()
            send(c, d).wait_send()

        @pl.when(z < zs - 1)
        def _():
            for q in range(4):
                pass_down(c, q).wait_send()

        @pl.when(z > 0)
        def _():
            for q in range(4):
                pass_up(c, q).wait_send()

    gather(halves - 1, (per - 1,), final=True)
    for lp in range(levels // 2):
        done(lp).wait()


def fast_device(p, v, inverse_spacing, inverse_pivot, lower_factor, upper_factor):
    levels, rows, nx = p.shape
    n = lax.axis_size("gy")
    width, ny = nx // n, n * rows
    y4 = ny // 4
    pairs, chunks = levels // 2, nx // n // ROWS
    th, tl = [jnp.asarray(t) for t in along_table(nx, n)]
    yh, yl = [jnp.asarray(t) for t in across_table(ny)]
    anyspace = pl.BlockSpec(memory_space=pl.ANY)
    vmem = pl.BlockSpec(memory_space=pltpu.VMEM)
    dma = pltpu.SemaphoreType.DMA
    message = 4 * width
    tables = [pltpu.VMEM(t.shape, BF16) for t in (th, tl, yh, yl)]
    low, top, gain = pl.pallas_call(
        functools.partial(forward_kernel, n, levels, nx),
        out_shape=[
            jax.ShapeDtypeStruct((pairs, 4, 2 * width, 2 * y4), F32),
            jax.ShapeDtypeStruct((2, width, ny), F32),
            jax.ShapeDtypeStruct((width, ny), F32),
        ],
        in_specs=[anyspace] * 2 + [pl.BlockSpec(memory_space=pltpu.SMEM)] + [anyspace] * 6,
        out_specs=[anyspace, vmem, vmem],
        scratch_shapes=[
            pltpu.VMEM((levels, rows, nx), BF16),
            pltpu.VMEM((levels + 1, rows, nx), BF16),
            *tables,
            pltpu.VMEM((2 * rows, nx), BF16),
            pltpu.VMEM((2 * rows, nx), BF16),
            pltpu.VMEM((2, n, message, 128), BF16),
            pltpu.VMEM((pairs, n, message, 128), BF16),
            pltpu.VMEM((2, 1, 128), F32),
            pltpu.VMEM((pairs, n, 1, 128), F32),
            pltpu.VMEM((4, 2 * width, 2 * y4), BF16),
            pltpu.VMEM((4, 2 * width, 2 * y4), BF16),
            pltpu.VMEM((4, 2 * width, 2 * y4), F32),
            pltpu.VMEM((ny // 128, 2, width, 128), F32),
            pltpu.VMEM((ny // 128, 2, width, 128), F32),
            dma((6,)), dma((2, chunks // 2)), dma, dma,
            dma((pairs, chunks // 2, n)), dma((pairs, chunks // 2, n)), dma((pairs, n)), dma((pairs, n)), dma((pairs,)), dma((2, ny // 128)), dma((2,)),
        ],
        compiler_params=pltpu.CompilerParams(
            collective_id=0, has_side_effects=True, vmem_limit_bytes=62 * 2**20
        ),
        name="forward",
    )(p, v, inverse_spacing, th, tl, yh, yl, inverse_pivot, lower_factor)

    low = low.reshape(pairs, 4, 2, 2, width // 2, 2 * y4)
    message = levels * 2 * ROWS
    per = 2 if chunks % 2 == 0 else 1
    count = levels * ROWS
    return pl.pallas_call(
        functools.partial(backward_kernel, n, levels, nx),
        out_shape=jax.ShapeDtypeStruct((levels, rows, nx), BF16),
        in_specs=[anyspace] * 9,
        out_specs=anyspace,
        scratch_shapes=[
            *tables,
            pltpu.VMEM((2, pairs, 4, 2, ROWS, 2 * y4), F32),
            pltpu.VMEM((2, ny // 128, levels, ROWS, 128), F32),
            pltpu.VMEM((2, ny // 128, levels, ROWS, 128), F32),
            pltpu.VMEM((2, 2, ROWS, ny), F32),
            pltpu.VMEM((2, ROWS, ny), F32),
            pltpu.VMEM((chunks, 2, ROWS, ny), F32),
            pltpu.VMEM((chunks, 2, ROWS, ny), F32),
            pltpu.VMEM((2, 2, ROWS, ny), F32),
            pltpu.VMEM((2, 2, ROWS, ny), F32),
            pltpu.VMEM((4, count, 2 * y4), BF16),
            pltpu.VMEM((4, count, 2 * y4), BF16),
            pltpu.VMEM((4, count, 2 * y4), F32),
            pltpu.VMEM((2, n, message, 128), BF16),
            pltpu.VMEM((chunks, n, message, 128), BF16),
            pltpu.VMEM((2, 1, 128), F32),
            pltpu.VMEM((chunks, n, 1, 128), F32),
            pltpu.VMEM((levels, rows, nx), BF16),
            pltpu.VMEM((4, 2 * rows, per * 16 * n), BF16),
            pltpu.VMEM((4, 2 * rows, per * 16 * n), BF16),
            pltpu.VMEM((levels * rows, nx), F32),
            dma((4,)), dma((2,)), dma((2, 2, ny // 128)), dma((2, 2)),
            dma((chunks, 4)), dma((chunks, 4)), dma((chunks, 4)), dma((chunks, 4)),
            dma((chunks, n)), dma((chunks, n)), dma((chunks, n)), dma((chunks, n)), dma((chunks,)), dma((pairs,)),
        ],
        compiler_params=pltpu.CompilerParams(
            collective_id=1, has_side_effects=True, vmem_limit_bytes=62 * 2**20
        ),
        name="backward",
    )(low, top, gain, lower_factor, upper_factor, th, tl, yh, yl)


def solution(mesh):
    spec = P("gz", "gy", None)

    def program(*arrays):
        levels, ny, nx = arrays[0].shape
        gy, gz = mesh.shape["gy"], mesh.shape["gz"]
        fast = ny // gy == 128 and gy % 4 == 0 and levels // gz % 2 == 0 and nx // gy % (4 * ROWS) == 0
        return jax.shard_map(
            fast_device if fast else on_device,
            mesh=mesh,
            in_specs=(spec, spec, P("gz"), spec, spec, spec),
            out_specs=spec,
            check_vma=False,
        )(*arrays)

    return program
```
